32 devices in a mesh: fsdp: 4 (over y, core), ctx: 2 (over x), tp: 4 (over z).
Axes of the slice: x: 2, y: 2, z: 4, core: 2. Of those that a mesh axis runs over, the one named last changes fastest.
Arguments:
- tokens: bfloat16 [8, 1024, 768], P('fsdp', 'ctx'), may hold values from -6 to 6
- lengths: int32 [8], P('fsdp'), may hold values from 256 to 1024, as said below
- cotangent: bfloat16 [8, 1024, 768], P('fsdp', 'ctx'), may hold values from -6 to 6
- w_query: bfloat16 [768, 768], P('fsdp', 'tp'), may hold values from -0.3125 to 0.3125
- w_key: bfloat16 [768, 768], P('fsdp', 'tp'), may hold values from -0.3125 to 0.3125
- w_value: bfloat16 [768, 768], P('fsdp', 'tp'), may hold values from -0.21875 to 0.21875
- b_query: bfloat16 [768], P('tp'), may hold values from -3 to 3
- b_value: bfloat16 [768], P('tp'), may hold values from -3 to 3
- w_out: bfloat16 [768, 768], P('tp', 'fsdp'), may hold values from -1.5 to 1.5
- b_out: bfloat16 [768], P('fsdp'), may hold values from -3 to 3
- ln1_gain: bfloat16 [768], P('fsdp'), may hold values from 0.5 to 1.5
- ln1_shift: bfloat16 [768], P('fsdp'), may hold values from -3 to 3
- w_up: bfloat16 [768, 3072], P('fsdp', 'tp'), may hold values from -0.21875 to 0.21875
- b_up: bfloat16 [3072], P('tp'), may hold values from -3 to 3
- w_down: bfloat16 [3072, 768], P('tp', 'fsdp'), may hold values from -0.109375 to 0.109375
- b_down: bfloat16 [768], P('fsdp'), may hold values from -3 to 3
- ln2_gain: bfloat16 [768], P('fsdp'), may hold values from 0.5 to 1.5
- ln2_shift: bfloat16 [768], P('fsdp'), may hold values from -3 to 3
Outputs:
- output: bfloat16 [8, 1024, 768], P('fsdp', 'ctx')
- grad_tokens: float32 [8, 1024, 768], P('fsdp', 'ctx')
- grad_w_query: float32 [768, 768], P('fsdp', 'tp')
- grad_w_key: float32 [768, 768], P('fsdp', 'tp')
- grad_w_value: float32 [768, 768], P('fsdp', 'tp')
- grad_b_query: float32 [768], P('tp')
- grad_b_value: float32 [768], P('tp')
- grad_w_out: float32 [768, 768], P('tp', 'fsdp')
- grad_b_out: float32 [768], P('fsdp')
- grad_ln1_gain: float32 [768], P('fsdp')
- grad_ln1_shift: float32 [768], P('fsdp')
- grad_w_up: float32 [768, 3072], P('fsdp', 'tp')
- grad_b_up: float32 [3072], P('tp')
- grad_w_down: float32 [3072, 768], P('tp', 'fsdp')
- grad_b_down: float32 [768], P('fsdp')
- grad_ln2_gain: float32 [768], P('fsdp')
- grad_ln2_shift: float32 [768], P('fsdp')
The draws below stay inside these ranges and needn't reach their ends.
Inputs may be any that keep to these rules, and one draw needn't show every extreme that they name: `lengths`: each sequence's count of real positions; positions from that count on are padding. In every draw some sequence has exactly 1024.
All inputs are finite; a program needn't handle non-finite values.
Results may differ from the reference program's by a relative error of at most 0.023.
Values may be sent and summed in bfloat16 or wider, within the bound.
No kernel may reach another device: no remote copies, remote signals or barrier semaphores. Data moves between devices by JAX's collectives and lax.ppermute only.
A program may use at most 128 MiB of HBM per device.

```python
import math
import jax
import jax.numpy as jnp
from jax import lax

D = 768
HEADS = 12
FF = 3072
HEAD_DIM = 64
LENGTH = 1024
SEQUENCES = 8


def draw_lengths(key, part):
    drawn = jax.random.randint(jax.random.fold_in(key, 11), (SEQUENCES,), LENGTH // 4, LENGTH + 1)
    longest = jax.random.randint(jax.random.fold_in(key, 12), (), 0, SEQUENCES)
    slots = jnp.arange(SEQUENCES, dtype=jnp.int32)
    return jnp.where(slots == longest, LENGTH, drawn).astype(jnp.int32)


def block_scale(key, dims, split, least, largest):
    def one(position, parts):
        heights = jax.random.uniform(jax.random.fold_in(jax.random.fold_in(key, 6), position), (parts,), jnp.float32, least / len(split), largest / len(split))
        return jnp.repeat(jnp.exp(heights), dims[position] // parts).reshape((-1,) + (1,) * (len(dims) - position - 1))

    gain = one(*split[0])
    for cut in split[1:]:
        gain = gain * one(*cut)
    return gain


def scatter_about(own_key, dims, scale, bound, pieces=(), kind=jnp.bfloat16):
    loudness = block_scale(own_key, dims, pieces, -0.22, 0.18) if pieces else 1.0
    values = jax.random.normal(own_key, dims, jnp.float32) * scale * loudness
    return jnp.minimum(jnp.maximum(values, -bound), bound).astype(kind)


def setup_inputs(seed: int = 0) -> dict:
    seeds = jax.random.split(jax.random.key(seed), 19)
    return {
        "tokens": scatter_about(seeds[0], (SEQUENCES, LENGTH, D), 1.0, 6.0, ((0, 4), (1, 2))),
        "lengths": draw_lengths(jax.random.fold_in(seeds[18], 71), 0),
        "cotangent": scatter_about(seeds[2], (SEQUENCES, LENGTH, D), 1.0, 6.0, ((0, 4), (1, 2))),
        "w_query": scatter_about(seeds[3], (D, D), (D // 2) ** -0.5, 0.3125, ((0, 4), (1, 4))),
        "w_key": scatter_about(seeds[4], (D, D), (D // 2) ** -0.5, 0.3125, ((0, 4), (1, 4))),
        "w_value": scatter_about(seeds[5], (D, D), D ** -0.5, 0.21875, ((0, 4), (1, 4))),
        "b_query": scatter_about(seeds[6], (D,), 0.5, 3.0, ((0, 4),)),
        "b_value": scatter_about(seeds[7], (D,), 0.5, 3.0, ((0, 4),)),
        "w_out": scatter_about(seeds[8], (D, D), 16 ** -0.5, 1.5, ((0, 4), (1, 4))),
        "b_out": scatter_about(seeds[9], (D,), 0.5, 3.0, ((0, 4),)),
        "ln1_gain": jnp.clip(1.0 + 0.1 * jax.random.normal(seeds[10], (D,), jnp.float32), 0.5, 1.5).astype(jnp.bfloat16),
        "ln1_shift": scatter_about(seeds[11], (D,), 0.5, 3.0, ((0, 4),)),
        "w_up": scatter_about(seeds[12], (D, FF), D ** -0.5, 0.21875, ((0, 4), (1, 4))),
        "b_up": scatter_about(seeds[13], (FF,), 0.5, 3.0, ((0, 4),)),
        "w_down": scatter_about(seeds[14], (FF, D), FF ** -0.5, 0.109375, ((0, 4), (1, 4))),
        "b_down": scatter_about(seeds[15], (D,), 0.5, 3.0, ((0, 4),)),
        "ln2_gain": jnp.clip(1.0 + 0.1 * jax.random.normal(seeds[16], (D,), jnp.float32), 0.5, 1.5).astype(jnp.bfloat16),
        "ln2_shift": scatter_about(seeds[17], (D,), 0.5, 3.0, ((0, 4),)),
    }


@jax.custom_vjp
def low(v):
    return lax.optimization_barrier(v.astype(jnp.bfloat16)).astype(jnp.float32)

@jax.custom_vjp
def low_back(v):
    return v

def low_keep(v):
    return (low(v), None)

def low_pass(kept, grad):
    return (grad,)

def back_keep(v):
    return (v, None)

def back_low(kept, grad):
    return (low(grad),)
low.defvjp(low_keep, low_pass)
low_back.defvjp(back_keep, back_low)
epsilon = 1e-12
masked_score = -1e+30
highest = lax.Precision.HIGHEST

def matmul(left_side, right_side):
    return jnp.dot(left_side, right_side, precision=highest, preferred_element_type=jnp.float32)

def layer_norm(inputs, gain_vector, shift_vector):
    center = lax.optimization_barrier(jnp.mean(inputs, axis=-1, keepdims=True))
    centered = inputs - center
    spread = lax.optimization_barrier(jnp.mean(centered * centered, axis=-1, keepdims=True))
    return centered * lax.rsqrt(spread + epsilon) * gain_vector + shift_vector

def attend_block(queries, key_heads, value_heads, usable):
    score_scale = HEAD_DIM ** (-0.5)
    scores = jnp.einsum('qhe,khe->hqk', queries, key_heads, precision=highest) * score_scale
    scores = low_back(jnp.where(usable[None, None, :], scores, masked_score))
    weights = low(jax.nn.softmax(scores, axis=-1))
    return jnp.einsum('hqk,khe->qhe', weights, value_heads, precision=highest)

def block_forward(inputs, usable, params):
    w_query, w_key, w_value, b_query, b_value, w_out, b_out, ln1_gain, ln1_shift, w_up, b_up, w_down, b_down, ln2_gain, ln2_shift = params
    queries = low_back(low(matmul(inputs, w_query) + b_query))
    key_vectors = low_back(low(matmul(inputs, w_key)))
    value_vectors = low_back(low(matmul(inputs, w_value) + b_value))
    block_size = math.gcd(LENGTH, 512)
    blocks = LENGTH // block_size
    query_blocks = queries.reshape(blocks, block_size, HEADS, HEAD_DIM)
    key_heads = key_vectors.reshape(LENGTH, HEADS, HEAD_DIM)
    value_heads = value_vectors.reshape(LENGTH, HEADS, HEAD_DIM)
    attend = jax.checkpoint(lambda query_block: attend_block(query_block, key_heads, value_heads, usable))
    attended = lax.map(attend, query_blocks).reshape(LENGTH, D)
    attended = low_back(low(attended))
    branch = low_back(matmul(attended, w_out) + b_out)
    normed_one = layer_norm(inputs + branch, ln1_gain, ln1_shift)
    hidden_in = low_back(matmul(low(normed_one), w_up) + b_up)
    active = low(jax.nn.gelu(hidden_in, approximate=False))
    second = low_back(matmul(active, w_down) + b_down)
    return layer_norm(normed_one + second, ln2_gain, ln2_shift)

def reference(tokens, lengths, cotangent, w_query, w_key, w_value, b_query, b_value, w_out, b_out, ln1_gain, ln1_shift, w_up, b_up, w_down, b_down, ln2_gain, ln2_shift):
    params = tuple((weight.astype(jnp.float32) for weight in (w_query, w_key, w_value, b_query, b_value, w_out, b_out, ln1_gain, ln1_shift, w_up, b_up, w_down, b_down, ln2_gain, ln2_shift)))
    positions = jnp.arange(LENGTH, dtype=jnp.int32)

    def one_sequence(totals, sequence_item):
        seq_tokens, seq_cot, seq_length = sequence_item
        usable = positions < seq_length
        output, pullback = jax.vjp(lambda inputs, weights: block_forward(inputs, usable, weights), seq_tokens.astype(jnp.float32), params)
        grad_in, grad_params = pullback(seq_cot.astype(jnp.float32) * usable[:, None].astype(jnp.float32))
        totals = jax.tree.map(lambda running, addition: running + addition, totals, grad_params)
        return (totals, (output.astype(jnp.bfloat16), grad_in))
    zero_grads = jax.tree.map(jnp.zeros_like, params)
    totals, (output, grad_tokens) = lax.scan(one_sequence, zero_grads, (tokens, cotangent, lengths))
    return (output, grad_tokens, totals[0], totals[1], totals[2], totals[3], totals[4], totals[5], totals[6], totals[7], totals[8], totals[9], totals[10], totals[11], totals[12], totals[13], totals[14])
```

```python
import math

import jax
import jax.numpy as jnp
from jax import lax
from jax.experimental import pallas as pl
from jax.experimental.pallas import tpu as pltpu
from jax.sharding import PartitionSpec as P

HEAD_DIM = 64


epsilon = 1e-12
masked_score = -1e30


def passed_along(value, axis, steps):
    count = lax.axis_size(axis)
    pairs = [(source, (source + steps) % count) for source in range(count)]
    return lax.ppermute(value, axis, pairs)


def layer_norm(inputs, gain_vector, shift_vector):
    center = jnp.mean(inputs, axis=-1, keepdims=True)
    centered = inputs - center
    spread = jnp.mean(centered * centered, axis=-1, keepdims=True)
    return centered * lax.rsqrt(spread + epsilon) * gain_vector + shift_vector


def gelu_exact(inputs):
    return jax.nn.gelu(inputs, approximate=False)


def live_keys(lengths, first_key, key_count):
    places = first_key + lax.iota(jnp.int32, key_count)
    return (places[None, :] < lengths[:, None])[:, None, None, :]


def absorb(carried, queries, key_block, value_block, usable, score_scale):
    row_peak, row_total, summed = carried
    scores = (
        jnp.einsum("sqhe,skhe->shqk", queries, key_block, preferred_element_type=jnp.float32)
        * score_scale
    )
    masked = jnp.where(usable, scores, masked_score)
    new_peak = jnp.maximum(row_peak, jnp.max(masked, axis=-1))
    factor = jnp.exp(row_peak - new_peak)
    weights = jnp.where(usable, jnp.exp(masked - new_peak[..., None]), 0.0)
    row_total = row_total * factor + jnp.sum(weights, axis=-1)
    summed = summed * factor[..., None] + jnp.einsum(
        "shqk,skhe->shqe",
        weights.astype(jnp.bfloat16),
        value_block,
        preferred_element_type=jnp.float32,
    )
    return (new_peak, row_total, summed)


def block_grads(
    queries, grad_att, log_total, row_delta, key_block, value_block, usable, score_scale
):
    scores = (
        jnp.einsum("sqhe,skhe->shqk", queries, key_block, preferred_element_type=jnp.float32)
        * score_scale
    )
    masked = jnp.where(usable, scores, masked_score)
    weights = jnp.where(usable, jnp.exp(masked - log_total[..., None]), 0.0)
    grad_value = jnp.einsum(
        "shqk,sqhe->skhe",
        weights.astype(jnp.bfloat16),
        grad_att,
        preferred_element_type=jnp.float32,
    )
    grad_weights = jnp.einsum(
        "sqhe,skhe->shqk", grad_att, value_block, preferred_element_type=jnp.float32
    )
    grad_scores = (weights * (grad_weights - row_delta[..., None])).astype(jnp.bfloat16)
    grad_query = (
        jnp.einsum("shqk,skhe->sqhe", grad_scores, key_block, preferred_element_type=jnp.float32)
        * score_scale
    )
    grad_key = (
        jnp.einsum("shqk,sqhe->skhe", grad_scores, queries, preferred_element_type=jnp.float32)
        * score_scale
    )
    return (grad_query, grad_key, grad_value)


def per_device(
    tokens,
    lengths,
    cotangent,
    w_query,
    w_key,
    w_value,
    b_query,
    b_value,
    w_out,
    b_out,
    ln1_gain,
    ln1_shift,
    w_up,
    b_up,
    w_down,
    b_down,
    ln2_gain,
    ln2_shift,
):
    sequences, local_rows, model_width = tokens.shape
    token_count = sequences * local_rows
    ctx_count = lax.axis_size("ctx")
    ctx_index = lax.axis_index("ctx")
    (
        query_full,
        key_full,
        value_full,
        out_full,
        up_full,
        down_full,
        bias_out,
        gain_one,
        shift_one,
        bias_down,
        gain_two,
        shift_two,
    ) = (
        lax.all_gather(w_query, "fsdp", axis=0, tiled=True),
        lax.all_gather(w_key, "fsdp", axis=0, tiled=True),
        lax.all_gather(w_value, "fsdp", axis=0, tiled=True),
        lax.all_gather(w_out, "fsdp", axis=1, tiled=True),
        lax.all_gather(w_up, "fsdp", axis=0, tiled=True),
        lax.all_gather(w_down, "fsdp", axis=1, tiled=True),
        lax.all_gather(b_out, "fsdp", axis=0, tiled=True),
        lax.all_gather(ln1_gain, "fsdp", axis=0, tiled=True),
        lax.all_gather(ln1_shift, "fsdp", axis=0, tiled=True),
        lax.all_gather(b_down, "fsdp", axis=0, tiled=True),
        lax.all_gather(ln2_gain, "fsdp", axis=0, tiled=True),
        lax.all_gather(ln2_shift, "fsdp", axis=0, tiled=True),
    )
    flat_tokens = tokens.reshape(token_count, model_width)
    local_width = query_full.shape[1]
    head_count = local_width // HEAD_DIM
    score_scale = HEAD_DIM ** (-0.5)
    query_low = (
        jnp.dot(flat_tokens, query_full, preferred_element_type=jnp.float32)
        + b_query.astype(jnp.float32)
    ).astype(jnp.bfloat16)
    key_low = jnp.dot(flat_tokens, key_full, preferred_element_type=jnp.float32).astype(
        jnp.bfloat16
    )
    value_low = (
        jnp.dot(flat_tokens, value_full, preferred_element_type=jnp.float32)
        + b_value.astype(jnp.float32)
    ).astype(jnp.bfloat16)
    query_heads = query_low.reshape(sequences, local_rows, head_count, HEAD_DIM)
    key_local = key_low.reshape(sequences, local_rows, local_width)
    value_local = value_low.reshape(sequences, local_rows, local_width)
    query_first = ctx_index * local_rows
    start_state = (
        jnp.full((sequences, head_count, local_rows), masked_score, jnp.float32),
        jnp.zeros((sequences, head_count, local_rows), jnp.float32),
        jnp.zeros((sequences, head_count, local_rows, HEAD_DIM), jnp.float32),
    )
    key_part = lax.all_gather(key_local, "ctx", axis=1, tiled=True)
    value_part = lax.all_gather(value_local, "ctx", axis=1, tiled=True)
    key_count = key_part.shape[1]
    block_size = math.gcd(key_count, 512)

    def one_block(position, state_in):
        offset = position * block_size
        key_block = lax.dynamic_slice_in_dim(key_part, offset, block_size, 1).reshape(
            sequences, block_size, head_count, HEAD_DIM
        )
        value_block = lax.dynamic_slice_in_dim(value_part, offset, block_size, 1).reshape(
            sequences, block_size, head_count, HEAD_DIM
        )
        usable = live_keys(lengths, offset, block_size)
        return absorb(state_in, query_heads, key_block, value_block, usable, score_scale)

    row_peak, row_total, summed = lax.fori_loop(0, key_count // block_size, one_block, start_state)
    attended = (summed / row_total[..., None]).transpose(0, 2, 1, 3)
    log_total = row_peak + jnp.log(row_total)
    attended_low = attended.reshape(token_count, local_width).astype(jnp.bfloat16)
    branch = lax.psum(
        jnp.dot(attended_low, out_full, preferred_element_type=jnp.float32).astype(jnp.bfloat16),
        "tp",
    ).astype(jnp.float32) + bias_out.astype(jnp.float32)
    normed_one, norm_one_back = jax.vjp(
        layer_norm,
        flat_tokens.astype(jnp.float32) + branch,
        gain_one.astype(jnp.float32),
        shift_one.astype(jnp.float32),
    )
    normed_low = normed_one.astype(jnp.bfloat16)
    hidden_in = jnp.dot(normed_low, up_full, preferred_element_type=jnp.float32) + b_up.astype(
        jnp.float32
    )
    active, gelu_back = jax.vjp(gelu_exact, hidden_in)
    active_low = active.astype(jnp.bfloat16)
    second = lax.psum(
        jnp.dot(active_low, down_full, preferred_element_type=jnp.float32).astype(jnp.bfloat16),
        "tp",
    ).astype(jnp.float32) + bias_down.astype(jnp.float32)
    output, norm_two_back = jax.vjp(
        layer_norm, normed_one + second, gain_two.astype(jnp.float32), shift_two.astype(jnp.float32)
    )
    positions = query_first + lax.iota(jnp.int32, local_rows)
    row_valid = (positions[None, :] < lengths[:, None]).astype(jnp.float32).reshape(token_count, 1)
    grad_output = cotangent.reshape(token_count, model_width).astype(jnp.float32) * row_valid
    grad_resid_two, grad_gain_two, grad_shift_two = norm_two_back(grad_output)
    grad_second = grad_resid_two.astype(jnp.bfloat16)
    grad_w_down = jnp.einsum(
        "nf,nd->fd", active_low, grad_second, preferred_element_type=jnp.float32
    )
    grad_b_down = jnp.sum(grad_second.astype(jnp.float32), axis=0)
    (grad_hidden,) = gelu_back(
        jnp.einsum("nd,fd->nf", grad_second, down_full, preferred_element_type=jnp.float32)
    )
    grad_hidden_low = grad_hidden.astype(jnp.bfloat16)
    grad_w_up = jnp.einsum(
        "nd,nf->df", normed_low, grad_hidden_low, preferred_element_type=jnp.float32
    )
    grad_b_up = jnp.sum(grad_hidden_low.astype(jnp.float32), axis=0)
    grad_normed = grad_resid_two + lax.psum(
        jnp.einsum(
            "nf,df->nd", grad_hidden_low, up_full, preferred_element_type=jnp.float32
        ).astype(jnp.bfloat16),
        "tp",
    ).astype(jnp.float32)
    grad_resid_one, grad_gain_one, grad_shift_one = norm_one_back(grad_normed)
    grad_branch = grad_resid_one.astype(jnp.bfloat16)
    grad_w_out = jnp.einsum(
        "nc,nd->cd", attended_low, grad_branch, preferred_element_type=jnp.float32
    )
    grad_b_out = jnp.sum(grad_branch.astype(jnp.float32), axis=0)
    grad_att = jnp.einsum(
        "nd,cd->nc", grad_branch, out_full, preferred_element_type=jnp.float32
    ).astype(jnp.bfloat16)
    grad_att_heads = grad_att.reshape(sequences, local_rows, head_count, HEAD_DIM)
    row_delta = jnp.sum(grad_att_heads.astype(jnp.float32) * attended, axis=-1).transpose(0, 2, 1)
    zero_block = jnp.zeros((sequences, local_rows, head_count, HEAD_DIM), jnp.float32)

    def turn_grads(first_key, key_block, value_block):
        usable = live_keys(lengths, first_key, local_rows)
        key_heads = key_block.reshape(sequences, local_rows, head_count, HEAD_DIM)
        value_heads = value_block.reshape(sequences, local_rows, head_count, HEAD_DIM)
        return block_grads(
            query_heads,
            grad_att_heads,
            log_total,
            row_delta,
            key_heads,
            value_heads,
            usable,
            score_scale,
        )

    def cycle_turn(turn_index, carried):
        key_block, value_block, grad_key, grad_value, grad_query = carried
        source = (ctx_index - turn_index) % ctx_count
        added_query, added_key, added_value = turn_grads(
            source * local_rows, key_block, value_block
        )
        key_block, value_block = passed_along((key_block, value_block), "ctx", 1)
        grad_key, grad_value = (
            passed_along((grad_key + added_key).astype(jnp.bfloat16), "ctx", 1).astype(jnp.float32),
            passed_along((grad_value + added_value).astype(jnp.bfloat16), "ctx", 1).astype(
                jnp.float32
            ),
        )
        return (key_block, value_block, grad_key, grad_value, grad_query + added_query)

    cycle_end = lax.fori_loop(
        0, ctx_count, cycle_turn, (key_local, value_local, zero_block, zero_block, zero_block)
    )
    grad_key, grad_value, grad_query = (cycle_end[2], cycle_end[3], cycle_end[4])
    grad_query_low = grad_query.reshape(token_count, local_width).astype(jnp.bfloat16)
    grad_key_low = grad_key.reshape(token_count, local_width).astype(jnp.bfloat16)
    grad_value_low = grad_value.reshape(token_count, local_width).astype(jnp.bfloat16)
    grad_w_query = jnp.einsum(
        "nd,nc->dc", flat_tokens, grad_query_low, preferred_element_type=jnp.float32
    )
    grad_w_key = jnp.einsum(
        "nd,nc->dc", flat_tokens, grad_key_low, preferred_element_type=jnp.float32
    )
    grad_w_value = jnp.einsum(
        "nd,nc->dc", flat_tokens, grad_value_low, preferred_element_type=jnp.float32
    )
    grad_b_query = jnp.sum(grad_query_low.astype(jnp.float32), axis=0)
    grad_b_value = jnp.sum(grad_value_low.astype(jnp.float32), axis=0)
    back_in = (
        jnp.einsum("nc,dc->nd", grad_query_low, query_full, preferred_element_type=jnp.float32)
        + jnp.einsum("nc,dc->nd", grad_key_low, key_full, preferred_element_type=jnp.float32)
        + jnp.einsum("nc,dc->nd", grad_value_low, value_full, preferred_element_type=jnp.float32)
    )
    grad_tokens = grad_resid_one + lax.psum(back_in.astype(jnp.bfloat16), "tp").astype(jnp.float32)
    (
        share_query,
        share_key,
        share_value,
        share_out,
        share_up,
        share_down,
        share_bias_out,
        share_gain_one,
        share_shift_one,
        share_bias_down,
        share_gain_two,
        share_shift_two,
    ) = (
        lax.psum_scatter(
            grad_w_query.astype(jnp.bfloat16), "fsdp", scatter_dimension=0, tiled=True
        ).astype(jnp.float32),
        lax.psum_scatter(
            grad_w_key.astype(jnp.bfloat16), "fsdp", scatter_dimension=0, tiled=True
        ).astype(jnp.float32),
        lax.psum_scatter(
            grad_w_value.astype(jnp.bfloat16), "fsdp", scatter_dimension=0, tiled=True
        ).astype(jnp.float32),
        lax.psum_scatter(
            grad_w_out.astype(jnp.bfloat16), "fsdp", scatter_dimension=1, tiled=True
        ).astype(jnp.float32),
        lax.psum_scatter(
            grad_w_up.astype(jnp.bfloat16), "fsdp", scatter_dimension=0, tiled=True
        ).astype(jnp.float32),
        lax.psum_scatter(
            grad_w_down.astype(jnp.bfloat16), "fsdp", scatter_dimension=1, tiled=True
        ).astype(jnp.float32),
        lax.psum_scatter(
            grad_b_out.astype(jnp.bfloat16), "fsdp", scatter_dimension=0, tiled=True
        ).astype(jnp.float32),
        lax.psum_scatter(
            grad_gain_one.astype(jnp.bfloat16), "fsdp", scatter_dimension=0, tiled=True
        ).astype(jnp.float32),
        lax.psum_scatter(
            grad_shift_one.astype(jnp.bfloat16), "fsdp", scatter_dimension=0, tiled=True
        ).astype(jnp.float32),
        lax.psum_scatter(
            grad_b_down.astype(jnp.bfloat16), "fsdp", scatter_dimension=0, tiled=True
        ).astype(jnp.float32),
        lax.psum_scatter(
            grad_gain_two.astype(jnp.bfloat16), "fsdp", scatter_dimension=0, tiled=True
        ).astype(jnp.float32),
        lax.psum_scatter(
            grad_shift_two.astype(jnp.bfloat16), "fsdp", scatter_dimension=0, tiled=True
        ).astype(jnp.float32),
    )
    (
        share_query,
        share_key,
        share_value,
        share_out,
        share_up,
        share_down,
        share_bias_out,
        share_gain_one,
        share_shift_one,
        share_bias_down,
        share_gain_two,
        share_shift_two,
    ) = (
        lax.psum(share_query.astype(jnp.bfloat16), "ctx").astype(jnp.float32),
        lax.psum(share_key.astype(jnp.bfloat16), "ctx").astype(jnp.float32),
        lax.psum(share_value.astype(jnp.bfloat16), "ctx").astype(jnp.float32),
        lax.psum(share_out.astype(jnp.bfloat16), "ctx").astype(jnp.float32),
        lax.psum(share_up.astype(jnp.bfloat16), "ctx").astype(jnp.float32),
        lax.psum(share_down.astype(jnp.bfloat16), "ctx").astype(jnp.float32),
        lax.psum(share_bias_out.astype(jnp.bfloat16), "ctx").astype(jnp.float32),
        lax.psum(share_gain_one.astype(jnp.bfloat16), "ctx").astype(jnp.float32),
        lax.psum(share_shift_one.astype(jnp.bfloat16), "ctx").astype(jnp.float32),
        lax.psum(share_bias_down.astype(jnp.bfloat16), "ctx").astype(jnp.float32),
        lax.psum(share_gain_two.astype(jnp.bfloat16), "ctx").astype(jnp.float32),
        lax.psum(share_shift_two.astype(jnp.bfloat16), "ctx").astype(jnp.float32),
    )
    total_b_query, total_b_value, total_b_up = lax.psum(
        (grad_b_query, grad_b_value, grad_b_up), ("fsdp", "ctx")
    )
    return (
        output.astype(jnp.bfloat16).reshape(sequences, local_rows, model_width),
        grad_tokens.reshape(sequences, local_rows, model_width),
        share_query,
        share_key,
        share_value,
        total_b_query,
        total_b_value,
        share_out,
        share_bias_out,
        share_gain_one,
        share_shift_one,
        share_up,
        total_b_up,
        share_down,
        share_bias_down,
        share_gain_two,
        share_shift_two,
    )


def swapped(value, axis, bit):
    count = lax.axis_size(axis)
    return lax.ppermute(value, axis, [(place, place ^ bit) for place in range(count)])


def shifted(value, axis, steps):
    count = lax.axis_size(axis)
    return lax.ppermute(value, axis, [(place, (place + steps) % count) for place in range(count)])


def to_owner(value, step, back=False):
    pairs = []
    for x in range(2):
        for z in range(4):
            block = z ^ step
            source = x * 4 + z
            target = (block >> 1) * 4 + 2 * (block & 1) + x
            pairs.append((target, source) if back else (source, target))
    return lax.ppermute(value, ("ctx", "tp"), pairs)


def xor_ordered(stack, bits):
    count = stack.shape[0]
    order = lax.iota(jnp.int32, count) ^ bits
    return jnp.take(stack, order, axis=0)


def line_gathered(value):
    z = lax.axis_index("tp")
    up_pairs, down_pairs = [(0, 1), (1, 2), (2, 3)], [(1, 0), (2, 1), (3, 2)]
    ups, downs = [], []
    going_up, going_down = value, value
    for step in range(3):
        going_up = lax.ppermute(going_up, "tp", up_pairs[step:])
        going_down = lax.ppermute(going_down, "tp", down_pairs[: 3 - step])
        ups.append(going_up)
        downs.append(going_down)
    blocks = []
    for block in range(4):
        choices = [
            value if place == block else (ups[place - block - 1] if place > block else downs[block - place - 1])
            for place in range(4)
        ]
        blocks.append(lax.select_n(z, *choices))
    return blocks


ANY = pl.BlockSpec(memory_space=pl.ANY)
WHOLE = pl.BlockSpec(memory_space=pltpu.VMEM)
log2_e = math.log2(math.e)


def low(value):
    return value.astype(jnp.bfloat16)


def wide(value):
    return value.astype(jnp.float32)


def dot32(left, right, left_dim, right_dim):
    return lax.dot_general(
        left, right, (((left_dim,), (right_dim,)), ((), ())), preferred_element_type=jnp.float32
    )


def struct(shape, dtype=jnp.bfloat16):
    return jax.ShapeDtypeStruct(shape, dtype)


def cost(flops, moved, special=0):
    return pl.CostEstimate(flops=int(flops), bytes_accessed=int(moved), transcendentals=int(special))


def stack_kernel(*refs):
    for place, ref in enumerate(refs[:-1]):
        refs[-1][place] = ref[...]


def stacked(pieces):
    shape = (len(pieces),) + pieces[0].shape
    return pl.pallas_call(
        stack_kernel,
        out_shape=struct(shape),
        in_specs=[WHOLE] * len(pieces),
        out_specs=WHOLE,
        cost_estimate=cost(0, 4 * math.prod(shape)),
        name="stack_pieces",
    )(*pieces)


def spread_pack(own_half, x_first):
    line = stacked([own_half] + [shifted(own_half, "tp", step) for step in (1, 2, 3)])
    if x_first:
        x_side = swapped(line, "ctx", 1)
        y_side, xy_side = swapped(line, "fsdp", 2), swapped(x_side, "fsdp", 2)
    else:
        y_side = swapped(line, "fsdp", 2)
        x_side, xy_side = swapped(line, "ctx", 1), swapped(y_side, "ctx", 1)
    near = (line, x_side, y_side, xy_side)
    return near + tuple(swapped(piece, "fsdp", 1) for piece in near)


def piece_copies(meta, pieces, columns, target, sems, first):
    x, z, f = meta[0], meta[1], meta[2]
    rows = pieces[0].shape[1]
    copies = []
    for place, piece in enumerate(pieces):
        across = (place % 2, 2 * ((place // 2) % 2) + place // 4)
        start = pl.multiple_of(((f ^ across[1]) * 2 + (x ^ across[0])) * rows, rows)
        for step in range(4):
            copies.append(
                pltpu.make_async_copy(
                    piece.at[step, :, columns],
                    target.at[(z + 4 - step) & 3, pl.ds(start, rows), :],
                    sems.at[first + len(copies)],
                )
            )
    return copies


def attend_kernel(
    meta, own, other, w0, w1, w2, w3, bias, qkv, o0, o1, o2, o3, stats, weight, mask, *, block, heads
):
    step = pl.program_id(0)
    shard = w0.shape[0]
    half = own.shape[1]
    scale = log2_e * HEAD_DIM ** (-0.5)

    @pl.when(step == 0)
    def _():
        for place, piece in enumerate((w0, w1, w2, w3)):
            start = pl.multiple_of((meta[2] ^ place) * shard, shard)
            weight[pl.ds(start, shard), :] = piece[...]
        for place, rows in enumerate((own, other)):
            source = rows[0] if place == 0 else rows[...]
            qkv[place * half : (place + 1) * half, :] = low(
                dot32(source, weight[...], 1, 0) + bias[...]
            )
            first = (meta[0] ^ place) * half
            position = first + lax.broadcasted_iota(jnp.int32, (half, block), 0)
            mask[place * half : (place + 1) * half, :] = jnp.where(
                position < meta[3], 0.0, masked_score
            )

    rows = pl.ds(pl.multiple_of((meta[7] ^ step) * block, block), block)
    outs, logs = [], []
    for head in range(heads):
        base = 3 * head * HEAD_DIM
        query = qkv[rows, base : base + HEAD_DIM]
        key = qkv[:, base + HEAD_DIM : base + 2 * HEAD_DIM]
        value = qkv[:, base + 2 * HEAD_DIM : base + 3 * HEAD_DIM]
        scores = dot32(key, query, 1, 1) * scale + mask[...]
        peak = jnp.max(scores, axis=0, keepdims=True)
        weights = jnp.exp2(scores - peak)
        total = jnp.sum(weights, axis=0, keepdims=True)
        outs.append((dot32(value, low(weights), 0, 0) / total).T)
        logs.append(peak + jnp.log2(total))
    result = low(jnp.concatenate(outs, axis=1))
    for place, out in enumerate((o0, o1, o2, o3)):

        @pl.when(step == place)
        def _(out=out):
            out[...] = result

    stats[0] = jnp.concatenate(logs + [jnp.zeros((8 - heads, block), jnp.float32)], axis=0)


def attend_call(meta, tokens, other, pieces, bias, heads):
    half, width = other.shape
    block = half // 2
    columns = pieces[0].shape[1]
    whole = lambda shape: pl.BlockSpec(shape, lambda step, meta: (0,) * len(shape))
    rows = 2 * half
    return pl.pallas_call(
        lambda *refs: attend_kernel(*refs, block=block, heads=heads),
        grid_spec=pltpu.PrefetchScalarGridSpec(
            num_scalar_prefetch=1,
            grid=(4,),
            in_specs=[
                pl.BlockSpec((1, half, width), lambda step, meta: (meta[0], 0, 0)),
                whole((half, width)),
                *[whole(piece.shape) for piece in pieces],
                whole((1, columns)),
            ],
            out_specs=[
                whole((rows, columns)),
                *[whole((block, columns // 3))] * 4,
                pl.BlockSpec((1, 8, block), lambda step, meta: (step, 0, 0)),
            ],
            scratch_shapes=[
                pltpu.VMEM((width, columns), jnp.bfloat16),
                pltpu.VMEM((rows, block), jnp.float32),
            ],
        ),
        out_shape=[struct((rows, columns))]
        + [struct((block, columns // 3))] * 4
        + [struct((4, 8, block), jnp.float32)],
        cost_estimate=cost(2 * rows * width * columns + 16 * rows * rows * columns, 8e6, rows * rows * 3),
        name="attend",
    )(meta, tokens, other, *pieces, bias)


def attend_back_kernel(
    meta, qkv, d0, d1, d2, d3, o0, o1, o2, o3, stats, full, p0, p1, p2, p3,
    grads, mask, grad_att, attended, *, block, heads
):
    step = pl.program_id(0)
    rows_all = qkv.shape[0]
    half = rows_all // 2
    scale = log2_e * HEAD_DIM ** (-0.5)

    @pl.when(step == 0)
    def _():
        grads[...] = jnp.zeros_like(grads)
        for place in range(2):
            first = (meta[0] ^ place) * half
            position = first + lax.broadcasted_iota(jnp.int32, (half, block), 0)
            mask[place * half : (place + 1) * half, :] = jnp.where(
                position < meta[3], 0.0, masked_score
            )

    for place, (grad, out) in enumerate(zip((d0, d1, d2, d3), (o0, o1, o2, o3))):

        @pl.when(step == place)
        def _(grad=grad, out=out):
            grad_att[...] = grad[...]
            attended[...] = out[...]

    rows = pl.ds(pl.multiple_of((meta[7] ^ step) * block, block), block)
    for head in range(heads):
        base = 3 * head * HEAD_DIM
        span = slice(head * HEAD_DIM, (head + 1) * HEAD_DIM)
        query = qkv[rows, base : base + HEAD_DIM]
        key = qkv[:, base + HEAD_DIM : base + 2 * HEAD_DIM]
        value = qkv[:, base + 2 * HEAD_DIM : base + 3 * HEAD_DIM]
        grad_out = grad_att[:, span]
        products = wide(grad_out) * wide(attended[:, span])
        delta = lax.dot_general(
            jnp.ones((8, HEAD_DIM), jnp.float32),
            products,
            (((1,), (1,)), ((), ())),
            precision=lax.Precision.HIGHEST,
            preferred_element_type=jnp.float32,
        )[:1]
        scores = dot32(key, query, 1, 1) * scale + mask[...]
        weights = jnp.exp2(scores - stats[0, head : head + 1, :])
        grad_weights = dot32(value, grad_out, 1, 1)
        grad_scores = low(weights * (grad_weights - delta))
        grads[2 * head] += dot32(grad_scores, query, 1, 0)
        grads[2 * head + 1] += dot32(low(weights), grad_out, 1, 0)
        full[rows, base : base + HEAD_DIM] = low(
            dot32(grad_scores, key, 0, 0) * HEAD_DIM ** (-0.5)
        )

    @pl.when(step == 3)
    def _():
        for head in range(heads):
            base = 3 * head * HEAD_DIM
            full[:, base + HEAD_DIM : base + 2 * HEAD_DIM] = low(
                grads[2 * head] * HEAD_DIM ** (-0.5)
            )
            full[:, base + 2 * HEAD_DIM : base + 3 * HEAD_DIM] = low(grads[2 * head + 1])
        for place, part in enumerate((p0, p1, p2, p3)):
            part[...] = full[pl.ds(pl.multiple_of((meta[7] ^ place) * block, block), block), :]


def attend_back_call(meta, qkv, grad_parts, parts, stats, heads):
    rows, columns = qkv.shape
    block = rows // 4
    whole = lambda shape: pl.BlockSpec(shape, lambda step, meta: (0,) * len(shape))
    small = whole((block, columns // 3))
    return pl.pallas_call(
        lambda *refs: attend_back_kernel(*refs, block=block, heads=heads),
        grid_spec=pltpu.PrefetchScalarGridSpec(
            num_scalar_prefetch=1,
            grid=(4,),
            in_specs=[whole((rows, columns))]
            + [small] * 8
            + [pl.BlockSpec((1, 8, block), lambda step, meta: (step, 0, 0))],
            out_specs=[whole((rows, columns))] + [whole((block, columns))] * 4,
            scratch_shapes=[
                pltpu.VMEM((2 * heads, rows, HEAD_DIM), jnp.float32),
                pltpu.VMEM((rows, block), jnp.float32),
                pltpu.VMEM((block, columns // 3), jnp.bfloat16),
                pltpu.VMEM((block, columns // 3), jnp.bfloat16),
            ],
        ),
        out_shape=[struct((rows, columns))] + [struct((block, columns))] * 4,
        cost_estimate=cost(40 * rows * rows * columns, 8e6, rows * rows * 3),
        name="attend_back",
    )(meta, qkv, *grad_parts, *parts, stats)


def norm_parts(inputs):
    center = jnp.mean(inputs, axis=-1, keepdims=True)
    centered = inputs - center
    spread = jnp.mean(centered * centered, axis=-1, keepdims=True)
    inverse = lax.rsqrt(spread + epsilon)
    return centered * inverse, inverse


def norm_back(grad_out, hat, inverse, gain):
    scaled = grad_out * gain
    return inverse * (
        scaled
        - jnp.mean(scaled, axis=-1, keepdims=True)
        - hat * jnp.mean(scaled * hat, axis=-1, keepdims=True)
    )


BIAS_OUT, GAIN_ONE, SHIFT_ONE, BIAS_DOWN, GAIN_TWO, SHIFT_TWO = range(6)


def first_kernel(meta, *refs, width):
    att, tok, vectors, up_bias = refs[:4], refs[4], refs[5], refs[6]
    pieces = refs[7:15]
    hat, inverse, active, slope, out_w, up_w, sems = refs[15:]
    hidden = up_w.shape[2]
    copies = piece_copies(meta, pieces, pl.ds(hidden, out_w.shape[2]), out_w, sems, 0)
    copies += piece_copies(meta, pieces, pl.ds(0, hidden), up_w, sems, 32)
    for copy in copies:
        copy.start()
    for copy in copies:
        copy.wait()
    branch = vectors[BIAS_OUT : BIAS_OUT + 1, :]
    for step in range(4):
        branch = branch + dot32(att[step][...], out_w[meta[4] ^ step][:, :width], 1, 1)
    hat_one, inverse_one = norm_parts(wide(tok[0]) + branch)
    hat[...] = hat_one
    inverse[...] = inverse_one
    normed = low(hat_one * vectors[GAIN_ONE : GAIN_ONE + 1, :] + vectors[SHIFT_ONE : SHIFT_ONE + 1, :])
    for place in range(4):
        inputs = dot32(normed, up_w[place], 1, 0) + up_bias[place : place + 1, :]
        cumulative = 0.5 * (1.0 + lax.erf(inputs * (0.5**0.5)))
        density = jnp.exp(-0.5 * inputs * inputs) * ((0.5 / math.pi) ** 0.5)
        active[place] = low(inputs * cumulative)
        slope[place] = low(cumulative + inputs * density)


def second_kernel(meta, *refs, width):
    hat, inverse, active, slope, cot, vectors = refs[:6]
    pieces_a, pieces_b = refs[6:14], refs[14:22]
    outputs = refs[22:34]
    output, resid, g0, g1, g2, g3, hidden_grad, keep, send, small, = outputs[:10]
    out_w, up_w, down_w, blocks, sems = refs[32:]
    model = hat.shape[1]
    rows = hat.shape[0]
    hidden = up_w.shape[2]
    down_copies = piece_copies(meta, pieces_b, pl.ds(0, hidden), down_w, sems, 0)
    copies = piece_copies(meta, pieces_a, pl.ds(0, hidden), up_w, sems, 32)
    copies += piece_copies(meta, pieces_a, pl.ds(hidden, out_w.shape[2]), out_w, sems, 64)
    for copy in down_copies + copies:
        copy.start()
    row = lambda place: vectors[place : place + 1, :]
    hat_one, inverse_one = hat[...], inverse[...]
    normed_one = hat_one * row(GAIN_ONE) + row(SHIFT_ONE)
    for copy in down_copies:
        copy.wait()
    second = row(BIAS_DOWN)
    for place in range(4):
        second = second + dot32(active[place], down_w[place], 1, 1)
    hat_two, inverse_two = norm_parts(normed_one + second)
    output[...] = low(hat_two * row(GAIN_TWO) + row(SHIFT_TWO))
    position = meta[4] * rows + lax.broadcasted_iota(jnp.int32, (rows, model), 0)
    grad_output = jnp.where(position < meta[8], wide(cot[0]), 0.0)
    grad_two = norm_back(grad_output, hat_two, inverse_two, row(GAIN_TWO))
    grad_second = low(grad_two)
    for copy in copies:
        copy.wait()
    grad_normed = grad_two
    sums = lambda array: jnp.sum(array, axis=0, keepdims=True)
    for place in range(4):
        grad_hidden = low(dot32(grad_second, down_w[place], 1, 0) * wide(slope[place]))
        hidden_grad[place] = grad_hidden
        grad_normed = grad_normed + dot32(grad_hidden, up_w[place], 1, 1)
        small[6 + place : 7 + place, :] = sums(wide(grad_hidden))
    grad_one = norm_back(grad_normed, hat_one, inverse_one, row(GAIN_ONE))
    resid[...] = grad_one
    grad_branch = low(grad_one)
    for step, out in enumerate((g0, g1, g2, g3)):
        out[...] = low(dot32(grad_branch, out_w[meta[4] ^ step][:, :width], 1, 0))
    small[0:1, :] = sums(wide(grad_branch))
    small[1:2, :] = sums(grad_normed * hat_one)
    small[2:3, :] = sums(grad_normed)
    small[3:4, :] = sums(wide(grad_second))
    small[4:5, :] = sums(grad_output * hat_two)
    small[5:6, :] = sums(grad_output)
    small[10:16, :] = jnp.zeros((6, model), jnp.float32)
    shard = model // 4
    for kind, array in enumerate((grad_second, low(normed_one), grad_branch)):
        for place in range(4):
            blocks[place] = array[:, place * shard : (place + 1) * shard]
        for far in range(2):
            keep[kind, far] = blocks[meta[2] ^ (2 * far)]
            send[kind, far] = blocks[meta[2] ^ (2 * far + 1)]


def weights_kernel(meta, *refs, width):
    keep, got = refs[0], refs[1]
    active, active_sib, grad, grad_sib = refs[2:6]
    att, att_sib = refs[6:10], refs[10:14]
    near_mine, near_theirs, far_mine, far_theirs = refs[14:18]
    turned, whole = refs[18:]
    shard = keep.shape[3]
    rows = keep.shape[2]
    half = shard // 2
    hidden = active.shape[2]
    mine = pl.multiple_of(meta[0] * half, half)
    theirs = pl.multiple_of((1 - meta[0]) * half, half)

    def store(value, target, first):
        columns = value.shape[1]
        whole[:, :columns] = value
        for far, pair in enumerate(((near_mine, near_theirs), (far_mine, far_theirs))):
            for start, out in zip((mine, theirs), pair):
                out[target, :, first : first + columns] = low(
                    whole[pl.ds(far * shard + start, half), :columns]
                )

    for kind, (own, sib, first) in enumerate(
        ((active, active_sib, hidden), (grad, grad_sib, 0), (att, att_sib, 2 * hidden))
    ):
        for far in range(2):
            span = slice(far * shard, (far + 1) * shard)
            turned[span, :rows] = keep[kind, far].T
            turned[span, rows:] = got[kind, far].T
        for place in range(4):
            left = own[place][...] if kind == 2 else own[place]
            right = sib[place][...] if kind == 2 else sib[place]
            value = dot32(turned[:, :rows], left, 1, 0) + dot32(turned[:, rows:], right, 1, 0)
            store(value, (meta[4] ^ place) if kind == 2 else place, first)


def tokens_kernel(meta, *refs):
    resid, parts, pieces = refs[0], refs[1:5], refs[5:13]
    out, weight, sems = refs[13:]
    copies = piece_copies(meta, pieces, pl.ds(0, weight.shape[2]), weight, sems, 0)
    for copy in copies:
        copy.start()
    total = resid[...]
    for copy in copies:
        copy.wait()
    for step in range(4):
        total = total + dot32(parts[step][...], weight[meta[4] ^ step], 1, 1)
    out[...] = low(total)


def per_device_rows(
    tokens,
    lengths,
    cotangent,
    w_query,
    w_key,
    w_value,
    b_query,
    b_value,
    w_out,
    b_out,
    ln1_gain,
    ln1_shift,
    w_up,
    b_up,
    w_down,
    b_down,
    ln2_gain,
    ln2_shift,
):
    sequences, local_rows, model = tokens.shape
    x, f, z = lax.axis_index("ctx"), lax.axis_index("fsdp"), lax.axis_index("tp")
    rows = local_rows // 2
    width = w_query.shape[1]
    heads = width // HEAD_DIM
    hidden = w_up.shape[1]
    shard = w_query.shape[0]
    half = shard // 2
    padded = -(-width // 128) * 128
    own_seq, own_place = z % 2, z // 2
    quarter = 2 * x + own_place
    length_of = lambda place: lax.dynamic_index_in_dim(lengths, place, 0, keepdims=False)
    meta = jnp.stack(
        [x, z, f, length_of(x), quarter, own_seq, own_place, z ^ (2 * x), length_of(own_seq)]
    ).astype(jnp.int32)
    smem = pl.BlockSpec(memory_space=pltpu.SMEM)

    other = swapped(lax.dynamic_index_in_dim(tokens, 1 - x, 0, keepdims=False), "ctx", 1)
    per_head = lambda weights: jnp.concatenate(
        [
            weight[..., head * HEAD_DIM : (head + 1) * HEAD_DIM]
            for head in range(heads)
            for weight in weights
        ],
        axis=-1,
    )
    qkv_shard = per_head((w_query, w_key, w_value))
    qkv_bias = wide(per_head((b_query, jnp.zeros_like(b_query), b_value)))[None, :]
    qkv_y = swapped(qkv_shard, "fsdp", 2)
    qkv_pieces = (qkv_shard, swapped(qkv_shard, "fsdp", 1), qkv_y, swapped(qkv_y, "fsdp", 1))

    vectors = jnp.stack([b_out, ln1_gain, ln1_shift, b_down, ln2_gain, ln2_shift])
    pair = jnp.stack([vectors, swapped(vectors, "fsdp", 1)])
    gathered = jnp.concatenate([pair, swapped(pair, "fsdp", 2)])
    vectors = wide(xor_ordered(gathered, f).transpose(1, 0, 2).reshape(6, model))
    up_near = jnp.stack([b_up, swapped(b_up, "tp", 1)])
    up_bias = wide(xor_ordered(jnp.concatenate([up_near, swapped(up_near, "tp", 2)]), z))

    take_half = lambda pack: lax.dynamic_slice_in_dim(pack, x * half, half, 0)
    pack_a = jnp.concatenate(
        [w_up, w_out.T, jnp.zeros((shard, padded - width), jnp.bfloat16)], axis=1
    )
    pieces_a = spread_pack(take_half(pack_a), True)
    pieces_b = spread_pack(take_half(w_down.T), False)
    pieces_c = spread_pack(take_half(qkv_shard), True)

    qkv, *parts, stats = attend_call(meta, tokens, other, qkv_pieces, qkv_bias, heads)
    att = [to_owner(part, step) for step, part in enumerate(parts)]

    def row_spec(array):
        return pl.BlockSpec((1, rows, model), lambda step, meta: (meta[5], meta[6], 0))

    one = lambda *refs: refs
    vm = lambda shape, dtype=jnp.bfloat16: pltpu.VMEM(shape, dtype)
    weights_scratch = [vm((4, model, padded)), vm((4, model, hidden))]
    grid = lambda inputs, outputs, scratch: pltpu.PrefetchScalarGridSpec(
        num_scalar_prefetch=1, grid=(1,), in_specs=inputs, out_specs=outputs, scratch_shapes=scratch
    )
    full = lambda shape: pl.BlockSpec(shape, lambda step, meta: (0,) * len(shape))
    specs = lambda shapes: [full(item.shape) for item in shapes]

    first_out = [
        struct((rows, model), jnp.float32),
        struct((rows, 1), jnp.float32),
        struct((4, rows, hidden)),
        struct((4, rows, hidden)),
    ]
    hat, inverse, active, slope = pl.pallas_call(
        lambda *refs: first_kernel(*refs, width=width),
        grid_spec=grid(
            [full((rows, width))] * 4
            + [row_spec(tokens), full((6, model)), full((4, hidden))]
            + [ANY] * 8,
            specs(first_out),
            weights_scratch + [pltpu.SemaphoreType.DMA((64,))],
        ),
        out_shape=first_out,
        cost_estimate=cost(2 * rows * model * (model + 4 * hidden), 12e6, rows * hidden * 8),
        name="feed_first",
    )(meta, *att, tokens, vectors, up_bias, *pieces_a)

    second_out = [
        struct((rows, model)),
        struct((rows, model), jnp.float32),
        *[struct((rows, width))] * 4,
        struct((4, rows, hidden)),
        struct((3, 2, rows, shard)),
        struct((3, 2, rows, shard)),
        struct((16, model), jnp.float32),
    ]
    output, resid, g0, g1, g2, g3, hidden_grad, keep, send, small = pl.pallas_call(
        lambda *refs: second_kernel(*refs, width=width),
        grid_spec=grid(
            specs(first_out) + [row_spec(cotangent), full((6, model))] + [ANY] * 16,
            specs(second_out),
            weights_scratch
            + [vm((4, model, hidden)), vm((4, rows, shard)), pltpu.SemaphoreType.DMA((96,))],
        ),
        out_shape=second_out,
        cost_estimate=cost(2 * rows * model * (model + 12 * hidden), 20e6),
        name="feed_second",
    )(meta, hat, inverse, active, slope, cotangent, vectors, *pieces_a, *pieces_b)

    grad_att = [to_owner(part, step, True) for step, part in enumerate((g0, g1, g2, g3))]

    core = lambda array: swapped(array, "fsdp", 1)
    half_pack = struct((4, half, 2 * hidden + padded))
    near_mine, near_theirs, far_mine, far_theirs = pl.pallas_call(
        lambda *refs: weights_kernel(*refs, width=width),
        grid_spec=grid(
            [full(keep.shape)] * 2 + [full(active.shape)] * 4 + [full((rows, width))] * 8,
            specs([half_pack] * 4),
            [vm((2 * shard, 2 * rows)), vm((2 * shard, hidden), jnp.float32)],
        ),
        out_shape=[half_pack] * 4,
        cost_estimate=cost(8 * rows * shard * (8 * hidden + 4 * width), 20e6),
        name="feed_weights",
    )(meta, keep, core(send), active, core(active), hidden_grad, core(hidden_grad), *att, *map(core, att))

    grad_full, *grad_parts = attend_back_call(meta, qkv, grad_att, parts, stats, heads)
    grad_rows = [to_owner(part, step) for step, part in enumerate(grad_parts)]
    token_rows = pl.pallas_call(
        tokens_kernel,
        grid_spec=grid(
            [full((rows, model))] + [full((rows, 3 * width))] * 4 + [ANY] * 8,
            full((rows, model)),
            [vm((4, model, 3 * width)), pltpu.SemaphoreType.DMA((32,))],
        ),
        out_shape=struct((rows, model)),
        cost_estimate=cost(24 * rows * model * width, 8e6),
        name="token_grads",
    )(meta, resid, *grad_rows, *pieces_c)

    def spread_rows(block, dtype):
        blocks = [item.astype(dtype) for item in line_gathered(block)]
        return jnp.stack([jnp.concatenate([blocks[seq], blocks[2 + seq]]) for seq in range(2)])

    output_full = spread_rows(output, jnp.bfloat16)
    grad_tokens = spread_rows(token_rows, jnp.float32)

    theirs = low(wide(near_theirs) + wide(swapped(far_theirs, "fsdp", 2)))
    mine = wide(near_mine) + wide(swapped(far_mine, "fsdp", 2))
    mine = low(mine + wide(swapped(theirs, "ctx", 1)))
    total = wide(lax.dynamic_index_in_dim(mine, z, 0, keepdims=False))
    for step in (1, 2, 3):
        piece = lax.dynamic_index_in_dim(mine, (z + step) % 4, 0, keepdims=False)
        total = total + wide(shifted(piece, "tp", step))
    total = low(total)
    other_half = swapped(total, "ctx", 1)
    total = wide(jnp.concatenate([jnp.where(x == 0, total, other_half), jnp.where(x == 0, other_half, total)]))
    grad_w_up = total[:, :hidden]
    grad_w_down = total[:, hidden : 2 * hidden].T
    grad_w_out = total[:, 2 * hidden : 2 * hidden + width].T

    own_half = lax.dynamic_index_in_dim(tokens, x, 0, keepdims=False)
    grad_w_qkv = dot32(own_half, grad_full[:local_rows], 0, 0) + dot32(other, grad_full[local_rows:], 0, 0)
    grad_w_qkv = jnp.concatenate(
        [
            grad_w_qkv.reshape(4, shard, 3 * width),
            jnp.broadcast_to(jnp.sum(wide(grad_full), axis=0), (4, 16, 3 * width)),
        ],
        axis=1,
    )
    at = lambda array, place: lax.dynamic_index_in_dim(array, place, 0, keepdims=False)
    sent = low(jnp.stack([at(grad_w_qkv, f ^ 1), at(grad_w_qkv, f ^ 3)]))
    kept = jnp.stack([at(grad_w_qkv, f), at(grad_w_qkv, f ^ 2)]) + wide(swapped(sent, "fsdp", 1))
    kept = low(kept[0] + wide(swapped(low(kept[1]), "fsdp", 2)))
    kept = wide(kept) + wide(swapped(kept, "ctx", 1))

    def unpack(array, part):
        return jnp.concatenate(
            [
                array[:, (3 * head + part) * HEAD_DIM : (3 * head + part + 1) * HEAD_DIM]
                for head in range(heads)
            ],
            axis=1,
        )

    grad_w_query, grad_w_key, grad_w_value = (unpack(kept[:shard], part) for part in range(3))
    grad_b_query, grad_b_value = (unpack(kept[shard : shard + 1], part)[0] for part in (0, 2))

    for axis, bit in (("fsdp", 1), ("fsdp", 2), ("ctx", 1), ("tp", 1), ("tp", 2)):
        small = small + swapped(small, axis, bit)
    small_own = lax.dynamic_slice_in_dim(small[:6], f * shard, shard, 1)
    grad_b_up = lax.dynamic_index_in_dim(small, 6 + z, 0, keepdims=False)
    return (
        output_full,
        grad_tokens,
        grad_w_query,
        grad_w_key,
        grad_w_value,
        grad_b_query,
        grad_b_value,
        grad_w_out,
        small_own[0],
        small_own[1],
        small_own[2],
        grad_w_up,
        grad_b_up,
        grad_w_down,
        small_own[3],
        small_own[4],
        small_own[5],
    )


def rows_path_fits(mesh, tokens, w_query, w_up):
    shape = dict(mesh.shape)
    return (
        shape["ctx"] == 2
        and shape["fsdp"] == 4
        and shape["tp"] == 4
        and tokens.shape[0] == 8
        and tokens.shape[1] % 1024 == 0
        and w_query.shape[0] == w_query.shape[1]
        and w_query.shape[0] % 768 == 0
        and w_up.shape[1] == 4 * w_up.shape[0]
    )


def solution(mesh):
    placed = (
        P("fsdp", "ctx", None),
        P("fsdp"),
        P("fsdp", "ctx", None),
        P("fsdp", "tp"),
        P("fsdp", "tp"),
        P("fsdp", "tp"),
        P("tp"),
        P("tp"),
        P("tp", "fsdp"),
        P("fsdp"),
        P("fsdp"),
        P("fsdp"),
        P("fsdp", "tp"),
        P("tp"),
        P("tp", "fsdp"),
        P("fsdp"),
        P("fsdp"),
        P("fsdp"),
    )
    def split(function):
        return jax.shard_map(
        function,
        mesh=mesh,
        in_specs=placed,
        out_specs=(
            P("fsdp", "ctx", None),
            P("fsdp", "ctx", None),
            P("fsdp", "tp"),
            P("fsdp", "tp"),
            P("fsdp", "tp"),
            P("tp"),
            P("tp"),
            P("tp", "fsdp"),
            P("fsdp"),
            P("fsdp"),
            P("fsdp"),
            P("fsdp", "tp"),
            P("tp"),
            P("tp", "fsdp"),
            P("fsdp"),
            P("fsdp"),
            P("fsdp"),
        ),
        check_vma=False,
    )

    def run(*arrays):
        fits = rows_path_fits(mesh, arrays[0], arrays[3], arrays[12])
        return split(per_device_rows if fits else per_device)(*arrays)

    return run
```

```python
import math

import jax
import jax.numpy as jnp
from jax import lax
from jax.experimental import pallas as pl
from jax.experimental.pallas import tpu as pltpu
from jax.sharding import PartitionSpec as P

HEAD_DIM = 64


epsilon = 1e-12
masked_score = -1e30


def passed_along(value, axis, steps):
    count = lax.axis_size(axis)
    pairs = [(source, (source + steps) % count) for source in range(count)]
    return lax.ppermute(value, axis, pairs)


def layer_norm(inputs, gain_vector, shift_vector):
    center = jnp.mean(inputs, axis=-1, keepdims=True)
    centered = inputs - center
    spread = jnp.mean(centered * centered, axis=-1, keepdims=True)
    return centered * lax.rsqrt(spread + epsilon) * gain_vector + shift_vector


def gelu_exact(inputs):
    return jax.nn.gelu(inputs, approximate=False)


def live_keys(lengths, first_key, key_count):
    places = first_key + lax.iota(jnp.int32, key_count)
    return (places[None, :] < lengths[:, None])[:, None, None, :]


def absorb(carried, queries, key_block, value_block, usable, score_scale):
    row_peak, row_total, summed = carried
    scores = (
        jnp.einsum("sqhe,skhe->shqk", queries, key_block, preferred_element_type=jnp.float32)
        * score_scale
    )
    masked = jnp.where(usable, scores, masked_score)
    new_peak = jnp.maximum(row_peak, jnp.max(masked, axis=-1))
    factor = jnp.exp(row_peak - new_peak)
    weights = jnp.where(usable, jnp.exp(masked - new_peak[..., None]), 0.0)
    row_total = row_total * factor + jnp.sum(weights, axis=-1)
    summed = summed * factor[..., None] + jnp.einsum(
        "shqk,skhe->shqe",
        weights.astype(jnp.bfloat16),
        value_block,
        preferred_element_type=jnp.float32,
    )
    return (new_peak, row_total, summed)


def block_grads(
    queries, grad_att, log_total, row_delta, key_block, value_block, usable, score_scale
):
    scores = (
        jnp.einsum("sqhe,skhe->shqk", queries, key_block, preferred_element_type=jnp.float32)
        * score_scale
    )
    masked = jnp.where(usable, scores, masked_score)
    weights = jnp.where(usable, jnp.exp(masked - log_total[..., None]), 0.0)
    grad_value = jnp.einsum(
        "shqk,sqhe->skhe",
        weights.astype(jnp.bfloat16),
        grad_att,
        preferred_element_type=jnp.float32,
    )
    grad_weights = jnp.einsum(
        "sqhe,skhe->shqk", grad_att, value_block, preferred_element_type=jnp.float32
    )
    grad_scores = (weights * (grad_weights - row_delta[..., None])).astype(jnp.bfloat16)
    grad_query = (
        jnp.einsum("shqk,skhe->sqhe", grad_scores, key_block, preferred_element_type=jnp.float32)
        * score_scale
    )
    grad_key = (
        jnp.einsum("shqk,sqhe->skhe", grad_scores, queries, preferred_element_type=jnp.float32)
        * score_scale
    )
    return (grad_query, grad_key, grad_value)


def per_device(
    tokens,
    lengths,
    cotangent,
    w_query,
    w_key,
    w_value,
    b_query,
    b_value,
    w_out,
    b_out,
    ln1_gain,
    ln1_shift,
    w_up,
    b_up,
    w_down,
    b_down,
    ln2_gain,
    ln2_shift,
):
    sequences, local_rows, model_width = tokens.shape
    token_count = sequences * local_rows
    ctx_count = lax.axis_size("ctx")
    ctx_index = lax.axis_index("ctx")
    (
        query_full,
        key_full,
        value_full,
        out_full,
        up_full,
        down_full,
        bias_out,
        gain_one,
        shift_one,
        bias_down,
        gain_two,
        shift_two,
    ) = (
        lax.all_gather(w_query, "fsdp", axis=0, tiled=True),
        lax.all_gather(w_key, "fsdp", axis=0, tiled=True),
        lax.all_gather(w_value, "fsdp", axis=0, tiled=True),
        lax.all_gather(w_out, "fsdp", axis=1, tiled=True),
        lax.all_gather(w_up, "fsdp", axis=0, tiled=True),
        lax.all_gather(w_down, "fsdp", axis=1, tiled=True),
        lax.all_gather(b_out, "fsdp", axis=0, tiled=True),
        lax.all_gather(ln1_gain, "fsdp", axis=0, tiled=True),
        lax.all_gather(ln1_shift, "fsdp", axis=0, tiled=True),
        lax.all_gather(b_down, "fsdp", axis=0, tiled=True),
        lax.all_gather(ln2_gain, "fsdp", axis=0, tiled=True),
        lax.all_gather(ln2_shift, "fsdp", axis=0, tiled=True),
    )
    flat_tokens = tokens.reshape(token_count, model_width)
    local_width = query_full.shape[1]
    head_count = local_width // HEAD_DIM
    score_scale = HEAD_DIM ** (-0.5)
    query_low = (
        jnp.dot(flat_tokens, query_full, preferred_element_type=jnp.float32)
        + b_query.astype(jnp.float32)
    ).astype(jnp.bfloat16)
    key_low = jnp.dot(flat_tokens, key_full, preferred_element_type=jnp.float32).astype(
        jnp.bfloat16
    )
    value_low = (
        jnp.dot(flat_tokens, value_full, preferred_element_type=jnp.float32)
        + b_value.astype(jnp.float32)
    ).astype(jnp.bfloat16)
    query_heads = query_low.reshape(sequences, local_rows, head_count, HEAD_DIM)
    key_local = key_low.reshape(sequences, local_rows, local_width)
    value_local = value_low.reshape(sequences, local_rows, local_width)
    query_first = ctx_index * local_rows
    start_state = (
        jnp.full((sequences, head_count, local_rows), masked_score, jnp.float32),
        jnp.zeros((sequences, head_count, local_rows), jnp.float32),
        jnp.zeros((sequences, head_count, local_rows, HEAD_DIM), jnp.float32),
    )
    key_part = lax.all_gather(key_local, "ctx", axis=1, tiled=True)
    value_part = lax.all_gather(value_local, "ctx", axis=1, tiled=True)
    key_count = key_part.shape[1]
    block_size = math.gcd(key_count, 512)

    def one_block(position, state_in):
        offset = position * block_size
        key_block = lax.dynamic_slice_in_dim(key_part, offset, block_size, 1).reshape(
            sequences, block_size, head_count, HEAD_DIM
        )
        value_block = lax.dynamic_slice_in_dim(value_part, offset, block_size, 1).reshape(
            sequences, block_size, head_count, HEAD_DIM
        )
        usable = live_keys(lengths, offset, block_size)
        return absorb(state_in, query_heads, key_block, value_block, usable, score_scale)

    row_peak, row_total, summed = lax.fori_loop(0, key_count // block_size, one_block, start_state)
    attended = (summed / row_total[..., None]).transpose(0, 2, 1, 3)
    log_total = row_peak + jnp.log(row_total)
    attended_low = attended.reshape(token_count, local_width).astype(jnp.bfloat16)
    branch = lax.psum(
        jnp.dot(attended_low, out_full, preferred_element_type=jnp.float32).astype(jnp.bfloat16),
        "tp",
    ).astype(jnp.float32) + bias_out.astype(jnp.float32)
    normed_one, norm_one_back = jax.vjp(
        layer_norm,
        flat_tokens.astype(jnp.float32) + branch,
        gain_one.astype(jnp.float32),
        shift_one.astype(jnp.float32),
    )
    normed_low = normed_one.astype(jnp.bfloat16)
    hidden_in = jnp.dot(normed_low, up_full, preferred_element_type=jnp.float32) + b_up.astype(
        jnp.float32
    )
    active, gelu_back = jax.vjp(gelu_exact, hidden_in)
    active_low = active.astype(jnp.bfloat16)
    second = lax.psum(
        jnp.dot(active_low, down_full, preferred_element_type=jnp.float32).astype(jnp.bfloat16),
        "tp",
    ).astype(jnp.float32) + bias_down.astype(jnp.float32)
    output, norm_two_back = jax.vjp(
        layer_norm, normed_one + second, gain_two.astype(jnp.float32), shift_two.astype(jnp.float32)
    )
    positions = query_first + lax.iota(jnp.int32, local_rows)
    row_valid = (positions[None, :] < lengths[:, None]).astype(jnp.float32).reshape(token_count, 1)
    grad_output = cotangent.reshape(token_count, model_width).astype(jnp.float32) * row_valid
    grad_resid_two, grad_gain_two, grad_shift_two = norm_two_back(grad_output)
    grad_second = grad_resid_two.astype(jnp.bfloat16)
    grad_w_down = jnp.einsum(
        "nf,nd->fd", active_low, grad_second, preferred_element_type=jnp.float32
    )
    grad_b_down = jnp.sum(grad_second.astype(jnp.float32), axis=0)
    (grad_hidden,) = gelu_back(
        jnp.einsum("nd,fd->nf", grad_second, down_full, preferred_element_type=jnp.float32)
    )
    grad_hidden_low = grad_hidden.astype(jnp.bfloat16)
    grad_w_up = jnp.einsum(
        "nd,nf->df", normed_low, grad_hidden_low, preferred_element_type=jnp.float32
    )
    grad_b_up = jnp.sum(grad_hidden_low.astype(jnp.float32), axis=0)
    grad_normed = grad_resid_two + lax.psum(
        jnp.einsum(
            "nf,df->nd", grad_hidden_low, up_full, preferred_element_type=jnp.float32
        ).astype(jnp.bfloat16),
        "tp",
    ).astype(jnp.float32)
    grad_resid_one, grad_gain_one, grad_shift_one = norm_one_back(grad_normed)
    grad_branch = grad_resid_one.astype(jnp.bfloat16)
    grad_w_out = jnp.einsum(
        "nc,nd->cd", attended_low, grad_branch, preferred_element_type=jnp.float32
    )
    grad_b_out = jnp.sum(grad_branch.astype(jnp.float32), axis=0)
    grad_att = jnp.einsum(
        "nd,cd->nc", grad_branch, out_full, preferred_element_type=jnp.float32
    ).astype(jnp.bfloat16)
    grad_att_heads = grad_att.reshape(sequences, local_rows, head_count, HEAD_DIM)
    row_delta = jnp.sum(grad_att_heads.astype(jnp.float32) * attended, axis=-1).transpose(0, 2, 1)
    zero_block = jnp.zeros((sequences, local_rows, head_count, HEAD_DIM), jnp.float32)

    def turn_grads(first_key, key_block, value_block):
        usable = live_keys(lengths, first_key, local_rows)
        key_heads = key_block.reshape(sequences, local_rows, head_count, HEAD_DIM)
        value_heads = value_block.reshape(sequences, local_rows, head_count, HEAD_DIM)
        return block_grads(
            query_heads,
            grad_att_heads,
            log_total,
            row_delta,
            key_heads,
            value_heads,
            usable,
            score_scale,
        )

    def cycle_turn(turn_index, carried):
        key_block, value_block, grad_key, grad_value, grad_query = carried
        source = (ctx_index - turn_index) % ctx_count
        added_query, added_key, added_value = turn_grads(
            source * local_rows, key_block, value_block
        )
        key_block, value_block = passed_along((key_block, value_block), "ctx", 1)
        grad_key, grad_value = (
            passed_along((grad_key + added_key).astype(jnp.bfloat16), "ctx", 1).astype(jnp.float32),
            passed_along((grad_value + added_value).astype(jnp.bfloat16), "ctx", 1).astype(
                jnp.float32
            ),
        )
        return (key_block, value_block, grad_key, grad_value, grad_query + added_query)

    cycle_end = lax.fori_loop(
        0, ctx_count, cycle_turn, (key_local, value_local, zero_block, zero_block, zero_block)
    )
    grad_key, grad_value, grad_query = (cycle_end[2], cycle_end[3], cycle_end[4])
    grad_query_low = grad_query.reshape(token_count, local_width).astype(jnp.bfloat16)
    grad_key_low = grad_key.reshape(token_count, local_width).astype(jnp.bfloat16)
    grad_value_low = grad_value.reshape(token_count, local_width).astype(jnp.bfloat16)
    grad_w_query = jnp.einsum(
        "nd,nc->dc", flat_tokens, grad_query_low, preferred_element_type=jnp.float32
    )
    grad_w_key = jnp.einsum(
        "nd,nc->dc", flat_tokens, grad_key_low, preferred_element_type=jnp.float32
    )
    grad_w_value = jnp.einsum(
        "nd,nc->dc", flat_tokens, grad_value_low, preferred_element_type=jnp.float32
    )
    grad_b_query = jnp.sum(grad_query_low.astype(jnp.float32), axis=0)
    grad_b_value = jnp.sum(grad_value_low.astype(jnp.float32), axis=0)
    back_in = (
        jnp.einsum("nc,dc->nd", grad_query_low, query_full, preferred_element_type=jnp.float32)
        + jnp.einsum("nc,dc->nd", grad_key_low, key_full, preferred_element_type=jnp.float32)
        + jnp.einsum("nc,dc->nd", grad_value_low, value_full, preferred_element_type=jnp.float32)
    )
    grad_tokens = grad_resid_one + lax.psum(back_in.astype(jnp.bfloat16), "tp").astype(jnp.float32)
    (
        share_query,
        share_key,
        share_value,
        share_out,
        share_up,
        share_down,
        share_bias_out,
        share_gain_one,
        share_shift_one,
        share_bias_down,
        share_gain_two,
        share_shift_two,
    ) = (
        lax.psum_scatter(
            grad_w_query.astype(jnp.bfloat16), "fsdp", scatter_dimension=0, tiled=True
        ).astype(jnp.float32),
        lax.psum_scatter(
            grad_w_key.astype(jnp.bfloat16), "fsdp", scatter_dimension=0, tiled=True
        ).astype(jnp.float32),
        lax.psum_scatter(
            grad_w_value.astype(jnp.bfloat16), "fsdp", scatter_dimension=0, tiled=True
        ).astype(jnp.float32),
        lax.psum_scatter(
            grad_w_out.astype(jnp.bfloat16), "fsdp", scatter_dimension=1, tiled=True
        ).astype(jnp.float32),
        lax.psum_scatter(
            grad_w_up.astype(jnp.bfloat16), "fsdp", scatter_dimension=0, tiled=True
        ).astype(jnp.float32),
        lax.psum_scatter(
            grad_w_down.astype(jnp.bfloat16), "fsdp", scatter_dimension=1, tiled=True
        ).astype(jnp.float32),
        lax.psum_scatter(
            grad_b_out.astype(jnp.bfloat16), "fsdp", scatter_dimension=0, tiled=True
        ).astype(jnp.float32),
        lax.psum_scatter(
            grad_gain_one.astype(jnp.bfloat16), "fsdp", scatter_dimension=0, tiled=True
        ).astype(jnp.float32),
        lax.psum_scatter(
            grad_shift_one.astype(jnp.bfloat16), "fsdp", scatter_dimension=0, tiled=True
        ).astype(jnp.float32),
        lax.psum_scatter(
            grad_b_down.astype(jnp.bfloat16), "fsdp", scatter_dimension=0, tiled=True
        ).astype(jnp.float32),
        lax.psum_scatter(
            grad_gain_two.astype(jnp.bfloat16), "fsdp", scatter_dimension=0, tiled=True
        ).astype(jnp.float32),
        lax.psum_scatter(
            grad_shift_two.astype(jnp.bfloat16), "fsdp", scatter_dimension=0, tiled=True
        ).astype(jnp.float32),
    )
    (
        share_query,
        share_key,
        share_value,
        share_out,
        share_up,
        share_down,
        share_bias_out,
        share_gain_one,
        share_shift_one,
        share_bias_down,
        share_gain_two,
        share_shift_two,
    ) = (
        lax.psum(share_query.astype(jnp.bfloat16), "ctx").astype(jnp.float32),
        lax.psum(share_key.astype(jnp.bfloat16), "ctx").astype(jnp.float32),
        lax.psum(share_value.astype(jnp.bfloat16), "ctx").astype(jnp.float32),
        lax.psum(share_out.astype(jnp.bfloat16), "ctx").astype(jnp.float32),
        lax.psum(share_up.astype(jnp.bfloat16), "ctx").astype(jnp.float32),
        lax.psum(share_down.astype(jnp.bfloat16), "ctx").astype(jnp.float32),
        lax.psum(share_bias_out.astype(jnp.bfloat16), "ctx").astype(jnp.float32),
        lax.psum(share_gain_one.astype(jnp.bfloat16), "ctx").astype(jnp.float32),
        lax.psum(share_shift_one.astype(jnp.bfloat16), "ctx").astype(jnp.float32),
        lax.psum(share_bias_down.astype(jnp.bfloat16), "ctx").astype(jnp.float32),
        lax.psum(share_gain_two.astype(jnp.bfloat16), "ctx").astype(jnp.float32),
        lax.psum(share_shift_two.astype(jnp.bfloat16), "ctx").astype(jnp.float32),
    )
    total_b_query, total_b_value, total_b_up = lax.psum(
        (grad_b_query, grad_b_value, grad_b_up), ("fsdp", "ctx")
    )
    return (
        output.astype(jnp.bfloat16).reshape(sequences, local_rows, model_width),
        grad_tokens.reshape(sequences, local_rows, model_width),
        share_query,
        share_key,
        share_value,
        total_b_query,
        total_b_value,
        share_out,
        share_bias_out,
        share_gain_one,
        share_shift_one,
        share_up,
        total_b_up,
        share_down,
        share_bias_down,
        share_gain_two,
        share_shift_two,
    )


def swapped(value, axis, bit):
    count = lax.axis_size(axis)
    return lax.ppermute(value, axis, [(place, place ^ bit) for place in range(count)])


def shifted(value, axis, steps):
    count = lax.axis_size(axis)
    return lax.ppermute(value, axis, [(place, (place + steps) % count) for place in range(count)])


def to_owner(value, step, back=False):
    pairs = []
    for x in range(2):
        for z in range(4):
            block = z ^ step
            source = x * 4 + z
            target = (block >> 1) * 4 + 2 * (block & 1) + x
            pairs.append((target, source) if back else (source, target))
    return lax.ppermute(value, ("ctx", "tp"), pairs)


ANY = pl.BlockSpec(memory_space=pl.ANY)
WHOLE = pl.BlockSpec(memory_space=pltpu.VMEM)
log2_e = math.log2(math.e)
EXTRA = 8


def low(value):
    return value.astype(jnp.bfloat16)


def wide(value):
    return value.astype(jnp.float32)


def dot32(left, right, left_dim, right_dim):
    return lax.dot_general(
        left, right, (((left_dim,), (right_dim,)), ((), ())), preferred_element_type=jnp.float32
    )


def struct(shape, dtype=jnp.bfloat16):
    return jax.ShapeDtypeStruct(shape, dtype)


def cost(flops, moved, special=0):
    return pl.CostEstimate(flops=int(flops), bytes_accessed=int(moved), transcendentals=int(special))


def stack_kernel(*refs):
    for place, ref in enumerate(refs[:-1]):
        refs[-1][place] = ref[...]


def stacked(pieces):
    shape = (len(pieces),) + pieces[0].shape
    return pl.pallas_call(
        stack_kernel,
        out_shape=struct(shape),
        in_specs=[WHOLE] * len(pieces),
        out_specs=WHOLE,
        cost_estimate=cost(0, 4 * math.prod(shape)),
        name="stack_pieces",
    )(*pieces)


def line_stack(own_half):
    far = swapped(own_half, "tp", 2)
    return stacked([own_half, swapped(own_half, "tp", 1), far, swapped(far, "tp", 1)])


def piece_copies(meta, pieces, taken, columns, target, sems, first):
    x, z, f = meta[0], meta[1], meta[2]
    copies = []
    parts = [(piece, step) for piece in pieces for step in range(piece.shape[0])]
    for index, (piece, step) in enumerate(parts):
        place, slot = index // 4, index % 4
        across = (place % 2, 2 * ((place // 2) % 2) + place // 4)
        start = pl.multiple_of(((f ^ across[1]) * 2 + (x ^ across[0])) * taken, taken)
        copies.append(
            pltpu.make_async_copy(
                piece.at[step, pl.ds(0, taken), columns],
                target.at[z ^ slot, pl.ds(start, taken), :],
                sems.at[first + len(copies)],
            )
        )
    return copies


def attend_kernel(
    meta, own, other, w0, w1, w2, w3, bias, qkv, o0, o1, o2, o3, stats, weight, vectors,
    mask, shards, *, block, heads
):
    step = pl.program_id(0)
    shard = w0.shape[0] - EXTRA
    half = own.shape[1]
    scale = log2_e * HEAD_DIM ** (-0.5)

    @pl.when(step == 0)
    def _():
        for place, piece in enumerate((w0, w1, w2, w3)):
            start = pl.multiple_of((meta[2] ^ place) * shard, shard)
            weight[pl.ds(start, shard), :] = piece[:shard, :]
            shards[meta[2] ^ place] = piece[shard:, :]
        vectors[6:8, :] = jnp.zeros((2, 4 * shard), jnp.float32)
        for place in range(4):
            for row in range(6):
                first = row % 3 * shard
                vectors[row : row + 1, place * shard : (place + 1) * shard] = wide(
                    shards[place, row // 3 : row // 3 + 1, first : first + shard]
                )
        for place, rows in enumerate((own, other)):
            source = rows[0] if place == 0 else rows[...]
            qkv[place * half : (place + 1) * half, :] = low(
                dot32(source, weight[...], 1, 0) + bias[...]
            )
            first = (meta[0] ^ place) * half
            position = first + lax.broadcasted_iota(jnp.int32, (half, block), 0)
            mask[place * half : (place + 1) * half, :] = jnp.where(
                position < meta[3], 0.0, masked_score
            )

    rows = pl.ds(pl.multiple_of((meta[7] ^ step) * block, block), block)
    outs, logs = [], []
    for head in range(heads):
        base = 3 * head * HEAD_DIM
        query = qkv[rows, base : base + HEAD_DIM]
        key = qkv[:, base + HEAD_DIM : base + 2 * HEAD_DIM]
        value = qkv[:, base + 2 * HEAD_DIM : base + 3 * HEAD_DIM]
        scores = dot32(key, query, 1, 1) * scale + mask[...]
        peak = jnp.max(scores, axis=0, keepdims=True)
        weights = jnp.exp2(scores - peak)
        total = jnp.sum(weights, axis=0, keepdims=True)
        outs.append((dot32(value, low(weights), 0, 0) / total).T)
        logs.append(peak + jnp.log2(total))
    result = low(jnp.concatenate(outs, axis=1))
    for place, out in enumerate((o0, o1, o2, o3)):

        @pl.when(step == place)
        def _(out=out):
            out[...] = result

    stats[0] = jnp.concatenate(logs + [jnp.zeros((8 - heads, block), jnp.float32)], axis=0)


def attend_call(meta, tokens, other, pieces, bias, heads):
    half, width = other.shape
    block = half // 2
    columns = pieces[0].shape[1]
    whole = lambda shape: pl.BlockSpec(shape, lambda step, meta: (0,) * len(shape))
    rows = 2 * half
    return pl.pallas_call(
        lambda *refs: attend_kernel(*refs, block=block, heads=heads),
        grid_spec=pltpu.PrefetchScalarGridSpec(
            num_scalar_prefetch=1,
            grid=(4,),
            in_specs=[
                pl.BlockSpec((1, half, width), lambda step, meta: (meta[0], 0, 0)),
                whole((half, width)),
                *[whole(piece.shape) for piece in pieces],
                whole((1, columns)),
            ],
            out_specs=[
                whole((rows, columns)),
                *[whole((block, columns // 3))] * 4,
                pl.BlockSpec((1, 8, block), lambda step, meta: (step, 0, 0)),
                whole((width, columns)),
                whole((EXTRA, width)),
            ],
            scratch_shapes=[
                pltpu.VMEM((rows, block), jnp.float32),
                pltpu.VMEM((4, EXTRA, columns), jnp.bfloat16),
            ],
        ),
        out_shape=[struct((rows, columns))]
        + [struct((block, columns // 3))] * 4
        + [struct((4, 8, block), jnp.float32), struct((width, columns))]
        + [struct((EXTRA, width), jnp.float32)],
        cost_estimate=cost(2 * rows * width * columns + 16 * rows * rows * columns, 8e6, rows * rows * 3),
        name="attend",
    )(meta, tokens, other, *pieces, bias)


def attend_back_kernel(
    meta, qkv, d0, d1, d2, d3, o0, o1, o2, o3, stats, weight, full, p0, p1, p2, p3,
    grads, mask, grad_att, attended, *, block, heads
):
    step = pl.program_id(0)
    rows_all = qkv.shape[0]
    half = rows_all // 2
    scale = log2_e * HEAD_DIM ** (-0.5)

    @pl.when(step == 0)
    def _():
        grads[...] = jnp.zeros_like(grads)
        for place in range(2):
            first = (meta[0] ^ place) * half
            position = first + lax.broadcasted_iota(jnp.int32, (half, block), 0)
            mask[place * half : (place + 1) * half, :] = jnp.where(
                position < meta[3], 0.0, masked_score
            )

    for place, (grad, out) in enumerate(zip((d0, d1, d2, d3), (o0, o1, o2, o3))):

        @pl.when(step == place)
        def _(grad=grad, out=out):
            grad_att[...] = grad[...]
            attended[...] = out[...]

    rows = pl.ds(pl.multiple_of((meta[7] ^ step) * block, block), block)
    for head in range(heads):
        base = 3 * head * HEAD_DIM
        span = slice(head * HEAD_DIM, (head + 1) * HEAD_DIM)
        query = qkv[rows, base : base + HEAD_DIM]
        key = qkv[:, base + HEAD_DIM : base + 2 * HEAD_DIM]
        value = qkv[:, base + 2 * HEAD_DIM : base + 3 * HEAD_DIM]
        grad_out = grad_att[:, span]
        products = wide(grad_out) * wide(attended[:, span])
        delta = lax.dot_general(
            jnp.ones((8, HEAD_DIM), jnp.float32),
            products,
            (((1,), (1,)), ((), ())),
            precision=lax.Precision.HIGHEST,
            preferred_element_type=jnp.float32,
        )[:1]
        scores = dot32(key, query, 1, 1) * scale + mask[...]
        weights = jnp.exp2(scores - stats[0, head : head + 1, :])
        grad_weights = dot32(value, grad_out, 1, 1)
        grad_scores = low(weights * (grad_weights - delta))
        grads[2 * head] += dot32(grad_scores, query, 1, 0)
        grads[2 * head + 1] += dot32(low(weights), grad_out, 1, 0)
        full[rows, base : base + HEAD_DIM] = low(
            dot32(grad_scores, key, 0, 0) * HEAD_DIM ** (-0.5)
        )

    @pl.when(step == 3)
    def _():
        for head in range(heads):
            base = 3 * head * HEAD_DIM
            full[:, base + HEAD_DIM : base + 2 * HEAD_DIM] = low(
                grads[2 * head] * HEAD_DIM ** (-0.5)
            )
            full[:, base + 2 * HEAD_DIM : base + 3 * HEAD_DIM] = low(grads[2 * head + 1])
        for place, part in enumerate((p0, p1, p2, p3)):
            span = pl.ds(pl.multiple_of((meta[7] ^ place) * block, block), block)
            part[...] = low(dot32(full[span, :], weight[...], 1, 1))


def attend_back_call(meta, qkv, grad_parts, parts, stats, weight, heads):
    rows, columns = qkv.shape
    width = weight.shape[0]
    block = rows // 4
    whole = lambda shape: pl.BlockSpec(shape, lambda step, meta: (0,) * len(shape))
    small = whole((block, columns // 3))
    return pl.pallas_call(
        lambda *refs: attend_back_kernel(*refs, block=block, heads=heads),
        grid_spec=pltpu.PrefetchScalarGridSpec(
            num_scalar_prefetch=1,
            grid=(4,),
            in_specs=[whole((rows, columns))]
            + [small] * 8
            + [pl.BlockSpec((1, 8, block), lambda step, meta: (step, 0, 0)), whole(weight.shape)],
            out_specs=[whole((rows, columns))] + [whole((block, width))] * 4,
            scratch_shapes=[
                pltpu.VMEM((2 * heads, rows, HEAD_DIM), jnp.float32),
                pltpu.VMEM((rows, block), jnp.float32),
                pltpu.VMEM((block, columns // 3), jnp.bfloat16),
                pltpu.VMEM((block, columns // 3), jnp.bfloat16),
            ],
        ),
        out_shape=[struct((rows, columns))] + [struct((block, width))] * 4,
        cost_estimate=cost(40 * rows * rows * columns, 8e6, rows * rows * 3),
        name="attend_back",
    )(meta, qkv, *grad_parts, *parts, stats, weight)


def norm_parts(inputs):
    center = jnp.mean(inputs, axis=-1, keepdims=True)
    centered = inputs - center
    spread = jnp.mean(centered * centered, axis=-1, keepdims=True)
    inverse = lax.rsqrt(spread + epsilon)
    return centered * inverse, inverse


def norm_back(grad_out, hat, inverse, gain):
    scaled = grad_out * gain
    return inverse * (
        scaled
        - jnp.mean(scaled, axis=-1, keepdims=True)
        - hat * jnp.mean(scaled * hat, axis=-1, keepdims=True)
    )


BIAS_OUT, GAIN_ONE, SHIFT_ONE, BIAS_DOWN, GAIN_TWO, SHIFT_TWO = range(6)


def first_kernel(meta, *refs, width):
    att, tok, vectors, lines, pieces = refs[:4], refs[4], refs[5], refs[6], refs[7:15]
    hat, inverse, both, slope, out_w, up_w, sems = refs[15:]
    hidden = up_w.shape[2]
    taken = pieces[0].shape[1]
    copies = piece_copies(meta, pieces, taken, pl.ds(hidden, out_w.shape[2]), out_w, sems, 0)
    copies += piece_copies(meta, pieces, taken, pl.ds(0, hidden), up_w, sems, 32)
    for copy in copies:
        copy.start()
    for step in range(4):
        both[step, :, hidden : hidden + width] = att[step][...]
        both[step, :, hidden + width :] = jnp.zeros_like(both[step, :, hidden + width :])
    for copy in copies:
        copy.wait()
    branch = vectors[BIAS_OUT : BIAS_OUT + 1, :]
    for step in range(4):
        branch = branch + dot32(att[step][...], out_w[meta[4] ^ step][:, :width], 1, 1)
    hat_one, inverse_one = norm_parts(wide(tok[0]) + branch)
    hat[...] = hat_one
    inverse[...] = inverse_one
    normed = low(hat_one * vectors[GAIN_ONE : GAIN_ONE + 1, :] + vectors[SHIFT_ONE : SHIFT_ONE + 1, :])
    for place in range(4):
        inputs = dot32(normed, up_w[place], 1, 0) + wide(lines[meta[1] ^ place, 0:1, :])
        cumulative = 0.5 * (1.0 + lax.erf(inputs * (0.5**0.5)))
        density = jnp.exp(-0.5 * inputs * inputs) * ((0.5 / math.pi) ** 0.5)
        both[place, :, :hidden] = low(inputs * cumulative)
        slope[place] = low(cumulative + inputs * density)


def second_kernel(meta, *refs, width):
    hat, inverse, both, slope, cot, vectors = refs[:6]
    pieces_a, pieces_b = refs[6:14], refs[14:24]
    output, resid, g0, g1, g2, g3, mixed, keep = refs[24:32]
    out_w, up_w, down_w, blocks, small, small_blocks, sems = refs[32:]
    rows, model = hat.shape
    hidden = up_w.shape[2]
    taken = pieces_a[0].shape[1]
    down_copies = piece_copies(meta, pieces_b, taken, pl.ds(0, hidden), down_w, sems, 0)
    copies = piece_copies(meta, pieces_a, taken, pl.ds(0, hidden), up_w, sems, 32)
    copies += piece_copies(meta, pieces_a, taken, pl.ds(hidden, out_w.shape[2]), out_w, sems, 64)
    for copy in down_copies + copies:
        copy.start()
    row = lambda place: vectors[place : place + 1, :]
    hat_one, inverse_one = hat[...], inverse[...]
    normed_one = hat_one * row(GAIN_ONE) + row(SHIFT_ONE)
    for copy in down_copies:
        copy.wait()
    second = row(BIAS_DOWN)
    for place in range(4):
        second = second + dot32(both[place, :, :hidden], down_w[place], 1, 1)
    hat_two, inverse_two = norm_parts(normed_one + second)
    output[...] = low(hat_two * row(GAIN_TWO) + row(SHIFT_TWO))
    position = meta[4] * rows + lax.broadcasted_iota(jnp.int32, (rows, model), 0)
    grad_output = jnp.where(position < meta[8], wide(cot[0]), 0.0)
    grad_two = norm_back(grad_output, hat_two, inverse_two, row(GAIN_TWO))
    grad_second = low(grad_two)
    for copy in copies:
        copy.wait()
    grad_normed = grad_two
    sums = lambda array: jnp.sum(array, axis=0, keepdims=True)
    for place in range(4):
        grad_hidden = low(dot32(grad_second, down_w[place], 1, 0) * wide(slope[place]))
        mixed[place, :rows, :] = grad_hidden
        mixed[place, rows:, :] = low(
            jnp.broadcast_to(sums(wide(grad_hidden)), (EXTRA, hidden))
        )
        grad_normed = grad_normed + dot32(grad_hidden, up_w[place], 1, 1)
    grad_one = norm_back(grad_normed, hat_one, inverse_one, row(GAIN_ONE))
    resid[...] = grad_one
    grad_branch = low(grad_one)
    for step, out in enumerate((g0, g1, g2, g3)):
        out[...] = low(dot32(grad_branch, out_w[meta[4] ^ step][:, :width], 1, 0))
    small[0:1, :] = sums(wide(grad_branch))
    small[1:2, :] = sums(grad_normed * hat_one)
    small[2:3, :] = sums(grad_normed)
    small[3:4, :] = sums(wide(grad_second))
    small[4:5, :] = sums(grad_output * hat_two)
    small[5:6, :] = sums(grad_output)
    small[6:8, :] = jnp.zeros((2, model), jnp.float32)
    shard = model // 4
    for place in range(4):
        small_blocks[place] = low(small[:, place * shard : (place + 1) * shard])
    for kind, array in enumerate((grad_second, low(normed_one), grad_branch)):
        for place in range(4):
            blocks[place] = array[:, place * shard : (place + 1) * shard]
        for far in range(2):
            keep[kind, far, :rows, :] = blocks[meta[2] ^ (2 * far)]
            keep[kind, far, rows:, :] = small_blocks[meta[2] ^ (2 * far)]
            columns = slice(kind * shard, (kind + 1) * shard)
            mixed[4 + far, :rows, columns] = blocks[meta[2] ^ (2 * far + 1)]
            mixed[4 + far, rows:, columns] = small_blocks[meta[2] ^ (2 * far + 1)]
    for far in range(2):
        mixed[4 + far, :, 3 * shard :] = jnp.zeros((rows + EXTRA, hidden - 3 * shard), jnp.bfloat16)


def weights_kernel(meta, *refs, width):
    keep, both, both_sib, mixed, mixed_sib = refs[:5]
    near_up, far_up, mine_down, theirs_down, turned, whole = refs[5:]
    shard = keep.shape[3]
    rows = both.shape[1]
    half = shard // 2
    hidden = mixed.shape[2]
    padded = both.shape[2] - hidden
    starts = [pl.multiple_of(side * half, half) for side in (meta[0], 1 - meta[0])]

    def slot(block):
        apart = block ^ meta[1]
        return 2 * (apart & 1) + (apart >> 1)

    for kind in range(3):
        for far in range(2):
            span = slice(far * shard, (far + 1) * shard)
            turned[span, :rows] = keep[kind, far, :rows, :].T
            turned[span, rows:] = mixed_sib[4 + far, :rows, kind * shard : (kind + 1) * shard].T
        for place in range(4):
            if kind == 1:
                left, right = mixed[place, :rows, :], mixed_sib[place, :rows, :]
            else:
                columns = slice(0, hidden) if kind == 0 else slice(hidden, None)
                left, right = both[place, :, columns], both_sib[place, :, columns]
            value = dot32(turned[:, :rows], left, 1, 0) + dot32(turned[:, rows:], right, 1, 0)
            target = slot(meta[4] ^ place if kind == 2 else place)
            count = value.shape[1]
            whole[:, :count] = value
            for far in range(2):
                for side, start in enumerate(starts):
                    part = low(whole[pl.ds(far * shard + start, half), :count])
                    if kind == 0:
                        kept = mine_down.shape[3]
                        (mine_down, theirs_down)[side][far, target, :half, :] = part[:, :kept]
                        (near_up, far_up)[far][side, target, :half, hidden + padded :] = part[:, kept:]
                    elif kind == 1:
                        (near_up, far_up)[far][side, target, :half, :hidden] = part
                    else:
                        (near_up, far_up)[far][side, target, :half, hidden : hidden + padded] = part
    for far in range(2):
        vector_sums = low(wide(keep[0, far, rows:, :]) + wide(mixed_sib[4 + far, rows:, :shard]))
        for place in range(4):
            hidden_sums = low(wide(mixed[place, rows:, :]) + wide(mixed_sib[place, rows:, :]))
            for side in range(2):
                out = (mine_down, theirs_down)[side]
                out[far, place, half:, :] = jnp.zeros((EXTRA, out.shape[3]), jnp.bfloat16)
                out = (near_up, far_up)[far]
                out[side, slot(place), half:, :hidden] = hidden_sums
                out[side, place, half:, hidden : hidden + shard] = vector_sums
                rest = slice(hidden + shard, None)
                out[side, place, half:, rest] = jnp.zeros_like(out[side, place, half:, rest])


def projections_kernel(meta, own, other, grads, kept, sent, whole):
    half, shard = other.shape[0], other.shape[1] // 4
    count = grads.shape[1]
    whole[...] = dot32(own[0], grads[:half, :], 0, 0) + dot32(other[...], grads[half:, :], 0, 0)
    sums = jnp.broadcast_to(jnp.sum(wide(grads[...]), axis=0, keepdims=True), (EXTRA, count))
    for far in range(2):
        for out, place in ((kept, meta[2] ^ (2 * far)), (sent, meta[2] ^ (2 * far + 1))):
            value = whole[pl.ds(pl.multiple_of(place * shard, shard), shard), :]
            out[far, :shard, :count] = value.astype(out.dtype)
            out[far, shard:, :count] = sums.astype(out.dtype)
            out[far, :, count:] = jnp.zeros_like(out[far, :, count:])


def per_device_rows(
    tokens,
    lengths,
    cotangent,
    w_query,
    w_key,
    w_value,
    b_query,
    b_value,
    w_out,
    b_out,
    ln1_gain,
    ln1_shift,
    w_up,
    b_up,
    w_down,
    b_down,
    ln2_gain,
    ln2_shift,
):
    sequences, local_rows, model = tokens.shape
    x, f, z = lax.axis_index("ctx"), lax.axis_index("fsdp"), lax.axis_index("tp")
    rows = local_rows // 2
    width = w_query.shape[1]
    heads = width // HEAD_DIM
    hidden = w_up.shape[1]
    shard = w_query.shape[0]
    half = shard // 2
    padded = -(-width // 128) * 128
    own_seq, own_place = z % 2, z // 2
    quarter = 2 * x + own_place
    length_of = lambda place: lax.dynamic_index_in_dim(lengths, place, 0, keepdims=False)
    entries = (x, z, f, length_of(x), quarter, own_seq, own_place, z ^ (2 * x), length_of(own_seq))
    places = lax.iota(jnp.int32, len(entries))
    meta = sum(jnp.where(places == place, entry, 0) for place, entry in enumerate(entries))
    meta = meta.astype(jnp.int32)
    tied = lambda *values: lax.optimization_barrier(values)

    take_half = lambda pack: lax.dynamic_slice_in_dim(pack, x * half, half, 0)
    wider = lambda array, columns: jnp.pad(array, ((0, 0), (0, columns - array.shape[1])))
    columns_a = hidden + padded
    half_a = wider(take_half(jnp.concatenate([w_up, w_out.T], axis=1)), columns_a)
    half_b = jnp.concatenate(
        [take_half(w_down.T), b_up[None], jnp.zeros((EXTRA - 1, hidden), jnp.bfloat16)]
    )

    other = lax.dynamic_index_in_dim(tokens, 1 - x, 0, keepdims=False)
    other, half_a = tied(other, half_a)
    other = swapped(other, "ctx", 1)
    line_a = line_stack(half_a)
    per_head = lambda weights: jnp.concatenate(
        [
            weight[..., head * HEAD_DIM : (head + 1) * HEAD_DIM]
            for head in range(heads)
            for weight in weights
        ],
        axis=-1,
    )
    vectors = jnp.concatenate([b_out, ln1_gain, ln1_shift, b_down, ln2_gain, ln2_shift])
    qkv_shard = jnp.concatenate(
        [
            per_head((w_query, w_key, w_value)),
            jnp.pad(vectors.reshape(2, 3 * width), ((0, EXTRA - 2), (0, 0))),
        ]
    )
    qkv_bias = wide(per_head((b_query, jnp.zeros_like(b_query), b_value)))[None, :]
    qkv_y = swapped(qkv_shard, "fsdp", 2)
    qkv_pieces = (qkv_shard, swapped(qkv_shard, "fsdp", 1), qkv_y, swapped(qkv_y, "fsdp", 1))

    core = lambda array: swapped(array, "fsdp", 1)
    meta, qkv_bias, other, line_a, half_b, *qkv_pieces = tied(
        meta, qkv_bias, other, line_a, half_b, *qkv_pieces
    )
    x_a, y_a = swapped(line_a, "ctx", 1), swapped(line_a, "fsdp", 2)
    qkv, *parts, stats, weight, vectors = attend_call(
        meta, tokens, other, qkv_pieces, qkv_bias, heads
    )
    b_pieces = [swapped(half_b, "tp", bit) for bit in (1, 2, 3)]

    x_a, y_a, line_a, *rest = tied(x_a, y_a, line_a, *b_pieces, *parts)
    b_pieces, parts = rest[:3], rest[3:]
    line_b = stacked([half_b, *b_pieces])
    att = [to_owner(part, step) for step, part in enumerate(parts)]
    x_y_a = swapped(x_a, "fsdp", 2)
    x_y_a, x_a, y_a, line_a, *att = tied(x_y_a, x_a, y_a, line_a, *att)
    near_a = (line_a, x_a, y_a, x_y_a)
    pieces_a = (*near_a, *map(core, near_a))
    x_b, y_b = swapped(line_b, "ctx", 1), swapped(line_b, "fsdp", 2)

    def row_spec(array):
        return pl.BlockSpec((1, rows, model), lambda step, meta: (meta[5], meta[6], 0))

    vm = lambda shape, dtype=jnp.bfloat16: pltpu.VMEM(shape, dtype)
    weights_scratch = [vm((4, model, padded)), vm((4, model, hidden))]
    grid = lambda inputs, outputs, scratch: pltpu.PrefetchScalarGridSpec(
        num_scalar_prefetch=1, grid=(1,), in_specs=inputs, out_specs=outputs, scratch_shapes=scratch
    )
    full = lambda shape: pl.BlockSpec(shape, lambda step, meta: (0,) * len(shape))
    specs = lambda shapes: [full(item.shape) for item in shapes]

    first_out = [
        struct((rows, model), jnp.float32),
        struct((rows, 1), jnp.float32),
        struct((4, rows, columns_a)),
        struct((4, rows, hidden)),
    ]
    hat, inverse, both, slope = pl.pallas_call(
        lambda *refs: first_kernel(*refs, width=width),
        grid_spec=grid(
            [full((rows, width))] * 4
            + [row_spec(tokens), full((EXTRA, model))]
            + [pl.BlockSpec((4, EXTRA, hidden), lambda step, meta: (0, half // EXTRA, 0))]
            + [ANY] * 8,
            specs(first_out),
            weights_scratch + [pltpu.SemaphoreType.DMA((64,))],
        ),
        out_shape=first_out,
        cost_estimate=cost(2 * rows * model * (model + 4 * hidden), 12e6, rows * hidden * 8),
        name="feed_first",
    )(meta, *att, tokens, vectors, line_b, *pieces_a)

    both, x_b, y_b, line_b = tied(both, x_b, y_b, line_b)
    x_y_b = [swapped(x_b[:2], "fsdp", 2), swapped(y_b[2:], "ctx", 1)]
    cores_b = [core(line_b), core(x_b), core(y_b)]
    rest = tied(*x_y_b, *cores_b)
    x_y_b, cores_b = rest[:2], rest[2:]
    both_sib = core(both)
    pieces_b = (line_b, x_b, y_b, *x_y_b, *cores_b, *map(core, x_y_b))

    second_out = [
        struct((rows, model)),
        struct((rows, model), jnp.float32),
        *[struct((rows, width))] * 4,
        struct((6, rows + EXTRA, hidden)),
        struct((3, 2, rows + EXTRA, shard)),
    ]
    output, resid, g0, g1, g2, g3, mixed, keep = pl.pallas_call(
        lambda *refs: second_kernel(*refs, width=width),
        grid_spec=grid(
            [full(item.shape) for item in (hat, inverse, both, slope)]
            + [row_spec(cotangent), full((EXTRA, model))]
            + [ANY] * 18,
            specs(second_out),
            weights_scratch
            + [
                vm((4, model, hidden)),
                vm((4, rows, shard)),
                vm((EXTRA, model), jnp.float32),
                vm((4, EXTRA, shard)),
                pltpu.SemaphoreType.DMA((96,)),
            ],
        ),
        out_shape=second_out,
        cost_estimate=cost(2 * rows * model * (model + 12 * hidden), 20e6),
        name="feed_second",
    )(meta, hat, inverse, both, slope, cotangent, vectors, *pieces_a, *pieces_b)

    grad_att = [to_owner(part, step, True) for step, part in enumerate((g0, g1, g2, g3))]

    first_x = 2 * padded
    pack = struct((2, 4, half + EXTRA, first_x))
    pack_up = struct((2, 4, half + EXTRA, columns_a + hidden - first_x))
    mixed_sib = core(mixed)
    near_up, far_up, mine_down, theirs_down = pl.pallas_call(
        lambda *refs: weights_kernel(*refs, width=width),
        grid_spec=grid(
            specs([keep, both, both_sib, mixed, mixed_sib]),
            specs([pack_up] * 2 + [pack] * 2),
            [vm((2 * shard, 2 * rows)), vm((2 * shard, hidden), jnp.float32)],
        ),
        out_shape=[pack_up] * 2 + [pack] * 2,
        cost_estimate=cost(8 * rows * shard * (8 * hidden + 4 * width), 20e6),
        name="feed_weights",
    )(meta, keep, both, both_sib, mixed, mixed_sib)

    far_up, theirs_down, *grad_att = tied(far_up, theirs_down, *grad_att)
    got_up, got_down = swapped(far_up, "fsdp", 2), swapped(theirs_down, "ctx", 1)
    far_z, near_z = swapped(output, "tp", 2), swapped(output, "tp", 1)
    grad_full, *grad_parts = attend_back_call(meta, qkv, grad_att, parts, stats, weight, heads)

    got_down, near_z, far_z, *grad_parts = tied(got_down, near_z, far_z, *grad_parts)
    grad_rows = [to_owner(part, step) for step, part in enumerate(grad_parts)]
    got_down, grad_full, grad_rows[0] = tied(got_down, grad_full, grad_rows[0])
    kept, sent = pl.pallas_call(
        projections_kernel,
        grid_spec=grid(
            [pl.BlockSpec((1, local_rows, model), lambda step, meta: (meta[0], 0, 0))]
            + [full((local_rows, model)), full(grad_full.shape)],
            [full((2, shard + EXTRA, 640 * width // 192))] * 2,
            [vm((model, 3 * width), jnp.float32)],
        ),
        out_shape=[
            struct((2, shard + EXTRA, 640 * width // 192), dtype) for dtype in (jnp.float32, jnp.bfloat16)
        ],
        cost_estimate=cost(12 * local_rows * model * width, 8e6),
        name="projection_weights",
    )(meta, tokens, other, grad_full)
    second_down = swapped(low(wide(mine_down[1]) + wide(got_down[1])), "fsdp", 2)
    got_up, second_down, kept, sent, far_z, *grad_rows = tied(
        got_up, second_down, kept, sent, far_z, *grad_rows
    )
    second_up = swapped(low(wide(near_up[1]) + wide(got_up[1])), "ctx", 1)
    token_rows = resid
    for part in grad_rows:
        token_rows = token_rows + wide(part)

    def spread_rows(pieces, dtype):
        blocks = [
            lax.select_n(z, *[pieces[block ^ place] for place in range(4)]).astype(dtype)
            for block in range(4)
        ]
        return jnp.stack([jnp.concatenate([blocks[seq], blocks[2 + seq]]) for seq in range(2)])

    token_rows = low(token_rows)
    up_lines = wide(near_up[0]) + wide(got_up[0]) + wide(second_up)
    down_lines = wide(mine_down[0]) + wide(got_down[0]) + wide(second_down)
    lines = jnp.concatenate([up_lines, down_lines], axis=2)
    lines, line_sent = lines[:2], low(lines[2:])
    lines = lines + wide(swapped(line_sent, "tp", 1))
    output_full = spread_rows([output, near_z, far_z, swapped(far_z, "tp", 1)], jnp.bfloat16)
    far_z, near_z = swapped(token_rows, "tp", 2), swapped(token_rows, "tp", 1)
    grad_tokens = spread_rows([token_rows, near_z, far_z, swapped(far_z, "tp", 1)], jnp.float32)
    total = low(lines[0] + wide(swapped(low(lines[1]), "tp", 2)))
    other_half = swapped(total, "ctx", 1)
    small = wide(total[half:])
    total = wide(
        jnp.concatenate(
            [
                jnp.where(x == 0, total[:half], other_half[:half]),
                jnp.where(x == 0, other_half[:half], total[:half]),
            ]
        )
    )
    grad_w_up = total[:, :hidden]
    tail = slice(columns_a, columns_a + hidden - first_x)
    grad_w_down = jnp.concatenate([total[:, tail.stop :], total[:, tail]], axis=1).T
    grad_w_out = total[:, hidden : hidden + width].T
    grad_b_up = small[0, :hidden]
    small_own = small[:, hidden : hidden + shard]

    kept = kept + wide(core(sent))
    kept = low(kept[0] + wide(swapped(low(kept[1]), "fsdp", 2)))
    kept = wide(kept) + wide(swapped(kept, "ctx", 1))

    def unpack(array, part):
        return jnp.concatenate(
            [
                array[:, (3 * head + part) * HEAD_DIM : (3 * head + part + 1) * HEAD_DIM]
                for head in range(heads)
            ],
            axis=1,
        )

    grad_w_query, grad_w_key, grad_w_value = (unpack(kept[:shard], part) for part in range(3))
    grad_b_query, grad_b_value = (unpack(kept[shard : shard + 1], part)[0] for part in (0, 2))
    return (
        output_full,
        grad_tokens,
        grad_w_query,
        grad_w_key,
        grad_w_value,
        grad_b_query,
        grad_b_value,
        grad_w_out,
        small_own[0],
        small_own[1],
        small_own[2],
        grad_w_up,
        grad_b_up,
        grad_w_down,
        small_own[3],
        small_own[4],
        small_own[5],
    )


def rows_path_fits(mesh, tokens, w_query, w_up):
    shape = dict(mesh.shape)
    return (
        shape["ctx"] == 2
        and shape["fsdp"] == 4
        and shape["tp"] == 4
        and tokens.shape[0] == 8
        and tokens.shape[1] % 1024 == 0
        and w_query.shape[0] == w_query.shape[1]
        and w_query.shape[0] % 768 == 0
        and w_up.shape[1] == 4 * w_up.shape[0]
    )


def solution(mesh):
    placed = (
        P("fsdp", "ctx", None),
        P("fsdp"),
        P("fsdp", "ctx", None),
        P("fsdp", "tp"),
        P("fsdp", "tp"),
        P("fsdp", "tp"),
        P("tp"),
        P("tp"),
        P("tp", "fsdp"),
        P("fsdp"),
        P("fsdp"),
        P("fsdp"),
        P("fsdp", "tp"),
        P("tp"),
        P("tp", "fsdp"),
        P("fsdp"),
        P("fsdp"),
        P("fsdp"),
    )
    def split(function):
        return jax.shard_map(
        function,
        mesh=mesh,
        in_specs=placed,
        out_specs=(
            P("fsdp", "ctx", None),
            P("fsdp", "ctx", None),
            P("fsdp", "tp"),
            P("fsdp", "tp"),
            P("fsdp", "tp"),
            P("tp"),
            P("tp"),
            P("tp", "fsdp"),
            P("fsdp"),
            P("fsdp"),
            P("fsdp"),
            P("fsdp", "tp"),
            P("tp"),
            P("tp", "fsdp"),
            P("fsdp"),
            P("fsdp"),
            P("fsdp"),
        ),
        check_vma=False,
    )

    def run(*arrays):
        fits = rows_path_fits(mesh, arrays[0], arrays[3], arrays[12])
        return split(per_device_rows if fits else per_device)(*arrays)

    return run
```

```python
import math

import jax
import jax.numpy as jnp
from jax import lax
from jax.experimental import pallas as pl
from jax.experimental.pallas import tpu as pltpu
from jax.sharding import PartitionSpec as P

HEAD_DIM = 64


epsilon = 1e-12
masked_score = -1e30


def passed_along(value, axis, steps):
    count = lax.axis_size(axis)
    pairs = [(source, (source + steps) % count) for source in range(count)]
    return lax.ppermute(value, axis, pairs)


def layer_norm(inputs, gain_vector, shift_vector):
    center = jnp.mean(inputs, axis=-1, keepdims=True)
    centered = inputs - center
    spread = jnp.mean(centered * centered, axis=-1, keepdims=True)
    return centered * lax.rsqrt(spread + epsilon) * gain_vector + shift_vector


def gelu_exact(inputs):
    return jax.nn.gelu(inputs, approximate=False)


def live_keys(lengths, first_key, key_count):
    places = first_key + lax.iota(jnp.int32, key_count)
    return (places[None, :] < lengths[:, None])[:, None, None, :]


def absorb(carried, queries, key_block, value_block, usable, score_scale):
    row_peak, row_total, summed = carried
    scores = (
        jnp.einsum("sqhe,skhe->shqk", queries, key_block, preferred_element_type=jnp.float32)
        * score_scale
    )
    masked = jnp.where(usable, scores, masked_score)
    new_peak = jnp.maximum(row_peak, jnp.max(masked, axis=-1))
    factor = jnp.exp(row_peak - new_peak)
    weights = jnp.where(usable, jnp.exp(masked - new_peak[..., None]), 0.0)
    row_total = row_total * factor + jnp.sum(weights, axis=-1)
    summed = summed * factor[..., None] + jnp.einsum(
        "shqk,skhe->shqe",
        weights.astype(jnp.bfloat16),
        value_block,
        preferred_element_type=jnp.float32,
    )
    return (new_peak, row_total, summed)


def block_grads(
    queries, grad_att, log_total, row_delta, key_block, value_block, usable, score_scale
):
    scores = (
        jnp.einsum("sqhe,skhe->shqk", queries, key_block, preferred_element_type=jnp.float32)
        * score_scale
    )
    masked = jnp.where(usable, scores, masked_score)
    weights = jnp.where(usable, jnp.exp(masked - log_total[..., None]), 0.0)
    grad_value = jnp.einsum(
        "shqk,sqhe->skhe",
        weights.astype(jnp.bfloat16),
        grad_att,
        preferred_element_type=jnp.float32,
    )
    grad_weights = jnp.einsum(
        "sqhe,skhe->shqk", grad_att, value_block, preferred_element_type=jnp.float32
    )
    grad_scores = (weights * (grad_weights - row_delta[..., None])).astype(jnp.bfloat16)
    grad_query = (
        jnp.einsum("shqk,skhe->sqhe", grad_scores, key_block, preferred_element_type=jnp.float32)
        * score_scale
    )
    grad_key = (
        jnp.einsum("shqk,sqhe->skhe", grad_scores, queries, preferred_element_type=jnp.float32)
        * score_scale
    )
    return (grad_query, grad_key, grad_value)


def per_device(
    tokens,
    lengths,
    cotangent,
    w_query,
    w_key,
    w_value,
    b_query,
    b_value,
    w_out,
    b_out,
    ln1_gain,
    ln1_shift,
    w_up,
    b_up,
    w_down,
    b_down,
    ln2_gain,
    ln2_shift,
):
    sequences, local_rows, model_width = tokens.shape
    token_count = sequences * local_rows
    ctx_count = lax.axis_size("ctx")
    ctx_index = lax.axis_index("ctx")
    (
        query_full,
        key_full,
        value_full,
        out_full,
        up_full,
        down_full,
        bias_out,
        gain_one,
        shift_one,
        bias_down,
        gain_two,
        shift_two,
    ) = (
        lax.all_gather(w_query, "fsdp", axis=0, tiled=True),
        lax.all_gather(w_key, "fsdp", axis=0, tiled=True),
        lax.all_gather(w_value, "fsdp", axis=0, tiled=True),
        lax.all_gather(w_out, "fsdp", axis=1, tiled=True),
        lax.all_gather(w_up, "fsdp", axis=0, tiled=True),
        lax.all_gather(w_down, "fsdp", axis=1, tiled=True),
        lax.all_gather(b_out, "fsdp", axis=0, tiled=True),
        lax.all_gather(ln1_gain, "fsdp", axis=0, tiled=True),
        lax.all_gather(ln1_shift, "fsdp", axis=0, tiled=True),
        lax.all_gather(b_down, "fsdp", axis=0, tiled=True),
        lax.all_gather(ln2_gain, "fsdp", axis=0, tiled=True),
        lax.all_gather(ln2_shift, "fsdp", axis=0, tiled=True),
    )
    flat_tokens = tokens.reshape(token_count, model_width)
    local_width = query_full.shape[1]
    head_count = local_width // HEAD_DIM
    score_scale = HEAD_DIM ** (-0.5)
    query_low = (
        jnp.dot(flat_tokens, query_full, preferred_element_type=jnp.float32)
        + b_query.astype(jnp.float32)
    ).astype(jnp.bfloat16)
    key_low = jnp.dot(flat_tokens, key_full, preferred_element_type=jnp.float32).astype(
        jnp.bfloat16
    )
    value_low = (
        jnp.dot(flat_tokens, value_full, preferred_element_type=jnp.float32)
        + b_value.astype(jnp.float32)
    ).astype(jnp.bfloat16)
    query_heads = query_low.reshape(sequences, local_rows, head_count, HEAD_DIM)
    key_local = key_low.reshape(sequences, local_rows, local_width)
    value_local = value_low.reshape(sequences, local_rows, local_width)
    query_first = ctx_index * local_rows
    start_state = (
        jnp.full((sequences, head_count, local_rows), masked_score, jnp.float32),
        jnp.zeros((sequences, head_count, local_rows), jnp.float32),
        jnp.zeros((sequences, head_count, local_rows, HEAD_DIM), jnp.float32),
    )
    key_part = lax.all_gather(key_local, "ctx", axis=1, tiled=True)
    value_part = lax.all_gather(value_local, "ctx", axis=1, tiled=True)
    key_count = key_part.shape[1]
    block_size = math.gcd(key_count, 512)

    def one_block(position, state_in):
        offset = position * block_size
        key_block = lax.dynamic_slice_in_dim(key_part, offset, block_size, 1).reshape(
            sequences, block_size, head_count, HEAD_DIM
        )
        value_block = lax.dynamic_slice_in_dim(value_part, offset, block_size, 1).reshape(
            sequences, block_size, head_count, HEAD_DIM
        )
        usable = live_keys(lengths, offset, block_size)
        return absorb(state_in, query_heads, key_block, value_block, usable, score_scale)

    row_peak, row_total, summed = lax.fori_loop(0, key_count // block_size, one_block, start_state)
    attended = (summed / row_total[..., None]).transpose(0, 2, 1, 3)
    log_total = row_peak + jnp.log(row_total)
    attended_low = attended.reshape(token_count, local_width).astype(jnp.bfloat16)
    branch = lax.psum(
        jnp.dot(attended_low, out_full, preferred_element_type=jnp.float32).astype(jnp.bfloat16),
        "tp",
    ).astype(jnp.float32) + bias_out.astype(jnp.float32)
    normed_one, norm_one_back = jax.vjp(
        layer_norm,
        flat_tokens.astype(jnp.float32) + branch,
        gain_one.astype(jnp.float32),
        shift_one.astype(jnp.float32),
    )
    normed_low = normed_one.astype(jnp.bfloat16)
    hidden_in = jnp.dot(normed_low, up_full, preferred_element_type=jnp.float32) + b_up.astype(
        jnp.float32
    )
    active, gelu_back = jax.vjp(gelu_exact, hidden_in)
    active_low = active.astype(jnp.bfloat16)
    second = lax.psum(
        jnp.dot(active_low, down_full, preferred_element_type=jnp.float32).astype(jnp.bfloat16),
        "tp",
    ).astype(jnp.float32) + bias_down.astype(jnp.float32)
    output, norm_two_back = jax.vjp(
        layer_norm, normed_one + second, gain_two.astype(jnp.float32), shift_two.astype(jnp.float32)
    )
    positions = query_first + lax.iota(jnp.int32, local_rows)
    row_valid = (positions[None, :] < lengths[:, None]).astype(jnp.float32).reshape(token_count, 1)
    grad_output = cotangent.reshape(token_count, model_width).astype(jnp.float32) * row_valid
    grad_resid_two, grad_gain_two, grad_shift_two = norm_two_back(grad_output)
    grad_second = grad_resid_two.astype(jnp.bfloat16)
    grad_w_down = jnp.einsum(
        "nf,nd->fd", active_low, grad_second, preferred_element_type=jnp.float32
    )
    grad_b_down = jnp.sum(grad_second.astype(jnp.float32), axis=0)
    (grad_hidden,) = gelu_back(
        jnp.einsum("nd,fd->nf", grad_second, down_full, preferred_element_type=jnp.float32)
    )
    grad_hidden_low = grad_hidden.astype(jnp.bfloat16)
    grad_w_up = jnp.einsum(
        "nd,nf->df", normed_low, grad_hidden_low, preferred_element_type=jnp.float32
    )
    grad_b_up = jnp.sum(grad_hidden_low.astype(jnp.float32), axis=0)
    grad_normed = grad_resid_two + lax.psum(
        jnp.einsum(
            "nf,df->nd", grad_hidden_low, up_full, preferred_element_type=jnp.float32
        ).astype(jnp.bfloat16),
        "tp",
    ).astype(jnp.float32)
    grad_resid_one, grad_gain_one, grad_shift_one = norm_one_back(grad_normed)
    grad_branch = grad_resid_one.astype(jnp.bfloat16)
    grad_w_out = jnp.einsum(
        "nc,nd->cd", attended_low, grad_branch, preferred_element_type=jnp.float32
    )
    grad_b_out = jnp.sum(grad_branch.astype(jnp.float32), axis=0)
    grad_att = jnp.einsum(
        "nd,cd->nc", grad_branch, out_full, preferred_element_type=jnp.float32
    ).astype(jnp.bfloat16)
    grad_att_heads = grad_att.reshape(sequences, local_rows, head_count, HEAD_DIM)
    row_delta = jnp.sum(grad_att_heads.astype(jnp.float32) * attended, axis=-1).transpose(0, 2, 1)
    zero_block = jnp.zeros((sequences, local_rows, head_count, HEAD_DIM), jnp.float32)

    def turn_grads(first_key, key_block, value_block):
        usable = live_keys(lengths, first_key, local_rows)
        key_heads = key_block.reshape(sequences, local_rows, head_count, HEAD_DIM)
        value_heads = value_block.reshape(sequences, local_rows, head_count, HEAD_DIM)
        return block_grads(
            query_heads,
            grad_att_heads,
            log_total,
            row_delta,
            key_heads,
            value_heads,
            usable,
            score_scale,
        )

    def cycle_turn(turn_index, carried):
        key_block, value_block, grad_key, grad_value, grad_query = carried
        source = (ctx_index - turn_index) % ctx_count
        added_query, added_key, added_value = turn_grads(
            source * local_rows, key_block, value_block
        )
        key_block, value_block = passed_along((key_block, value_block), "ctx", 1)
        grad_key, grad_value = (
            passed_along((grad_key + added_key).astype(jnp.bfloat16), "ctx", 1).astype(jnp.float32),
            passed_along((grad_value + added_value).astype(jnp.bfloat16), "ctx", 1).astype(
                jnp.float32
            ),
        )
        return (key_block, value_block, grad_key, grad_value, grad_query + added_query)

    cycle_end = lax.fori_loop(
        0, ctx_count, cycle_turn, (key_local, value_local, zero_block, zero_block, zero_block)
    )
    grad_key, grad_value, grad_query = (cycle_end[2], cycle_end[3], cycle_end[4])
    grad_query_low = grad_query.reshape(token_count, local_width).astype(jnp.bfloat16)
    grad_key_low = grad_key.reshape(token_count, local_width).astype(jnp.bfloat16)
    grad_value_low = grad_value.reshape(token_count, local_width).astype(jnp.bfloat16)
    grad_w_query = jnp.einsum(
        "nd,nc->dc", flat_tokens, grad_query_low, preferred_element_type=jnp.float32
    )
    grad_w_key = jnp.einsum(
        "nd,nc->dc", flat_tokens, grad_key_low, preferred_element_type=jnp.float32
    )
    grad_w_value = jnp.einsum(
        "nd,nc->dc", flat_tokens, grad_value_low, preferred_element_type=jnp.float32
    )
    grad_b_query = jnp.sum(grad_query_low.astype(jnp.float32), axis=0)
    grad_b_value = jnp.sum(grad_value_low.astype(jnp.float32), axis=0)
    back_in = (
        jnp.einsum("nc,dc->nd", grad_query_low, query_full, preferred_element_type=jnp.float32)
        + jnp.einsum("nc,dc->nd", grad_key_low, key_full, preferred_element_type=jnp.float32)
        + jnp.einsum("nc,dc->nd", grad_value_low, value_full, preferred_element_type=jnp.float32)
    )
    grad_tokens = grad_resid_one + lax.psum(back_in.astype(jnp.bfloat16), "tp").astype(jnp.float32)
    (
        share_query,
        share_key,
        share_value,
        share_out,
        share_up,
        share_down,
        share_bias_out,
        share_gain_one,
        share_shift_one,
        share_bias_down,
        share_gain_two,
        share_shift_two,
    ) = (
        lax.psum_scatter(
            grad_w_query.astype(jnp.bfloat16), "fsdp", scatter_dimension=0, tiled=True
        ).astype(jnp.float32),
        lax.psum_scatter(
            grad_w_key.astype(jnp.bfloat16), "fsdp", scatter_dimension=0, tiled=True
        ).astype(jnp.float32),
        lax.psum_scatter(
            grad_w_value.astype(jnp.bfloat16), "fsdp", scatter_dimension=0, tiled=True
        ).astype(jnp.float32),
        lax.psum_scatter(
            grad_w_out.astype(jnp.bfloat16), "fsdp", scatter_dimension=1, tiled=True
        ).astype(jnp.float32),
        lax.psum_scatter(
            grad_w_up.astype(jnp.bfloat16), "fsdp", scatter_dimension=0, tiled=True
        ).astype(jnp.float32),
        lax.psum_scatter(
            grad_w_down.astype(jnp.bfloat16), "fsdp", scatter_dimension=1, tiled=True
        ).astype(jnp.float32),
        lax.psum_scatter(
            grad_b_out.astype(jnp.bfloat16), "fsdp", scatter_dimension=0, tiled=True
        ).astype(jnp.float32),
        lax.psum_scatter(
            grad_gain_one.astype(jnp.bfloat16), "fsdp", scatter_dimension=0, tiled=True
        ).astype(jnp.float32),
        lax.psum_scatter(
            grad_shift_one.astype(jnp.bfloat16), "fsdp", scatter_dimension=0, tiled=True
        ).astype(jnp.float32),
        lax.psum_scatter(
            grad_b_down.astype(jnp.bfloat16), "fsdp", scatter_dimension=0, tiled=True
        ).astype(jnp.float32),
        lax.psum_scatter(
            grad_gain_two.astype(jnp.bfloat16), "fsdp", scatter_dimension=0, tiled=True
        ).astype(jnp.float32),
        lax.psum_scatter(
            grad_shift_two.astype(jnp.bfloat16), "fsdp", scatter_dimension=0, tiled=True
        ).astype(jnp.float32),
    )
    (
        share_query,
        share_key,
        share_value,
        share_out,
        share_up,
        share_down,
        share_bias_out,
        share_gain_one,
        share_shift_one,
        share_bias_down,
        share_gain_two,
        share_shift_two,
    ) = (
        lax.psum(share_query.astype(jnp.bfloat16), "ctx").astype(jnp.float32),
        lax.psum(share_key.astype(jnp.bfloat16), "ctx").astype(jnp.float32),
        lax.psum(share_value.astype(jnp.bfloat16), "ctx").astype(jnp.float32),
        lax.psum(share_out.astype(jnp.bfloat16), "ctx").astype(jnp.float32),
        lax.psum(share_up.astype(jnp.bfloat16), "ctx").astype(jnp.float32),
        lax.psum(share_down.astype(jnp.bfloat16), "ctx").astype(jnp.float32),
        lax.psum(share_bias_out.astype(jnp.bfloat16), "ctx").astype(jnp.float32),
        lax.psum(share_gain_one.astype(jnp.bfloat16), "ctx").astype(jnp.float32),
        lax.psum(share_shift_one.astype(jnp.bfloat16), "ctx").astype(jnp.float32),
        lax.psum(share_bias_down.astype(jnp.bfloat16), "ctx").astype(jnp.float32),
        lax.psum(share_gain_two.astype(jnp.bfloat16), "ctx").astype(jnp.float32),
        lax.psum(share_shift_two.astype(jnp.bfloat16), "ctx").astype(jnp.float32),
    )
    total_b_query, total_b_value, total_b_up = lax.psum(
        (grad_b_query, grad_b_value, grad_b_up), ("fsdp", "ctx")
    )
    return (
        output.astype(jnp.bfloat16).reshape(sequences, local_rows, model_width),
        grad_tokens.reshape(sequences, local_rows, model_width),
        share_query,
        share_key,
        share_value,
        total_b_query,
        total_b_value,
        share_out,
        share_bias_out,
        share_gain_one,
        share_shift_one,
        share_up,
        total_b_up,
        share_down,
        share_bias_down,
        share_gain_two,
        share_shift_two,
    )


def swapped(value, axis, bit):
    count = lax.axis_size(axis)
    return lax.ppermute(value, axis, [(place, place ^ bit) for place in range(count)])


def shifted(value, axis, steps):
    count = lax.axis_size(axis)
    return lax.ppermute(value, axis, [(place, (place + steps) % count) for place in range(count)])


def to_owner(value, step, back=False):
    pairs = []
    for x in range(2):
        for z in range(4):
            block = z ^ step
            source = x * 4 + z
            target = (block >> 1) * 4 + (block ^ (2 * x))
            pairs.append((target, source) if back else (source, target))
    return lax.ppermute(value, ("ctx", "tp"), pairs)


ANY = pl.BlockSpec(memory_space=pl.ANY)
WHOLE = pl.BlockSpec(memory_space=pltpu.VMEM)
log2_e = math.log2(math.e)
EXTRA = 8


def low(value):
    return value.astype(jnp.bfloat16)


def wide(value):
    return value.astype(jnp.float32)


def dot32(left, right, left_dim, right_dim):
    return lax.dot_general(
        left, right, (((left_dim,), (right_dim,)), ((), ())), preferred_element_type=jnp.float32
    )


def struct(shape, dtype=jnp.bfloat16):
    return jax.ShapeDtypeStruct(shape, dtype)


def cost(flops, moved, special=0):
    return pl.CostEstimate(flops=int(flops), bytes_accessed=int(moved), transcendentals=int(special))


def stack_kernel(*refs):
    for place, ref in enumerate(refs[:-1]):
        refs[-1][place] = ref[...]


def stacked(pieces):
    shape = (len(pieces),) + pieces[0].shape
    return pl.pallas_call(
        stack_kernel,
        out_shape=struct(shape),
        in_specs=[WHOLE] * len(pieces),
        out_specs=WHOLE,
        cost_estimate=cost(0, 4 * math.prod(shape)),
        name="stack_pieces",
    )(*pieces)


def piece_copies(meta, pieces, taken, columns, target, sems, first):
    x, z, f = meta[0], meta[1], meta[2]
    copies = []
    parts = [(piece, step) for piece in pieces for step in range(piece.shape[0])]
    for index, (piece, step) in enumerate(parts):
        place, slot = index // 4, index % 4
        across = (place % 2, 2 * ((place // 2) % 2) + place // 4)
        start = pl.multiple_of(((f ^ across[1]) * 2 + (x ^ across[0])) * taken, taken)
        copies.append(
            pltpu.make_async_copy(
                piece.at[step, pl.ds(0, taken), columns],
                target.at[z ^ slot, pl.ds(start, taken), :],
                sems.at[first + len(copies)],
            )
        )
    return copies


def attend_kernel(
    meta, own, other, w0, w1, w2, w3, bias, qkv, o0, o1, o2, o3, stats, weight, vectors,
    mask, shards, *, block, heads
):
    step = pl.program_id(0)
    shard = w0.shape[0] - EXTRA
    half = own.shape[1]
    scale = log2_e * HEAD_DIM ** (-0.5)

    @pl.when(step == 0)
    def _():
        for place, piece in enumerate((w0, w1, w2, w3)):
            start = pl.multiple_of((meta[2] ^ place) * shard, shard)
            weight[pl.ds(start, shard), :] = piece[:shard, :]
            shards[meta[2] ^ place] = piece[shard:, :]
        vectors[6:8, :] = jnp.zeros((2, 4 * shard), jnp.float32)
        for place in range(4):
            for row in range(6):
                first = row % 3 * shard
                vectors[row : row + 1, place * shard : (place + 1) * shard] = wide(
                    shards[place, row // 3 : row // 3 + 1, first : first + shard]
                )
        for place, rows in enumerate((own, other)):
            source = rows[0] if place == 0 else rows[...]
            qkv[place * half : (place + 1) * half, :] = low(
                dot32(source, weight[...], 1, 0) + bias[...]
            )
            first = (meta[0] ^ place) * half
            position = first + lax.broadcasted_iota(jnp.int32, (half, block), 0)
            mask[place * half : (place + 1) * half, :] = jnp.where(
                position < meta[3], 0.0, masked_score
            )

    rows = pl.ds(pl.multiple_of((meta[7] ^ step) * block, block), block)
    outs, logs = [], []
    for head in range(heads):
        base = 3 * head * HEAD_DIM
        query = qkv[rows, base : base + HEAD_DIM]
        key = qkv[:, base + HEAD_DIM : base + 2 * HEAD_DIM]
        value = qkv[:, base + 2 * HEAD_DIM : base + 3 * HEAD_DIM]
        scores = dot32(key, query, 1, 1) * scale + mask[...]
        peak = jnp.max(scores, axis=0, keepdims=True)
        weights = jnp.exp2(scores - peak)
        total = jnp.sum(weights, axis=0, keepdims=True)
        outs.append((dot32(value, low(weights), 0, 0) / total).T)
        logs.append(peak + jnp.log2(total))
    result = low(jnp.concatenate(outs, axis=1))
    for place, out in enumerate((o0, o1, o2, o3)):

        @pl.when(step == place)
        def _(out=out):
            out[...] = result

    stats[0] = jnp.concatenate(logs + [jnp.zeros((8 - heads, block), jnp.float32)], axis=0)


def attend_call(meta, tokens, other, pieces, bias, heads):
    half, width = other.shape
    block = half // 2
    columns = pieces[0].shape[1]
    whole = lambda shape: pl.BlockSpec(shape, lambda step, meta: (0,) * len(shape))
    rows = 2 * half
    return pl.pallas_call(
        lambda *refs: attend_kernel(*refs, block=block, heads=heads),
        grid_spec=pltpu.PrefetchScalarGridSpec(
            num_scalar_prefetch=1,
            grid=(4,),
            in_specs=[
                pl.BlockSpec((1, half, width), lambda step, meta: (meta[0], 0, 0)),
                whole((half, width)),
                *[whole(piece.shape) for piece in pieces],
                whole((1, columns)),
            ],
            out_specs=[
                whole((rows, columns)),
                *[whole((block, columns // 3))] * 4,
                pl.BlockSpec((1, 8, block), lambda step, meta: (step, 0, 0)),
                whole((width, columns)),
                whole((EXTRA, width)),
            ],
            scratch_shapes=[
                pltpu.VMEM((rows, block), jnp.float32),
                pltpu.VMEM((4, EXTRA, columns), jnp.bfloat16),
            ],
        ),
        out_shape=[struct((rows, columns))]
        + [struct((block, columns // 3))] * 4
        + [struct((4, 8, block), jnp.float32), struct((width, columns))]
        + [struct((EXTRA, width), jnp.float32)],
        cost_estimate=cost(2 * rows * width * columns + 16 * rows * rows * columns, 8e6, rows * rows * 3),
        name="attend",
    )(meta, tokens, other, *pieces, bias)


def attend_back_kernel(
    meta, qkv, d0, d1, d2, d3, o0, o1, o2, o3, stats, weight, full, p0, p1, p2, p3,
    grads, mask, grad_att, attended, *, block, heads
):
    step = pl.program_id(0)
    rows_all = qkv.shape[0]
    half = rows_all // 2
    scale = log2_e * HEAD_DIM ** (-0.5)

    @pl.when(step == 0)
    def _():
        grads[...] = jnp.zeros_like(grads)
        for place in range(2):
            first = (meta[0] ^ place) * half
            position = first + lax.broadcasted_iota(jnp.int32, (half, block), 0)
            mask[place * half : (place + 1) * half, :] = jnp.where(
                position < meta[3], 0.0, masked_score
            )

    for place, (grad, out) in enumerate(zip((d0, d1, d2, d3), (o0, o1, o2, o3))):

        @pl.when(step == place)
        def _(grad=grad, out=out):
            grad_att[...] = grad[...]
            attended[...] = out[...]

    rows = pl.ds(pl.multiple_of((meta[7] ^ step) * block, block), block)
    for head in range(heads):
        base = 3 * head * HEAD_DIM
        span = slice(head * HEAD_DIM, (head + 1) * HEAD_DIM)
        query = qkv[rows, base : base + HEAD_DIM]
        key = qkv[:, base + HEAD_DIM : base + 2 * HEAD_DIM]
        value = qkv[:, base + 2 * HEAD_DIM : base + 3 * HEAD_DIM]
        grad_out = grad_att[:, span]
        products = wide(grad_out) * wide(attended[:, span])
        delta = lax.dot_general(
            jnp.ones((8, HEAD_DIM), jnp.float32),
            products,
            (((1,), (1,)), ((), ())),
            precision=lax.Precision.HIGHEST,
            preferred_element_type=jnp.float32,
        )[:1]
        scores = dot32(key, query, 1, 1) * scale + mask[...]
        weights = jnp.exp2(scores - stats[0, head : head + 1, :])
        grad_weights = dot32(value, grad_out, 1, 1)
        grad_scores = low(weights * (grad_weights - delta))
        grads[2 * head] += dot32(grad_scores, query, 1, 0)
        grads[2 * head + 1] += dot32(low(weights), grad_out, 1, 0)
        full[rows, base : base + HEAD_DIM] = low(
            dot32(grad_scores, key, 0, 0) * HEAD_DIM ** (-0.5)
        )

    @pl.when(step == 3)
    def _():
        for head in range(heads):
            base = 3 * head * HEAD_DIM
            full[:, base + HEAD_DIM : base + 2 * HEAD_DIM] = low(
                grads[2 * head] * HEAD_DIM ** (-0.5)
            )
            full[:, base + 2 * HEAD_DIM : base + 3 * HEAD_DIM] = low(grads[2 * head + 1])
        for place, part in enumerate((p0, p1, p2, p3)):
            span = pl.ds(pl.multiple_of((meta[7] ^ place) * block, block), block)
            part[...] = low(dot32(full[span, :], weight[...], 1, 1))


def attend_back_call(meta, qkv, grad_parts, parts, stats, weight, heads):
    rows, columns = qkv.shape
    width = weight.shape[0]
    block = rows // 4
    whole = lambda shape: pl.BlockSpec(shape, lambda step, meta: (0,) * len(shape))
    small = whole((block, columns // 3))
    return pl.pallas_call(
        lambda *refs: attend_back_kernel(*refs, block=block, heads=heads),
        grid_spec=pltpu.PrefetchScalarGridSpec(
            num_scalar_prefetch=1,
            grid=(4,),
            in_specs=[whole((rows, columns))]
            + [small] * 8
            + [pl.BlockSpec((1, 8, block), lambda step, meta: (step, 0, 0)), whole(weight.shape)],
            out_specs=[whole((rows, columns))] + [whole((block, width))] * 4,
            scratch_shapes=[
                pltpu.VMEM((2 * heads, rows, HEAD_DIM), jnp.float32),
                pltpu.VMEM((rows, block), jnp.float32),
                pltpu.VMEM((block, columns // 3), jnp.bfloat16),
                pltpu.VMEM((block, columns // 3), jnp.bfloat16),
            ],
        ),
        out_shape=[struct((rows, columns))] + [struct((block, width))] * 4,
        cost_estimate=cost(40 * rows * rows * columns, 8e6, rows * rows * 3),
        name="attend_back",
    )(meta, qkv, *grad_parts, *parts, stats, weight)


def norm_parts(inputs):
    center = jnp.mean(inputs, axis=-1, keepdims=True)
    centered = inputs - center
    spread = jnp.mean(centered * centered, axis=-1, keepdims=True)
    inverse = lax.rsqrt(spread + epsilon)
    return centered * inverse, inverse


def norm_back(grad_out, hat, inverse, gain):
    scaled = grad_out * gain
    return inverse * (
        scaled
        - jnp.mean(scaled, axis=-1, keepdims=True)
        - hat * jnp.mean(scaled * hat, axis=-1, keepdims=True)
    )


BIAS_OUT, GAIN_ONE, SHIFT_ONE, BIAS_DOWN, GAIN_TWO, SHIFT_TWO = range(6)


def first_kernel(meta, *refs, width):
    att, tok, vectors, lines, pieces = refs[:4], refs[4], refs[5], refs[6], refs[7:15]
    hat, inverse, both, slope, out_w, up_w, sems = refs[15:]
    hidden = up_w.shape[2]
    taken = pieces[0].shape[1]
    copies = piece_copies(meta, pieces, taken, pl.ds(hidden, out_w.shape[2]), out_w, sems, 0)
    copies += piece_copies(meta, pieces, taken, pl.ds(0, hidden), up_w, sems, 32)
    for copy in copies:
        copy.start()
    for step in range(4):
        both[step, :, hidden : hidden + width] = att[step][...]
        both[step, :, hidden + width :] = jnp.zeros_like(both[step, :, hidden + width :])
    for copy in copies:
        copy.wait()
    branch = vectors[BIAS_OUT : BIAS_OUT + 1, :]
    for step in range(4):
        branch = branch + dot32(att[step][...], out_w[meta[4] ^ step][:, :width], 1, 1)
    hat_one, inverse_one = norm_parts(wide(tok[0]) + branch)
    hat[...] = hat_one
    inverse[...] = inverse_one
    normed = low(hat_one * vectors[GAIN_ONE : GAIN_ONE + 1, :] + vectors[SHIFT_ONE : SHIFT_ONE + 1, :])
    for place in range(4):
        inputs = dot32(normed, up_w[place], 1, 0) + wide(lines[meta[1] ^ place, 0:1, :])
        cumulative = 0.5 * (1.0 + lax.erf(inputs * (0.5**0.5)))
        density = jnp.exp(-0.5 * inputs * inputs) * ((0.5 / math.pi) ** 0.5)
        both[place, :, :hidden] = low(inputs * cumulative)
        slope[place] = low(cumulative + inputs * density)


def second_kernel(meta, *refs, width):
    hat, inverse, both, slope, cot, vectors = refs[:6]
    pieces_a, pieces_b = refs[6:14], refs[14:24]
    output, resid, g0, g1, g2, g3, mixed, keep = refs[24:32]
    out_w, up_w, down_w, blocks, small, small_blocks, sems = refs[32:]
    rows, model = hat.shape
    hidden = up_w.shape[2]
    taken = pieces_a[0].shape[1]
    down_copies = piece_copies(meta, pieces_b, taken, pl.ds(0, hidden), down_w, sems, 0)
    copies = piece_copies(meta, pieces_a, taken, pl.ds(0, hidden), up_w, sems, 32)
    copies += piece_copies(meta, pieces_a, taken, pl.ds(hidden, out_w.shape[2]), out_w, sems, 64)
    for copy in down_copies + copies:
        copy.start()
    row = lambda place: vectors[place : place + 1, :]
    hat_one, inverse_one = hat[...], inverse[...]
    normed_one = hat_one * row(GAIN_ONE) + row(SHIFT_ONE)
    for copy in down_copies:
        copy.wait()
    second = row(BIAS_DOWN)
    for place in range(4):
        second = second + dot32(both[place, :, :hidden], down_w[place], 1, 1)
    hat_two, inverse_two = norm_parts(normed_one + second)
    output[...] = low(hat_two * row(GAIN_TWO) + row(SHIFT_TWO))
    position = meta[4] * rows + lax.broadcasted_iota(jnp.int32, (rows, model), 0)
    grad_output = jnp.where(position < meta[8], wide(cot[0]), 0.0)
    grad_two = norm_back(grad_output, hat_two, inverse_two, row(GAIN_TWO))
    grad_second = low(grad_two)
    for copy in copies:
        copy.wait()
    grad_normed = grad_two
    sums = lambda array: jnp.sum(array, axis=0, keepdims=True)
    for place in range(4):
        grad_hidden = low(dot32(grad_second, down_w[place], 1, 0) * wide(slope[place]))
        mixed[place, :rows, :] = grad_hidden
        mixed[place, rows:, :] = low(
            jnp.broadcast_to(sums(wide(grad_hidden)), (EXTRA, hidden))
        )
        grad_normed = grad_normed + dot32(grad_hidden, up_w[place], 1, 1)
    grad_one = norm_back(grad_normed, hat_one, inverse_one, row(GAIN_ONE))
    resid[...] = grad_one
    grad_branch = low(grad_one)
    for step, out in enumerate((g0, g1, g2, g3)):
        out[...] = low(dot32(grad_branch, out_w[meta[4] ^ step][:, :width], 1, 0))
    small[0:1, :] = sums(wide(grad_branch))
    small[1:2, :] = sums(grad_normed * hat_one)
    small[2:3, :] = sums(grad_normed)
    small[3:4, :] = sums(wide(grad_second))
    small[4:5, :] = sums(grad_output * hat_two)
    small[5:6, :] = sums(grad_output)
    small[6:8, :] = jnp.zeros((2, model), jnp.float32)
    shard = model // 4
    for place in range(4):
        small_blocks[place] = low(small[:, place * shard : (place + 1) * shard])
    for kind, array in enumerate((grad_second, low(normed_one), grad_branch)):
        for place in range(4):
            blocks[place] = array[:, place * shard : (place + 1) * shard]
        for far in range(2):
            keep[kind, far, :rows, :] = blocks[meta[2] ^ (2 * far)]
            keep[kind, far, rows:, :] = small_blocks[meta[2] ^ (2 * far)]
            columns = slice(kind * shard, (kind + 1) * shard)
            mixed[4 + far, :rows, columns] = blocks[meta[2] ^ (2 * far + 1)]
            mixed[4 + far, rows:, columns] = small_blocks[meta[2] ^ (2 * far + 1)]
    for far in range(2):
        mixed[4 + far, :, 3 * shard :] = jnp.zeros((rows + EXTRA, hidden - 3 * shard), jnp.bfloat16)


def weights_kernel(meta, *refs, width):
    keep, both, both_sib, mixed, mixed_sib = refs[:5]
    near_up, far_up, mine_down, theirs_down, turned, whole = refs[5:]
    shard = keep.shape[3]
    rows = both.shape[1]
    half = shard // 2
    hidden = mixed.shape[2]
    padded = both.shape[2] - hidden
    starts = [pl.multiple_of(side * half, half) for side in (meta[0], 1 - meta[0])]

    def slot(block):
        apart = block ^ meta[1]
        return 2 * (apart & 1) + (apart >> 1)

    for kind in range(3):
        for far in range(2):
            span = slice(far * shard, (far + 1) * shard)
            turned[span, :rows] = keep[kind, far, :rows, :].T
            turned[span, rows:] = mixed_sib[4 + far, :rows, kind * shard : (kind + 1) * shard].T
        for place in range(4):
            if kind == 1:
                left, right = mixed[place, :rows, :], mixed_sib[place, :rows, :]
            else:
                columns = slice(0, hidden) if kind == 0 else slice(hidden, None)
                left, right = both[place, :, columns], both_sib[place, :, columns]
            value = dot32(turned[:, :rows], left, 1, 0) + dot32(turned[:, rows:], right, 1, 0)
            target = slot(meta[4] ^ place if kind == 2 else place)
            count = value.shape[1]
            whole[:, :count] = value
            for far in range(2):
                for side, start in enumerate(starts):
                    part = low(whole[pl.ds(far * shard + start, half), :count])
                    if kind == 0:
                        kept = mine_down.shape[3]
                        (mine_down, theirs_down)[side][far, target, :half, :] = part[:, :kept]
                        (near_up, far_up)[far][side, target, :half, hidden + padded :] = part[:, kept:]
                    elif kind == 1:
                        (near_up, far_up)[far][side, target, :half, :hidden] = part
                    else:
                        (near_up, far_up)[far][side, target, :half, hidden : hidden + padded] = part
    for far in range(2):
        vector_sums = low(wide(keep[0, far, rows:, :]) + wide(mixed_sib[4 + far, rows:, :shard]))
        for place in range(4):
            hidden_sums = low(wide(mixed[place, rows:, :]) + wide(mixed_sib[place, rows:, :]))
            for side in range(2):
                out = (mine_down, theirs_down)[side]
                out[far, place, half:, :] = jnp.zeros((EXTRA, out.shape[3]), jnp.bfloat16)
                out = (near_up, far_up)[far]
                out[side, slot(place), half:, :hidden] = hidden_sums
                out[side, place, half:, hidden : hidden + shard] = vector_sums
                rest = slice(hidden + shard, None)
                out[side, place, half:, rest] = jnp.zeros_like(out[side, place, half:, rest])


def projections_kernel(meta, own, other, grads, kept, sent, whole):
    half, shard = other.shape[0], other.shape[1] // 4
    count = grads.shape[1]
    whole[...] = dot32(own[0], grads[:half, :], 0, 0) + dot32(other[...], grads[half:, :], 0, 0)
    sums = jnp.broadcast_to(jnp.sum(wide(grads[...]), axis=0, keepdims=True), (EXTRA, count))
    for far in range(2):
        for out, place in ((kept, meta[2] ^ (2 * far)), (sent, meta[2] ^ (2 * far + 1))):
            value = whole[pl.ds(pl.multiple_of(place * shard, shard), shard), :]
            out[far, :shard, :count] = value.astype(out.dtype)
            out[far, shard:, :count] = sums.astype(out.dtype)
            out[far, :, count:] = jnp.zeros_like(out[far, :, count:])


def per_device_rows(
    tokens,
    lengths,
    cotangent,
    w_query,
    w_key,
    w_value,
    b_query,
    b_value,
    w_out,
    b_out,
    ln1_gain,
    ln1_shift,
    w_up,
    b_up,
    w_down,
    b_down,
    ln2_gain,
    ln2_shift,
):
    sequences, local_rows, model = tokens.shape
    x, f, z = lax.axis_index("ctx"), lax.axis_index("fsdp"), lax.axis_index("tp")
    rows = local_rows // 2
    width = w_query.shape[1]
    heads = width // HEAD_DIM
    hidden = w_up.shape[1]
    shard = w_query.shape[0]
    half = shard // 2
    padded = -(-width // 128) * 128
    own_seq, own_place = (z // 2) ^ x, z % 2
    quarter = 2 * x + own_place
    length_of = lambda place: lax.dynamic_index_in_dim(lengths, place, 0, keepdims=False)
    entries = (x, z, f, length_of(x), quarter, own_seq, own_place, z ^ (2 * x), length_of(own_seq))
    places = lax.iota(jnp.int32, len(entries))
    meta = sum(jnp.where(places == place, entry, 0) for place, entry in enumerate(entries))
    meta = meta.astype(jnp.int32)
    tied = lambda *values: lax.optimization_barrier(values)

    take_half = lambda pack: lax.dynamic_slice_in_dim(pack, x * half, half, 0)
    wider = lambda array, columns: jnp.pad(array, ((0, 0), (0, columns - array.shape[1])))
    columns_a = hidden + padded
    half_a = wider(take_half(jnp.concatenate([w_up, w_out.T], axis=1)), columns_a)
    half_b = jnp.concatenate(
        [take_half(w_down.T), b_up[None], jnp.zeros((EXTRA - 1, hidden), jnp.bfloat16)]
    )

    other = lax.dynamic_index_in_dim(tokens, 1 - x, 0, keepdims=False)
    other, half_a = tied(other, half_a)
    other = swapped(other, "ctx", 1)
    far_a, near_half = swapped(half_a, "tp", 2), swapped(half_a, "tp", 1)
    per_head = lambda weights: jnp.concatenate(
        [
            weight[..., head * HEAD_DIM : (head + 1) * HEAD_DIM]
            for head in range(heads)
            for weight in weights
        ],
        axis=-1,
    )
    vectors = jnp.concatenate([b_out, ln1_gain, ln1_shift, b_down, ln2_gain, ln2_shift])
    qkv_shard = jnp.concatenate(
        [
            per_head((w_query, w_key, w_value)),
            jnp.pad(vectors.reshape(2, 3 * width), ((0, EXTRA - 2), (0, 0))),
        ]
    )
    qkv_bias = wide(per_head((b_query, jnp.zeros_like(b_query), b_value)))[None, :]
    qkv_y, far_a, meta = tied(swapped(qkv_shard, "fsdp", 2), far_a, meta)
    line_a = stacked([half_a, near_half, far_a, swapped(far_a, "tp", 1)])
    qkv_pieces = (qkv_shard, swapped(qkv_shard, "fsdp", 1), qkv_y, swapped(qkv_y, "fsdp", 1))

    core = lambda array: swapped(array, "fsdp", 1)
    meta, qkv_bias, other, line_a, half_b, *qkv_pieces = tied(
        meta, qkv_bias, other, line_a, half_b, *qkv_pieces
    )
    x_a, y_a = swapped(line_a, "ctx", 1), swapped(line_a, "fsdp", 2)
    qkv, *parts, stats, weight, vectors = attend_call(
        meta, tokens, other, qkv_pieces, qkv_bias, heads
    )
    b_pieces = [swapped(half_b, "tp", bit) for bit in (1, 2, 3)]

    x_a, y_a, line_a, *rest = tied(x_a, y_a, line_a, *b_pieces, *parts)
    b_pieces, parts = rest[:3], rest[3:]
    line_b = stacked([half_b, *b_pieces])
    att = [to_owner(part, step) for step, part in enumerate(parts)]
    x_y_a = swapped(x_a, "fsdp", 2)
    x_y_a, x_a, y_a, line_a, line_b, *att = tied(x_y_a, x_a, y_a, line_a, line_b, *att)
    near_a = (line_a, x_a, y_a, x_y_a)
    pieces_a = (*near_a, *map(core, near_a))
    x_b, y_b, line_core = swapped(line_b, "ctx", 1), swapped(line_b, "fsdp", 2), core(line_b)

    def row_spec(array):
        return pl.BlockSpec((1, rows, model), lambda step, meta: (meta[5], meta[6], 0))

    vm = lambda shape, dtype=jnp.bfloat16: pltpu.VMEM(shape, dtype)
    weights_scratch = [vm((4, model, padded)), vm((4, model, hidden))]
    grid = lambda inputs, outputs, scratch: pltpu.PrefetchScalarGridSpec(
        num_scalar_prefetch=1, grid=(1,), in_specs=inputs, out_specs=outputs, scratch_shapes=scratch
    )
    full = lambda shape: pl.BlockSpec(shape, lambda step, meta: (0,) * len(shape))
    specs = lambda shapes: [full(item.shape) for item in shapes]

    first_out = [
        struct((rows, model), jnp.float32),
        struct((rows, 1), jnp.float32),
        struct((4, rows, columns_a)),
        struct((4, rows, hidden)),
    ]
    hat, inverse, both, slope = pl.pallas_call(
        lambda *refs: first_kernel(*refs, width=width),
        grid_spec=grid(
            [full((rows, width))] * 4
            + [row_spec(tokens), full((EXTRA, model))]
            + [pl.BlockSpec((4, EXTRA, hidden), lambda step, meta: (0, half // EXTRA, 0))]
            + [ANY] * 8,
            specs(first_out),
            weights_scratch + [pltpu.SemaphoreType.DMA((64,))],
        ),
        out_shape=first_out,
        cost_estimate=cost(2 * rows * model * (model + 4 * hidden), 12e6, rows * hidden * 8),
        name="feed_first",
    )(meta, *att, tokens, vectors, line_b, *pieces_a)

    both, x_b, y_b, line_b, line_core = tied(both, x_b, y_b, line_b, line_core)
    x_y_b = [swapped(x_b[:2], "fsdp", 2), swapped(y_b[2:], "ctx", 1)]
    *x_y_b, x_core, y_core, both_sib = tied(*x_y_b, core(x_b), core(y_b), core(both))
    pieces_b = (line_b, x_b, y_b, *x_y_b, line_core, x_core, y_core, *map(core, x_y_b))

    second_out = [
        struct((rows, model)),
        struct((rows, model), jnp.float32),
        *[struct((rows, width))] * 4,
        struct((6, rows + EXTRA, hidden)),
        struct((3, 2, rows + EXTRA, shard)),
    ]
    output, resid, g0, g1, g2, g3, mixed, keep = pl.pallas_call(
        lambda *refs: second_kernel(*refs, width=width),
        grid_spec=grid(
            [full(item.shape) for item in (hat, inverse, both, slope)]
            + [row_spec(cotangent), full((EXTRA, model))]
            + [ANY] * 18,
            specs(second_out),
            weights_scratch
            + [
                vm((4, model, hidden)),
                vm((4, rows, shard)),
                vm((EXTRA, model), jnp.float32),
                vm((4, EXTRA, shard)),
                pltpu.SemaphoreType.DMA((96,)),
            ],
        ),
        out_shape=second_out,
        cost_estimate=cost(2 * rows * model * (model + 12 * hidden), 20e6),
        name="feed_second",
    )(meta, hat, inverse, both, slope, cotangent, vectors, *pieces_a, *pieces_b)

    grad_att = [to_owner(part, step, True) for step, part in enumerate((g0, g1, g2, g3))]

    first_x = 2 * padded
    pack = struct((2, 4, half + EXTRA, first_x))
    pack_up = struct((2, 4, half + EXTRA, columns_a + hidden - first_x))
    mixed_sib = core(mixed)
    near_up, far_up, mine_down, theirs_down = pl.pallas_call(
        lambda *refs: weights_kernel(*refs, width=width),
        grid_spec=grid(
            specs([keep, both, both_sib, mixed, mixed_sib]),
            specs([pack_up] * 2 + [pack] * 2),
            [vm((2 * shard, 2 * rows)), vm((2 * shard, hidden), jnp.float32)],
        ),
        out_shape=[pack_up] * 2 + [pack] * 2,
        cost_estimate=cost(8 * rows * shard * (8 * hidden + 4 * width), 20e6),
        name="feed_weights",
    )(meta, keep, both, both_sib, mixed, mixed_sib)

    near_out = swapped(output, "tp", 1)
    far_up, theirs_down, output, *grad_att = tied(far_up, theirs_down, output, *grad_att)
    got_up, got_down = swapped(far_up, "fsdp", 2), swapped(theirs_down, "ctx", 1)
    far_out = swapped(output, "tp", 2)
    grad_full, *grad_parts = attend_back_call(meta, qkv, grad_att, parts, stats, weight, heads)

    near_out, far_out, *grad_parts = tied(near_out, far_out, *grad_parts)
    grad_rows = [to_owner(part, step) for step, part in enumerate(grad_parts)]
    grad_full, grad_rows[0] = tied(grad_full, grad_rows[0])
    kept, sent = pl.pallas_call(
        projections_kernel,
        grid_spec=grid(
            [pl.BlockSpec((1, local_rows, model), lambda step, meta: (meta[0], 0, 0))]
            + [full((local_rows, model)), full(grad_full.shape)],
            [full((2, shard + EXTRA, 640 * width // 192))] * 2,
            [vm((model, 3 * width), jnp.float32)],
        ),
        out_shape=[
            struct((2, shard + EXTRA, 640 * width // 192), dtype) for dtype in (jnp.float32, jnp.bfloat16)
        ],
        cost_estimate=cost(12 * local_rows * model * width, 8e6),
        name="projection_weights",
    )(meta, tokens, other, grad_full)
    up_sent, down_sent, kept, sent, *grad_rows = tied(
        low(wide(near_up[1]) + wide(got_up[1])),
        low(wide(mine_down[1]) + wide(got_down[1])),
        kept,
        sent,
        *grad_rows,
    )
    second_up, second_down = swapped(up_sent, "ctx", 1), swapped(down_sent, "fsdp", 2)
    token_rows = resid
    for part in grad_rows:
        token_rows = token_rows + wide(part)

    def spread_rows(pieces, dtype):
        blocks = [
            lax.select_n(z ^ (2 * x), *[pieces[block ^ place] for place in range(4)]).astype(dtype)
            for block in range(4)
        ]
        return jnp.stack([jnp.concatenate(blocks[2 * seq : 2 * seq + 2]) for seq in range(2)])

    token_rows = low(token_rows)
    far_z, near_z, sent, second_up, second_down = tied(
        swapped(token_rows, "tp", 2), token_rows, sent, second_up, second_down
    )
    up_lines = wide(near_up[0]) + wide(got_up[0]) + wide(second_up)
    down_lines = wide(mine_down[0]) + wide(got_down[0]) + wide(second_down)
    lines = jnp.concatenate([up_lines, down_lines], axis=2)
    lines, line_sent = lines[:2], low(lines[2:])
    lines = lines + wide(swapped(line_sent, "tp", 1))
    near_z = swapped(near_z, "tp", 1)
    last_z, _ = tied(far_z, line_sent)
    last_z = swapped(last_z, "tp", 1)
    grad_tokens = spread_rows([token_rows, near_z, far_z, last_z], jnp.float32)
    line_last, far_out = tied(swapped(low(lines[1]), "tp", 2), far_out)
    output_full = spread_rows(
        [output, near_out, far_out, swapped(far_out, "tp", 1)], jnp.bfloat16
    )
    total = low(lines[0] + wide(line_last))
    other_half = swapped(total, "ctx", 1)
    small = wide(total[half:])
    total = wide(
        jnp.concatenate(
            [
                jnp.where(x == 0, total[:half], other_half[:half]),
                jnp.where(x == 0, other_half[:half], total[:half]),
            ]
        )
    )
    grad_w_up = total[:, :hidden]
    tail = slice(columns_a, columns_a + hidden - first_x)
    grad_w_down = jnp.concatenate([total[:, tail.stop :], total[:, tail]], axis=1).T
    grad_w_out = total[:, hidden : hidden + width].T
    grad_b_up = small[0, :hidden]
    small_own = small[:, hidden : hidden + shard]

    kept = kept + wide(core(sent))
    kept = low(kept[0] + wide(swapped(low(kept[1]), "fsdp", 2)))
    kept = wide(kept) + wide(swapped(kept, "ctx", 1))

    def unpack(array, part):
        return jnp.concatenate(
            [
                array[:, (3 * head + part) * HEAD_DIM : (3 * head + part + 1) * HEAD_DIM]
                for head in range(heads)
            ],
            axis=1,
        )

    grad_w_query, grad_w_key, grad_w_value = (unpack(kept[:shard], part) for part in range(3))
    grad_b_query, grad_b_value = (unpack(kept[shard : shard + 1], part)[0] for part in (0, 2))
    return (
        output_full,
        grad_tokens,
        grad_w_query,
        grad_w_key,
        grad_w_value,
        grad_b_query,
        grad_b_value,
        grad_w_out,
        small_own[0],
        small_own[1],
        small_own[2],
        grad_w_up,
        grad_b_up,
        grad_w_down,
        small_own[3],
        small_own[4],
        small_own[5],
    )


def rows_path_fits(mesh, tokens, w_query, w_up):
    shape = dict(mesh.shape)
    return (
        shape["ctx"] == 2
        and shape["fsdp"] == 4
        and shape["tp"] == 4
        and tokens.shape[0] == 8
        and tokens.shape[1] % 1024 == 0
        and w_query.shape[0] == w_query.shape[1]
        and w_query.shape[0] % 768 == 0
        and w_up.shape[1] == 4 * w_up.shape[0]
    )


def solution(mesh):
    placed = (
        P("fsdp", "ctx", None),
        P("fsdp"),
        P("fsdp", "ctx", None),
        P("fsdp", "tp"),
        P("fsdp", "tp"),
        P("fsdp", "tp"),
        P("tp"),
        P("tp"),
        P("tp", "fsdp"),
        P("fsdp"),
        P("fsdp"),
        P("fsdp"),
        P("fsdp", "tp"),
        P("tp"),
        P("tp", "fsdp"),
        P("fsdp"),
        P("fsdp"),
        P("fsdp"),
    )
    def split(function):
        return jax.shard_map(
        function,
        mesh=mesh,
        in_specs=placed,
        out_specs=(
            P("fsdp", "ctx", None),
            P("fsdp", "ctx", None),
            P("fsdp", "tp"),
            P("fsdp", "tp"),
            P("fsdp", "tp"),
            P("tp"),
            P("tp"),
            P("tp", "fsdp"),
            P("fsdp"),
            P("fsdp"),
            P("fsdp"),
            P("fsdp", "tp"),
            P("tp"),
            P("tp", "fsdp"),
            P("fsdp"),
            P("fsdp"),
            P("fsdp"),
        ),
        check_vma=False,
    )

    def run(*arrays):
        fits = rows_path_fits(mesh, arrays[0], arrays[3], arrays[12])
        return split(per_device_rows if fits else per_device)(*arrays)

    return run
```

```python
import math

import jax
import jax.numpy as jnp
from jax import lax
from jax.experimental import pallas as pl
from jax.experimental.pallas import tpu as pltpu
from jax.sharding import PartitionSpec as P

HEAD_DIM = 64


epsilon = 1e-12
masked_score = -1e30


def passed_along(value, axis, steps):
    count = lax.axis_size(axis)
    pairs = [(source, (source + steps) % count) for source in range(count)]
    return lax.ppermute(value, axis, pairs)


def layer_norm(inputs, gain_vector, shift_vector):
    center = jnp.mean(inputs, axis=-1, keepdims=True)
    centered = inputs - center
    spread = jnp.mean(centered * centered, axis=-1, keepdims=True)
    return centered * lax.rsqrt(spread + epsilon) * gain_vector + shift_vector


def gelu_exact(inputs):
    return jax.nn.gelu(inputs, approximate=False)


def live_keys(lengths, first_key, key_count):
    places = first_key + lax.iota(jnp.int32, key_count)
    return (places[None, :] < lengths[:, None])[:, None, None, :]


def absorb(carried, queries, key_block, value_block, usable, score_scale):
    row_peak, row_total, summed = carried
    scores = (
        jnp.einsum("sqhe,skhe->shqk", queries, key_block, preferred_element_type=jnp.float32)
        * score_scale
    )
    masked = jnp.where(usable, scores, masked_score)
    new_peak = jnp.maximum(row_peak, jnp.max(masked, axis=-1))
    factor = jnp.exp(row_peak - new_peak)
    weights = jnp.where(usable, jnp.exp(masked - new_peak[..., None]), 0.0)
    row_total = row_total * factor + jnp.sum(weights, axis=-1)
    summed = summed * factor[..., None] + jnp.einsum(
        "shqk,skhe->shqe",
        weights.astype(jnp.bfloat16),
        value_block,
        preferred_element_type=jnp.float32,
    )
    return (new_peak, row_total, summed)


def block_grads(
    queries, grad_att, log_total, row_delta, key_block, value_block, usable, score_scale
):
    scores = (
        jnp.einsum("sqhe,skhe->shqk", queries, key_block, preferred_element_type=jnp.float32)
        * score_scale
    )
    masked = jnp.where(usable, scores, masked_score)
    weights = jnp.where(usable, jnp.exp(masked - log_total[..., None]), 0.0)
    grad_value = jnp.einsum(
        "shqk,sqhe->skhe",
        weights.astype(jnp.bfloat16),
        grad_att,
        preferred_element_type=jnp.float32,
    )
    grad_weights = jnp.einsum(
        "sqhe,skhe->shqk", grad_att, value_block, preferred_element_type=jnp.float32
    )
    grad_scores = (weights * (grad_weights - row_delta[..., None])).astype(jnp.bfloat16)
    grad_query = (
        jnp.einsum("shqk,skhe->sqhe", grad_scores, key_block, preferred_element_type=jnp.float32)
        * score_scale
    )
    grad_key = (
        jnp.einsum("shqk,sqhe->skhe", grad_scores, queries, preferred_element_type=jnp.float32)
        * score_scale
    )
    return (grad_query, grad_key, grad_value)


def per_device(
    tokens,
    lengths,
    cotangent,
    w_query,
    w_key,
    w_value,
    b_query,
    b_value,
    w_out,
    b_out,
    ln1_gain,
    ln1_shift,
    w_up,
    b_up,
    w_down,
    b_down,
    ln2_gain,
    ln2_shift,
):
    sequences, local_rows, model_width = tokens.shape
    token_count = sequences * local_rows
    ctx_count = lax.axis_size("ctx")
    ctx_index = lax.axis_index("ctx")
    (
        query_full,
        key_full,
        value_full,
        out_full,
        up_full,
        down_full,
        bias_out,
        gain_one,
        shift_one,
        bias_down,
        gain_two,
        shift_two,
    ) = (
        lax.all_gather(w_query, "fsdp", axis=0, tiled=True),
        lax.all_gather(w_key, "fsdp", axis=0, tiled=True),
        lax.all_gather(w_value, "fsdp", axis=0, tiled=True),
        lax.all_gather(w_out, "fsdp", axis=1, tiled=True),
        lax.all_gather(w_up, "fsdp", axis=0, tiled=True),
        lax.all_gather(w_down, "fsdp", axis=1, tiled=True),
        lax.all_gather(b_out, "fsdp", axis=0, tiled=True),
        lax.all_gather(ln1_gain, "fsdp", axis=0, tiled=True),
        lax.all_gather(ln1_shift, "fsdp", axis=0, tiled=True),
        lax.all_gather(b_down, "fsdp", axis=0, tiled=True),
        lax.all_gather(ln2_gain, "fsdp", axis=0, tiled=True),
        lax.all_gather(ln2_shift, "fsdp", axis=0, tiled=True),
    )
    flat_tokens = tokens.reshape(token_count, model_width)
    local_width = query_full.shape[1]
    head_count = local_width // HEAD_DIM
    score_scale = HEAD_DIM ** (-0.5)
    query_low = (
        jnp.dot(flat_tokens, query_full, preferred_element_type=jnp.float32)
        + b_query.astype(jnp.float32)
    ).astype(jnp.bfloat16)
    key_low = jnp.dot(flat_tokens, key_full, preferred_element_type=jnp.float32).astype(
        jnp.bfloat16
    )
    value_low = (
        jnp.dot(flat_tokens, value_full, preferred_element_type=jnp.float32)
        + b_value.astype(jnp.float32)
    ).astype(jnp.bfloat16)
    query_heads = query_low.reshape(sequences, local_rows, head_count, HEAD_DIM)
    key_local = key_low.reshape(sequences, local_rows, local_width)
    value_local = value_low.reshape(sequences, local_rows, local_width)
    query_first = ctx_index * local_rows
    start_state = (
        jnp.full((sequences, head_count, local_rows), masked_score, jnp.float32),
        jnp.zeros((sequences, head_count, local_rows), jnp.float32),
        jnp.zeros((sequences, head_count, local_rows, HEAD_DIM), jnp.float32),
    )
    key_part = lax.all_gather(key_local, "ctx", axis=1, tiled=True)
    value_part = lax.all_gather(value_local, "ctx", axis=1, tiled=True)
    key_count = key_part.shape[1]
    block_size = math.gcd(key_count, 512)

    def one_block(position, state_in):
        offset = position * block_size
        key_block = lax.dynamic_slice_in_dim(key_part, offset, block_size, 1).reshape(
            sequences, block_size, head_count, HEAD_DIM
        )
        value_block = lax.dynamic_slice_in_dim(value_part, offset, block_size, 1).reshape(
            sequences, block_size, head_count, HEAD_DIM
        )
        usable = live_keys(lengths, offset, block_size)
        return absorb(state_in, query_heads, key_block, value_block, usable, score_scale)

    row_peak, row_total, summed = lax.fori_loop(0, key_count // block_size, one_block, start_state)
    attended = (summed / row_total[..., None]).transpose(0, 2, 1, 3)
    log_total = row_peak + jnp.log(row_total)
    attended_low = attended.reshape(token_count, local_width).astype(jnp.bfloat16)
    branch = lax.psum(
        jnp.dot(attended_low, out_full, preferred_element_type=jnp.float32).astype(jnp.bfloat16),
        "tp",
    ).astype(jnp.float32) + bias_out.astype(jnp.float32)
    normed_one, norm_one_back = jax.vjp(
        layer_norm,
        flat_tokens.astype(jnp.float32) + branch,
        gain_one.astype(jnp.float32),
        shift_one.astype(jnp.float32),
    )
    normed_low = normed_one.astype(jnp.bfloat16)
    hidden_in = jnp.dot(normed_low, up_full, preferred_element_type=jnp.float32) + b_up.astype(
        jnp.float32
    )
    active, gelu_back = jax.vjp(gelu_exact, hidden_in)
    active_low = active.astype(jnp.bfloat16)
    second = lax.psum(
        jnp.dot(active_low, down_full, preferred_element_type=jnp.float32).astype(jnp.bfloat16),
        "tp",
    ).astype(jnp.float32) + bias_down.astype(jnp.float32)
    output, norm_two_back = jax.vjp(
        layer_norm, normed_one + second, gain_two.astype(jnp.float32), shift_two.astype(jnp.float32)
    )
    positions = query_first + lax.iota(jnp.int32, local_rows)
    row_valid = (positions[None, :] < lengths[:, None]).astype(jnp.float32).reshape(token_count, 1)
    grad_output = cotangent.reshape(token_count, model_width).astype(jnp.float32) * row_valid
    grad_resid_two, grad_gain_two, grad_shift_two = norm_two_back(grad_output)
    grad_second = grad_resid_two.astype(jnp.bfloat16)
    grad_w_down = jnp.einsum(
        "nf,nd->fd", active_low, grad_second, preferred_element_type=jnp.float32
    )
    grad_b_down = jnp.sum(grad_second.astype(jnp.float32), axis=0)
    (grad_hidden,) = gelu_back(
        jnp.einsum("nd,fd->nf", grad_second, down_full, preferred_element_type=jnp.float32)
    )
    grad_hidden_low = grad_hidden.astype(jnp.bfloat16)
    grad_w_up = jnp.einsum(
        "nd,nf->df", normed_low, grad_hidden_low, preferred_element_type=jnp.float32
    )
    grad_b_up = jnp.sum(grad_hidden_low.astype(jnp.float32), axis=0)
    grad_normed = grad_resid_two + lax.psum(
        jnp.einsum(
            "nf,df->nd", grad_hidden_low, up_full, preferred_element_type=jnp.float32
        ).astype(jnp.bfloat16),
        "tp",
    ).astype(jnp.float32)
    grad_resid_one, grad_gain_one, grad_shift_one = norm_one_back(grad_normed)
    grad_branch = grad_resid_one.astype(jnp.bfloat16)
    grad_w_out = jnp.einsum(
        "nc,nd->cd", attended_low, grad_branch, preferred_element_type=jnp.float32
    )
    grad_b_out = jnp.sum(grad_branch.astype(jnp.float32), axis=0)
    grad_att = jnp.einsum(
        "nd,cd->nc", grad_branch, out_full, preferred_element_type=jnp.float32
    ).astype(jnp.bfloat16)
    grad_att_heads = grad_att.reshape(sequences, local_rows, head_count, HEAD_DIM)
    row_delta = jnp.sum(grad_att_heads.astype(jnp.float32) * attended, axis=-1).transpose(0, 2, 1)
    zero_block = jnp.zeros((sequences, local_rows, head_count, HEAD_DIM), jnp.float32)

    def turn_grads(first_key, key_block, value_block):
        usable = live_keys(lengths, first_key, local_rows)
        key_heads = key_block.reshape(sequences, local_rows, head_count, HEAD_DIM)
        value_heads = value_block.reshape(sequences, local_rows, head_count, HEAD_DIM)
        return block_grads(
            query_heads,
            grad_att_heads,
            log_total,
            row_delta,
            key_heads,
            value_heads,
            usable,
            score_scale,
        )

    def cycle_turn(turn_index, carried):
        key_block, value_block, grad_key, grad_value, grad_query = carried
        source = (ctx_index - turn_index) % ctx_count
        added_query, added_key, added_value = turn_grads(
            source * local_rows, key_block, value_block
        )
        key_block, value_block = passed_along((key_block, value_block), "ctx", 1)
        grad_key, grad_value = (
            passed_along((grad_key + added_key).astype(jnp.bfloat16), "ctx", 1).astype(jnp.float32),
            passed_along((grad_value + added_value).astype(jnp.bfloat16), "ctx", 1).astype(
                jnp.float32
            ),
        )
        return (key_block, value_block, grad_key, grad_value, grad_query + added_query)

    cycle_end = lax.fori_loop(
        0, ctx_count, cycle_turn, (key_local, value_local, zero_block, zero_block, zero_block)
    )
    grad_key, grad_value, grad_query = (cycle_end[2], cycle_end[3], cycle_end[4])
    grad_query_low = grad_query.reshape(token_count, local_width).astype(jnp.bfloat16)
    grad_key_low = grad_key.reshape(token_count, local_width).astype(jnp.bfloat16)
    grad_value_low = grad_value.reshape(token_count, local_width).astype(jnp.bfloat16)
    grad_w_query = jnp.einsum(
        "nd,nc->dc", flat_tokens, grad_query_low, preferred_element_type=jnp.float32
    )
    grad_w_key = jnp.einsum(
        "nd,nc->dc", flat_tokens, grad_key_low, preferred_element_type=jnp.float32
    )
    grad_w_value = jnp.einsum(
        "nd,nc->dc", flat_tokens, grad_value_low, preferred_element_type=jnp.float32
    )
    grad_b_query = jnp.sum(grad_query_low.astype(jnp.float32), axis=0)
    grad_b_value = jnp.sum(grad_value_low.astype(jnp.float32), axis=0)
    back_in = (
        jnp.einsum("nc,dc->nd", grad_query_low, query_full, preferred_element_type=jnp.float32)
        + jnp.einsum("nc,dc->nd", grad_key_low, key_full, preferred_element_type=jnp.float32)
        + jnp.einsum("nc,dc->nd", grad_value_low, value_full, preferred_element_type=jnp.float32)
    )
    grad_tokens = grad_resid_one + lax.psum(back_in.astype(jnp.bfloat16), "tp").astype(jnp.float32)
    (
        share_query,
        share_key,
        share_value,
        share_out,
        share_up,
        share_down,
        share_bias_out,
        share_gain_one,
        share_shift_one,
        share_bias_down,
        share_gain_two,
        share_shift_two,
    ) = (
        lax.psum_scatter(
            grad_w_query.astype(jnp.bfloat16), "fsdp", scatter_dimension=0, tiled=True
        ).astype(jnp.float32),
        lax.psum_scatter(
            grad_w_key.astype(jnp.bfloat16), "fsdp", scatter_dimension=0, tiled=True
        ).astype(jnp.float32),
        lax.psum_scatter(
            grad_w_value.astype(jnp.bfloat16), "fsdp", scatter_dimension=0, tiled=True
        ).astype(jnp.float32),
        lax.psum_scatter(
            grad_w_out.astype(jnp.bfloat16), "fsdp", scatter_dimension=1, tiled=True
        ).astype(jnp.float32),
        lax.psum_scatter(
            grad_w_up.astype(jnp.bfloat16), "fsdp", scatter_dimension=0, tiled=True
        ).astype(jnp.float32),
        lax.psum_scatter(
            grad_w_down.astype(jnp.bfloat16), "fsdp", scatter_dimension=1, tiled=True
        ).astype(jnp.float32),
        lax.psum_scatter(
            grad_b_out.astype(jnp.bfloat16), "fsdp", scatter_dimension=0, tiled=True
        ).astype(jnp.float32),
        lax.psum_scatter(
            grad_gain_one.astype(jnp.bfloat16), "fsdp", scatter_dimension=0, tiled=True
        ).astype(jnp.float32),
        lax.psum_scatter(
            grad_shift_one.astype(jnp.bfloat16), "fsdp", scatter_dimension=0, tiled=True
        ).astype(jnp.float32),
        lax.psum_scatter(
            grad_b_down.astype(jnp.bfloat16), "fsdp", scatter_dimension=0, tiled=True
        ).astype(jnp.float32),
        lax.psum_scatter(
            grad_gain_two.astype(jnp.bfloat16), "fsdp", scatter_dimension=0, tiled=True
        ).astype(jnp.float32),
        lax.psum_scatter(
            grad_shift_two.astype(jnp.bfloat16), "fsdp", scatter_dimension=0, tiled=True
        ).astype(jnp.float32),
    )
    (
        share_query,
        share_key,
        share_value,
        share_out,
        share_up,
        share_down,
        share_bias_out,
        share_gain_one,
        share_shift_one,
        share_bias_down,
        share_gain_two,
        share_shift_two,
    ) = (
        lax.psum(share_query.astype(jnp.bfloat16), "ctx").astype(jnp.float32),
        lax.psum(share_key.astype(jnp.bfloat16), "ctx").astype(jnp.float32),
        lax.psum(share_value.astype(jnp.bfloat16), "ctx").astype(jnp.float32),
        lax.psum(share_out.astype(jnp.bfloat16), "ctx").astype(jnp.float32),
        lax.psum(share_up.astype(jnp.bfloat16), "ctx").astype(jnp.float32),
        lax.psum(share_down.astype(jnp.bfloat16), "ctx").astype(jnp.float32),
        lax.psum(share_bias_out.astype(jnp.bfloat16), "ctx").astype(jnp.float32),
        lax.psum(share_gain_one.astype(jnp.bfloat16), "ctx").astype(jnp.float32),
        lax.psum(share_shift_one.astype(jnp.bfloat16), "ctx").astype(jnp.float32),
        lax.psum(share_bias_down.astype(jnp.bfloat16), "ctx").astype(jnp.float32),
        lax.psum(share_gain_two.astype(jnp.bfloat16), "ctx").astype(jnp.float32),
        lax.psum(share_shift_two.astype(jnp.bfloat16), "ctx").astype(jnp.float32),
    )
    total_b_query, total_b_value, total_b_up = lax.psum(
        (grad_b_query, grad_b_value, grad_b_up), ("fsdp", "ctx")
    )
    return (
        output.astype(jnp.bfloat16).reshape(sequences, local_rows, model_width),
        grad_tokens.reshape(sequences, local_rows, model_width),
        share_query,
        share_key,
        share_value,
        total_b_query,
        total_b_value,
        share_out,
        share_bias_out,
        share_gain_one,
        share_shift_one,
        share_up,
        total_b_up,
        share_down,
        share_bias_down,
        share_gain_two,
        share_shift_two,
    )


def swapped(value, axis, bit):
    count = lax.axis_size(axis)
    return lax.ppermute(value, axis, [(place, place ^ bit) for place in range(count)])


def shifted(value, axis, steps):
    count = lax.axis_size(axis)
    return lax.ppermute(value, axis, [(place, (place + steps) % count) for place in range(count)])


def to_owner(value, step, back=False):
    pairs = []
    for x in range(2):
        for z in range(4):
            block = z ^ step
            source = x * 4 + z
            target = (block >> 1) * 4 + (block ^ (2 * x))
            pairs.append((target, source) if back else (source, target))
    return lax.ppermute(value, ("ctx", "tp"), pairs)


ANY = pl.BlockSpec(memory_space=pl.ANY)
WHOLE = pl.BlockSpec(memory_space=pltpu.VMEM)
log2_e = math.log2(math.e)
EXTRA = 8


def low(value):
    return value.astype(jnp.bfloat16)


def wide(value):
    return value.astype(jnp.float32)


def dot32(left, right, left_dim, right_dim):
    return lax.dot_general(
        left, right, (((left_dim,), (right_dim,)), ((), ())), preferred_element_type=jnp.float32
    )


def struct(shape, dtype=jnp.bfloat16):
    return jax.ShapeDtypeStruct(shape, dtype)


def cost(flops, moved, special=0):
    return pl.CostEstimate(flops=int(flops), bytes_accessed=int(moved), transcendentals=int(special))


def stack_kernel(*refs):
    for place, ref in enumerate(refs[:-1]):
        refs[-1][place] = ref[...]


def stacked(pieces):
    shape = (len(pieces),) + pieces[0].shape
    return pl.pallas_call(
        stack_kernel,
        out_shape=struct(shape),
        in_specs=[WHOLE] * len(pieces),
        out_specs=WHOLE,
        cost_estimate=cost(0, 4 * math.prod(shape)),
        name="stack_pieces",
    )(*pieces)


def piece_copies(meta, pieces, taken, columns, target, sems, first):
    x, z, f = meta[0], meta[1], meta[2]
    copies = []
    parts = [(piece, step) for piece in pieces for step in range(piece.shape[0])]
    for index, (piece, step) in enumerate(parts):
        place, slot = index // 4, index % 4
        across = (place % 2, 2 * ((place // 2) % 2) + place // 4)
        start = pl.multiple_of(((f ^ across[1]) * 2 + (x ^ across[0])) * taken, taken)
        copies.append(
            pltpu.make_async_copy(
                piece.at[step, pl.ds(0, taken), columns],
                target.at[z ^ slot, pl.ds(start, taken), :],
                sems.at[first + len(copies)],
            )
        )
    return copies


def attend_kernel(
    meta, own, other, w0, w1, w2, w3, bias, qkv, o0, o1, o2, o3, stats, weight, vectors,
    mask, shards, *, block, heads
):
    step = pl.program_id(0)
    shard = w0.shape[0] - EXTRA
    half = own.shape[1]
    scale = log2_e * HEAD_DIM ** (-0.5)

    @pl.when(step == 0)
    def _():
        for place, piece in enumerate((w0, w1, w2, w3)):
            start = pl.multiple_of((meta[2] ^ place) * shard, shard)
            weight[pl.ds(start, shard), :] = piece[:shard, :]
            shards[meta[2] ^ place] = piece[shard:, :]
        vectors[6:8, :] = jnp.zeros((2, 4 * shard), jnp.float32)
        for place in range(4):
            for row in range(6):
                first = row % 3 * shard
                vectors[row : row + 1, place * shard : (place + 1) * shard] = wide(
                    shards[place, row // 3 : row // 3 + 1, first : first + shard]
                )
        for place, rows in enumerate((own, other)):
            source = rows[0] if place == 0 else rows[...]
            qkv[place * half : (place + 1) * half, :] = low(
                dot32(source, weight[...], 1, 0) + bias[...]
            )
            first = (meta[0] ^ place) * half
            position = first + lax.broadcasted_iota(jnp.int32, (half, block), 0)
            mask[place * half : (place + 1) * half, :] = jnp.where(
                position < meta[3], 0.0, masked_score
            )

    rows = pl.ds(pl.multiple_of((meta[7] ^ step) * block, block), block)
    outs, logs = [], []
    for head in range(heads):
        base = 3 * head * HEAD_DIM
        query = qkv[rows, base : base + HEAD_DIM]
        key = qkv[:, base + HEAD_DIM : base + 2 * HEAD_DIM]
        value = qkv[:, base + 2 * HEAD_DIM : base + 3 * HEAD_DIM]
        scores = dot32(key, query, 1, 1) * scale + mask[...]
        peak = jnp.max(scores, axis=0, keepdims=True)
        weights = jnp.exp2(scores - peak)
        total = jnp.sum(weights, axis=0, keepdims=True)
        outs.append((dot32(value, low(weights), 0, 0) / total).T)
        logs.append(peak + jnp.log2(total))
    result = low(jnp.concatenate(outs, axis=1))
    for place, out in enumerate((o0, o1, o2, o3)):

        @pl.when(step == place)
        def _(out=out):
            out[...] = result

    stats[0] = jnp.concatenate(logs + [jnp.zeros((8 - heads, block), jnp.float32)], axis=0)


def attend_call(meta, tokens, other, pieces, bias, heads):
    half, width = other.shape
    block = half // 2
    columns = pieces[0].shape[1]
    whole = lambda shape: pl.BlockSpec(shape, lambda step, meta: (0,) * len(shape))
    rows = 2 * half
    return pl.pallas_call(
        lambda *refs: attend_kernel(*refs, block=block, heads=heads),
        grid_spec=pltpu.PrefetchScalarGridSpec(
            num_scalar_prefetch=1,
            grid=(4,),
            in_specs=[
                pl.BlockSpec((1, half, width), lambda step, meta: (meta[0], 0, 0)),
                whole((half, width)),
                *[whole(piece.shape) for piece in pieces],
                whole((1, columns)),
            ],
            out_specs=[
                whole((rows, columns)),
                *[whole((block, columns // 3))] * 4,
                pl.BlockSpec((1, 8, block), lambda step, meta: (step, 0, 0)),
                whole((width, columns)),
                whole((EXTRA, width)),
            ],
            scratch_shapes=[
                pltpu.VMEM((rows, block), jnp.float32),
                pltpu.VMEM((4, EXTRA, columns), jnp.bfloat16),
            ],
        ),
        out_shape=[struct((rows, columns))]
        + [struct((block, columns // 3))] * 4
        + [struct((4, 8, block), jnp.float32), struct((width, columns))]
        + [struct((EXTRA, width), jnp.float32)],
        cost_estimate=cost(2 * rows * width * columns + 16 * rows * rows * columns, 8e6, rows * rows * 3),
        name="attend",
    )(meta, tokens, other, *pieces, bias)


def attend_back_kernel(
    meta, qkv, d0, d1, d2, d3, o0, o1, o2, o3, stats, weight, full, p0, p1, p2, p3,
    grads, mask, grad_att, attended, *, block, heads
):
    step = pl.program_id(0)
    rows_all = qkv.shape[0]
    half = rows_all // 2
    scale = log2_e * HEAD_DIM ** (-0.5)

    @pl.when(step == 0)
    def _():
        grads[...] = jnp.zeros_like(grads)
        for place in range(2):
            first = (meta[0] ^ place) * half
            position = first + lax.broadcasted_iota(jnp.int32, (half, block), 0)
            mask[place * half : (place + 1) * half, :] = jnp.where(
                position < meta[3], 0.0, masked_score
            )

    for place, (grad, out) in enumerate(zip((d0, d1, d2, d3), (o0, o1, o2, o3))):

        @pl.when(step == place)
        def _(grad=grad, out=out):
            grad_att[...] = grad[...]
            attended[...] = out[...]

    rows = pl.ds(pl.multiple_of((meta[7] ^ step) * block, block), block)
    for head in range(heads):
        base = 3 * head * HEAD_DIM
        span = slice(head * HEAD_DIM, (head + 1) * HEAD_DIM)
        query = qkv[rows, base : base + HEAD_DIM]
        key = qkv[:, base + HEAD_DIM : base + 2 * HEAD_DIM]
        value = qkv[:, base + 2 * HEAD_DIM : base + 3 * HEAD_DIM]
        grad_out = grad_att[:, span]
        products = wide(grad_out) * wide(attended[:, span])
        delta = lax.dot_general(
            jnp.ones((8, HEAD_DIM), jnp.float32),
            products,
            (((1,), (1,)), ((), ())),
            precision=lax.Precision.HIGHEST,
            preferred_element_type=jnp.float32,
        )[:1]
        scores = dot32(key, query, 1, 1) * scale + mask[...]
        weights = jnp.exp2(scores - stats[0, head : head + 1, :])
        grad_weights = dot32(value, grad_out, 1, 1)
        grad_scores = low(weights * (grad_weights - delta))
        grads[2 * head] += dot32(grad_scores, query, 1, 0)
        grads[2 * head + 1] += dot32(low(weights), grad_out, 1, 0)
        full[rows, base : base + HEAD_DIM] = low(
            dot32(grad_scores, key, 0, 0) * HEAD_DIM ** (-0.5)
        )

    @pl.when(step == 3)
    def _():
        for head in range(heads):
            base = 3 * head * HEAD_DIM
            full[:, base + HEAD_DIM : base + 2 * HEAD_DIM] = low(
                grads[2 * head] * HEAD_DIM ** (-0.5)
            )
            full[:, base + 2 * HEAD_DIM : base + 3 * HEAD_DIM] = low(grads[2 * head + 1])
        for place, part in enumerate((p0, p1, p2, p3)):
            span = pl.ds(pl.multiple_of((meta[7] ^ place) * block, block), block)
            part[...] = low(dot32(full[span, :], weight[...], 1, 1))


def attend_back_call(meta, qkv, grad_parts, parts, stats, weight, heads):
    rows, columns = qkv.shape
    width = weight.shape[0]
    block = rows // 4
    whole = lambda shape: pl.BlockSpec(shape, lambda step, meta: (0,) * len(shape))
    small = whole((block, columns // 3))
    return pl.pallas_call(
        lambda *refs: attend_back_kernel(*refs, block=block, heads=heads),
        grid_spec=pltpu.PrefetchScalarGridSpec(
            num_scalar_prefetch=1,
            grid=(4,),
            in_specs=[whole((rows, columns))]
            + [small] * 8
            + [pl.BlockSpec((1, 8, block), lambda step, meta: (step, 0, 0)), whole(weight.shape)],
            out_specs=[whole((rows, columns))] + [whole((block, width))] * 4,
            scratch_shapes=[
                pltpu.VMEM((2 * heads, rows, HEAD_DIM), jnp.float32),
                pltpu.VMEM((rows, block), jnp.float32),
                pltpu.VMEM((block, columns // 3), jnp.bfloat16),
                pltpu.VMEM((block, columns // 3), jnp.bfloat16),
            ],
        ),
        out_shape=[struct((rows, columns))] + [struct((block, width))] * 4,
        cost_estimate=cost(40 * rows * rows * columns, 8e6, rows * rows * 3),
        name="attend_back",
    )(meta, qkv, *grad_parts, *parts, stats, weight)


def norm_parts(inputs):
    center = jnp.mean(inputs, axis=-1, keepdims=True)
    centered = inputs - center
    spread = jnp.mean(centered * centered, axis=-1, keepdims=True)
    inverse = lax.rsqrt(spread + epsilon)
    return centered * inverse, inverse


def norm_back(grad_out, hat, inverse, gain):
    scaled = grad_out * gain
    return inverse * (
        scaled
        - jnp.mean(scaled, axis=-1, keepdims=True)
        - hat * jnp.mean(scaled * hat, axis=-1, keepdims=True)
    )


BIAS_OUT, GAIN_ONE, SHIFT_ONE, BIAS_DOWN, GAIN_TWO, SHIFT_TWO = range(6)


def first_kernel(meta, *refs, width):
    att, tok, vectors, lines, pieces = refs[:4], refs[4], refs[5], refs[6], refs[7:15]
    hat, inverse, both, slope, out_w, up_w, sems = refs[15:]
    hidden = up_w.shape[2]
    taken = pieces[0].shape[1]
    copies = piece_copies(meta, pieces, taken, pl.ds(hidden, out_w.shape[2]), out_w, sems, 0)
    copies += piece_copies(meta, pieces, taken, pl.ds(0, hidden), up_w, sems, 32)
    for copy in copies:
        copy.start()
    for step in range(4):
        both[step, :, hidden : hidden + width] = att[step][...]
        both[step, :, hidden + width :] = jnp.zeros_like(both[step, :, hidden + width :])
    for copy in copies:
        copy.wait()
    branch = vectors[BIAS_OUT : BIAS_OUT + 1, :]
    for step in range(4):
        branch = branch + dot32(att[step][...], out_w[meta[4] ^ step][:, :width], 1, 1)
    hat_one, inverse_one = norm_parts(wide(tok[0]) + branch)
    hat[...] = hat_one
    inverse[...] = inverse_one
    normed = low(hat_one * vectors[GAIN_ONE : GAIN_ONE + 1, :] + vectors[SHIFT_ONE : SHIFT_ONE + 1, :])
    for place in range(4):
        inputs = dot32(normed, up_w[place], 1, 0) + wide(lines[meta[1] ^ place, 0:1, :])
        cumulative = 0.5 * (1.0 + lax.erf(inputs * (0.5**0.5)))
        density = jnp.exp(-0.5 * inputs * inputs) * ((0.5 / math.pi) ** 0.5)
        both[place, :, :hidden] = low(inputs * cumulative)
        slope[place] = low(cumulative + inputs * density)


def second_kernel(meta, *refs, width):
    hat, inverse, both, slope, cot, vectors = refs[:6]
    pieces_a, pieces_b = refs[6:14], refs[14:24]
    output, resid, g0, g1, g2, g3, mixed, keep = refs[24:32]
    out_w, up_w, down_w, blocks, small, small_blocks, sems = refs[32:]
    rows, model = hat.shape
    hidden = up_w.shape[2]
    taken = pieces_a[0].shape[1]
    down_copies = piece_copies(meta, pieces_b, taken, pl.ds(0, hidden), down_w, sems, 0)
    copies = piece_copies(meta, pieces_a, taken, pl.ds(0, hidden), up_w, sems, 32)
    copies += piece_copies(meta, pieces_a, taken, pl.ds(hidden, out_w.shape[2]), out_w, sems, 64)
    for copy in down_copies + copies:
        copy.start()
    row = lambda place: vectors[place : place + 1, :]
    hat_one, inverse_one = hat[...], inverse[...]
    normed_one = hat_one * row(GAIN_ONE) + row(SHIFT_ONE)
    for copy in down_copies:
        copy.wait()
    second = row(BIAS_DOWN)
    for place in range(4):
        second = second + dot32(both[place, :, :hidden], down_w[place], 1, 1)
    hat_two, inverse_two = norm_parts(normed_one + second)
    output[...] = low(hat_two * row(GAIN_TWO) + row(SHIFT_TWO))
    position = meta[4] * rows + lax.broadcasted_iota(jnp.int32, (rows, model), 0)
    grad_output = jnp.where(position < meta[8], wide(cot[0]), 0.0)
    grad_two = norm_back(grad_output, hat_two, inverse_two, row(GAIN_TWO))
    grad_second = low(grad_two)
    for copy in copies:
        copy.wait()
    grad_normed = grad_two
    sums = lambda array: jnp.sum(array, axis=0, keepdims=True)
    for place in range(4):
        grad_hidden = low(dot32(grad_second, down_w[place], 1, 0) * wide(slope[place]))
        mixed[place, :rows, :] = grad_hidden
        mixed[place, rows:, :] = low(
            jnp.broadcast_to(sums(wide(grad_hidden)), (EXTRA, hidden))
        )
        grad_normed = grad_normed + dot32(grad_hidden, up_w[place], 1, 1)
    grad_one = norm_back(grad_normed, hat_one, inverse_one, row(GAIN_ONE))
    resid[...] = grad_one
    grad_branch = low(grad_one)
    for step, out in enumerate((g0, g1, g2, g3)):
        out[...] = low(dot32(grad_branch, out_w[meta[4] ^ step][:, :width], 1, 0))
    small[0:1, :] = sums(wide(grad_branch))
    small[1:2, :] = sums(grad_normed * hat_one)
    small[2:3, :] = sums(grad_normed)
    small[3:4, :] = sums(wide(grad_second))
    small[4:5, :] = sums(grad_output * hat_two)
    small[5:6, :] = sums(grad_output)
    small[6:8, :] = jnp.zeros((2, model), jnp.float32)
    shard = model // 4
    for place in range(4):
        small_blocks[place] = low(small[:, place * shard : (place + 1) * shard])
    for kind, array in enumerate((grad_second, low(normed_one), grad_branch)):
        for place in range(4):
            blocks[place] = array[:, place * shard : (place + 1) * shard]
        for far in range(2):
            keep[kind, far, :rows, :] = blocks[meta[2] ^ (2 * far)]
            keep[kind, far, rows:, :] = small_blocks[meta[2] ^ (2 * far)]
            columns = slice(kind * shard, (kind + 1) * shard)
            mixed[4 + far, :rows, columns] = blocks[meta[2] ^ (2 * far + 1)]
            mixed[4 + far, rows:, columns] = small_blocks[meta[2] ^ (2 * far + 1)]
    for far in range(2):
        mixed[4 + far, :, 3 * shard :] = jnp.zeros((rows + EXTRA, hidden - 3 * shard), jnp.bfloat16)


def weights_kernel(meta, *refs, width):
    keep, both, both_sib, mixed, mixed_sib = refs[:5]
    near_up, far_up, mine_down, theirs_down, turned, whole = refs[5:]
    shard = keep.shape[3]
    rows = both.shape[1]
    half = shard // 2
    hidden = mixed.shape[2]
    padded = both.shape[2] - hidden
    starts = [pl.multiple_of(side * half, half) for side in (meta[0], 1 - meta[0])]

    def slot(block):
        apart = block ^ meta[1]
        return 2 * (apart & 1) + (apart >> 1)

    for kind in range(3):
        for far in range(2):
            span = slice(far * shard, (far + 1) * shard)
            turned[span, :rows] = keep[kind, far, :rows, :].T
            turned[span, rows:] = mixed_sib[4 + far, :rows, kind * shard : (kind + 1) * shard].T
        for place in range(4):
            if kind == 1:
                left, right = mixed[place, :rows, :], mixed_sib[place, :rows, :]
            else:
                columns = slice(0, hidden) if kind == 0 else slice(hidden, None)
                left, right = both[place, :, columns], both_sib[place, :, columns]
            value = dot32(turned[:, :rows], left, 1, 0) + dot32(turned[:, rows:], right, 1, 0)
            target = slot(meta[4] ^ place if kind == 2 else place)
            count = value.shape[1]
            whole[:, :count] = value
            for far in range(2):
                for side, start in enumerate(starts):
                    part = low(whole[pl.ds(far * shard + start, half), :count])
                    if kind == 0:
                        split = hidden - mine_down.shape[3]
                        (mine_down, theirs_down)[side][far, target, :half, :] = part[:, split:]
                        (near_up, far_up)[far][side, target, :half, hidden + padded :] = part[:, :split]
                    elif kind == 1:
                        (near_up, far_up)[far][side, target, :half, :hidden] = part
                    else:
                        (near_up, far_up)[far][side, target, :half, hidden : hidden + padded] = part
    for far in range(2):
        vector_sums = low(wide(keep[0, far, rows:, :]) + wide(mixed_sib[4 + far, rows:, :shard]))
        for place in range(4):
            hidden_sums = low(wide(mixed[place, rows:, :]) + wide(mixed_sib[place, rows:, :]))
            for side in range(2):
                out = (mine_down, theirs_down)[side]
                out[far, place, half:, :] = jnp.zeros((EXTRA, out.shape[3]), jnp.bfloat16)
                out = (near_up, far_up)[far]
                out[side, slot(place), half:, :hidden] = hidden_sums
                out[side, place, half:, hidden : hidden + shard] = vector_sums
                rest = slice(hidden + shard, None)
                out[side, place, half:, rest] = jnp.zeros_like(out[side, place, half:, rest])


def projections_kernel(meta, own, other, grads, kept, sent, whole):
    half, shard = other.shape[0], other.shape[1] // 4
    count = grads.shape[1]
    whole[...] = dot32(own[0], grads[:half, :], 0, 0) + dot32(other[...], grads[half:, :], 0, 0)
    sums = jnp.broadcast_to(jnp.sum(wide(grads[...]), axis=0, keepdims=True), (EXTRA, count))
    for far in range(2):
        for out, place in ((kept, meta[2] ^ (2 * far)), (sent, meta[2] ^ (2 * far + 1))):
            value = whole[pl.ds(pl.multiple_of(place * shard, shard), shard), :]
            out[far, :shard, :count] = value.astype(out.dtype)
            out[far, shard:, :count] = sums.astype(out.dtype)
            out[far, :, count:] = jnp.zeros_like(out[far, :, count:])


def per_device_rows(
    tokens,
    lengths,
    cotangent,
    w_query,
    w_key,
    w_value,
    b_query,
    b_value,
    w_out,
    b_out,
    ln1_gain,
    ln1_shift,
    w_up,
    b_up,
    w_down,
    b_down,
    ln2_gain,
    ln2_shift,
):
    sequences, local_rows, model = tokens.shape
    x, f, z = lax.axis_index("ctx"), lax.axis_index("fsdp"), lax.axis_index("tp")
    rows = local_rows // 2
    width = w_query.shape[1]
    heads = width // HEAD_DIM
    hidden = w_up.shape[1]
    shard = w_query.shape[0]
    half = shard // 2
    padded = -(-width // 128) * 128
    own_seq, own_place = (z // 2) ^ x, z % 2
    quarter = 2 * x + own_place
    length_of = lambda place: lax.dynamic_index_in_dim(lengths, place, 0, keepdims=False)
    entries = (x, z, f, length_of(x), quarter, own_seq, own_place, z ^ (2 * x), length_of(own_seq))
    places = lax.iota(jnp.int32, len(entries))
    meta = sum(jnp.where(places == place, entry, 0) for place, entry in enumerate(entries))
    meta = meta.astype(jnp.int32)
    tied = lambda *values: lax.optimization_barrier(values)

    take_half = lambda pack: lax.dynamic_slice_in_dim(pack, x * half, half, 0)
    wider = lambda array, columns: jnp.pad(array, ((0, 0), (0, columns - array.shape[1])))
    columns_a = hidden + padded
    half_a = wider(take_half(jnp.concatenate([w_up, w_out.T], axis=1)), columns_a)
    half_b = jnp.concatenate(
        [take_half(w_down.T), b_up[None], jnp.zeros((EXTRA - 1, hidden), jnp.bfloat16)]
    )

    other = lax.dynamic_index_in_dim(tokens, 1 - x, 0, keepdims=False)
    other, half_a = tied(other, half_a)
    other = swapped(other, "ctx", 1)
    far_a, near_half = swapped(half_a, "tp", 2), swapped(half_a, "tp", 1)
    per_head = lambda weights: jnp.concatenate(
        [
            weight[..., head * HEAD_DIM : (head + 1) * HEAD_DIM]
            for head in range(heads)
            for weight in weights
        ],
        axis=-1,
    )
    vectors = jnp.concatenate([b_out, ln1_gain, ln1_shift, b_down, ln2_gain, ln2_shift])
    qkv_shard = jnp.concatenate(
        [
            per_head((w_query, w_key, w_value)),
            jnp.pad(vectors.reshape(2, 3 * width), ((0, EXTRA - 2), (0, 0))),
        ]
    )
    qkv_bias = wide(per_head((b_query, jnp.zeros_like(b_query), b_value)))[None, :]
    qkv_y, far_a, meta = tied(swapped(qkv_shard, "fsdp", 2), far_a, meta)
    line_a = stacked([half_a, near_half, far_a, swapped(far_a, "tp", 1)])
    qkv_pieces = (qkv_shard, swapped(qkv_shard, "fsdp", 1), qkv_y, swapped(qkv_y, "fsdp", 1))

    core = lambda array: swapped(array, "fsdp", 1)
    meta, qkv_bias, other, line_a, half_b, *qkv_pieces = tied(
        meta, qkv_bias, other, line_a, half_b, *qkv_pieces
    )
    x_a, y_a = swapped(line_a, "ctx", 1), swapped(line_a, "fsdp", 2)
    qkv, *parts, stats, weight, vectors = attend_call(
        meta, tokens, other, qkv_pieces, qkv_bias, heads
    )
    b_pieces = [swapped(half_b, "tp", bit) for bit in (1, 2, 3)]

    x_a, y_a, line_a, *rest = tied(x_a, y_a, line_a, *b_pieces, *parts)
    b_pieces, parts = rest[:3], rest[3:]
    line_b = stacked([half_b, *b_pieces])
    att = [to_owner(part, step) for step, part in enumerate(parts)]
    x_y_a = swapped(x_a, "fsdp", 2)
    x_y_a, x_a, y_a, line_a, line_b, *att = tied(x_y_a, x_a, y_a, line_a, line_b, *att)
    near_a = (line_a, x_a, y_a, x_y_a)
    pieces_a = (*near_a, *map(core, near_a))
    x_b, y_b, line_core = swapped(line_b, "ctx", 1), swapped(line_b, "fsdp", 2), core(line_b)

    def row_spec(array):
        return pl.BlockSpec((1, rows, model), lambda step, meta: (meta[5], meta[6], 0))

    vm = lambda shape, dtype=jnp.bfloat16: pltpu.VMEM(shape, dtype)
    weights_scratch = [vm((4, model, padded)), vm((4, model, hidden))]
    grid = lambda inputs, outputs, scratch: pltpu.PrefetchScalarGridSpec(
        num_scalar_prefetch=1, grid=(1,), in_specs=inputs, out_specs=outputs, scratch_shapes=scratch
    )
    full = lambda shape: pl.BlockSpec(shape, lambda step, meta: (0,) * len(shape))
    specs = lambda shapes: [full(item.shape) for item in shapes]

    first_out = [
        struct((rows, model), jnp.float32),
        struct((rows, 1), jnp.float32),
        struct((4, rows, columns_a)),
        struct((4, rows, hidden)),
    ]
    hat, inverse, both, slope = pl.pallas_call(
        lambda *refs: first_kernel(*refs, width=width),
        grid_spec=grid(
            [full((rows, width))] * 4
            + [row_spec(tokens), full((EXTRA, model))]
            + [pl.BlockSpec((4, EXTRA, hidden), lambda step, meta: (0, half // EXTRA, 0))]
            + [ANY] * 8,
            specs(first_out),
            weights_scratch + [pltpu.SemaphoreType.DMA((64,))],
        ),
        out_shape=first_out,
        cost_estimate=cost(2 * rows * model * (model + 4 * hidden), 12e6, rows * hidden * 8),
        name="feed_first",
    )(meta, *att, tokens, vectors, line_b, *pieces_a)

    both, x_b, y_b, line_b, line_core = tied(both, x_b, y_b, line_b, line_core)
    x_y_b = [swapped(x_b[:2], "fsdp", 2), swapped(y_b[2:], "ctx", 1)]
    *x_y_b, x_core, y_core, both_sib = tied(*x_y_b, core(x_b), core(y_b), core(both))
    pieces_b = (line_b, x_b, y_b, *x_y_b, line_core, x_core, y_core, *map(core, x_y_b))

    second_out = [
        struct((rows, model)),
        struct((rows, model), jnp.float32),
        *[struct((rows, width))] * 4,
        struct((6, rows + EXTRA, hidden)),
        struct((3, 2, rows + EXTRA, shard)),
    ]
    output, resid, g0, g1, g2, g3, mixed, keep = pl.pallas_call(
        lambda *refs: second_kernel(*refs, width=width),
        grid_spec=grid(
            [full(item.shape) for item in (hat, inverse, both, slope)]
            + [row_spec(cotangent), full((EXTRA, model))]
            + [ANY] * 18,
            specs(second_out),
            weights_scratch
            + [
                vm((4, model, hidden)),
                vm((4, rows, shard)),
                vm((EXTRA, model), jnp.float32),
                vm((4, EXTRA, shard)),
                pltpu.SemaphoreType.DMA((96,)),
            ],
        ),
        out_shape=second_out,
        cost_estimate=cost(2 * rows * model * (model + 12 * hidden), 20e6),
        name="feed_second",
    )(meta, hat, inverse, both, slope, cotangent, vectors, *pieces_a, *pieces_b)

    grad_att = [to_owner(part, step, True) for step, part in enumerate((g0, g1, g2, g3))]

    first_x = 2 * padded
    pack = struct((2, 4, half + EXTRA, first_x))
    pack_up = struct((2, 4, half + EXTRA, columns_a + hidden - first_x))
    mixed_sib = core(mixed)
    near_up, far_up, mine_down, theirs_down = pl.pallas_call(
        lambda *refs: weights_kernel(*refs, width=width),
        grid_spec=grid(
            specs([keep, both, both_sib, mixed, mixed_sib]),
            specs([pack_up] * 2 + [pack] * 2),
            [vm((2 * shard, 2 * rows)), vm((2 * shard, hidden), jnp.float32)],
        ),
        out_shape=[pack_up] * 2 + [pack] * 2,
        cost_estimate=cost(8 * rows * shard * (8 * hidden + 4 * width), 20e6),
        name="feed_weights",
    )(meta, keep, both, both_sib, mixed, mixed_sib)

    near_out = swapped(output, "tp", 1)
    far_up, theirs_down, output, *grad_att = tied(far_up, theirs_down, output, *grad_att)
    got_up, got_down = swapped(far_up, "fsdp", 2), swapped(theirs_down, "ctx", 1)
    far_out = swapped(output, "tp", 2)
    grad_full, *grad_parts = attend_back_call(meta, qkv, grad_att, parts, stats, weight, heads)

    near_out, far_out, *grad_parts = tied(near_out, far_out, *grad_parts)
    grad_rows = [to_owner(part, step) for step, part in enumerate(grad_parts)]
    grad_full, grad_rows[0] = tied(grad_full, grad_rows[0])
    kept, sent = pl.pallas_call(
        projections_kernel,
        grid_spec=grid(
            [pl.BlockSpec((1, local_rows, model), lambda step, meta: (meta[0], 0, 0))]
            + [full((local_rows, model)), full(grad_full.shape)],
            [full((2, shard + EXTRA, 640 * width // 192))] * 2,
            [vm((model, 3 * width), jnp.float32)],
        ),
        out_shape=[
            struct((2, shard + EXTRA, 640 * width // 192), dtype) for dtype in (jnp.float32, jnp.bfloat16)
        ],
        cost_estimate=cost(12 * local_rows * model * width, 8e6),
        name="projection_weights",
    )(meta, tokens, other, grad_full)
    far_out, up_sent, down_sent, kept, sent, *grad_rows = tied(
        far_out,
        low(wide(near_up[1]) + wide(got_up[1])),
        low(wide(mine_down[1]) + wide(got_down[1])),
        kept,
        sent,
        *grad_rows,
    )
    second_up, second_down = swapped(up_sent, "ctx", 1), swapped(down_sent, "fsdp", 2)
    def spread_rows(pieces, dtype):
        blocks = [
            lax.select_n(z ^ (2 * x), *[pieces[block ^ place] for place in range(4)]).astype(dtype)
            for block in range(4)
        ]
        return jnp.stack([jnp.concatenate(blocks[2 * seq : 2 * seq + 2]) for seq in range(2)])

    token_rows = resid
    for part in grad_rows:
        token_rows = token_rows + wide(part)

    token_rows = low(token_rows)
    far_z, last_out, near_z, sent, second_up, second_down = tied(
        swapped(token_rows, "tp", 2),
        swapped(far_out, "tp", 1),
        token_rows,
        sent,
        second_up,
        second_down,
    )
    output_full = spread_rows([output, near_out, far_out, last_out], jnp.bfloat16)
    up_lines = wide(near_up[0]) + wide(got_up[0]) + wide(second_up)
    down_lines = wide(mine_down[0]) + wide(got_down[0]) + wide(second_down)
    lines = jnp.concatenate([up_lines, down_lines], axis=2)
    lines, line_sent = lines[:2], low(lines[2:])
    line_got, last_z = tied(swapped(line_sent, "tp", 1), far_z)
    lines = lines + wide(line_got)
    near_z, last_z = swapped(near_z, "tp", 1), swapped(last_z, "tp", 1)
    grad_tokens = spread_rows([token_rows, near_z, far_z, last_z], jnp.float32)
    line_last = swapped(low(lines[1]), "tp", 2)
    total = low(lines[0] + wide(line_last))
    other_half = swapped(total, "ctx", 1)
    small = wide(total[half:])
    total = wide(
        jnp.concatenate(
            [
                jnp.where(x == 0, total[:half], other_half[:half]),
                jnp.where(x == 0, other_half[:half], total[:half]),
            ]
        )
    )
    grad_w_up = total[:, :hidden]
    grad_w_down = total[:, columns_a:].T
    grad_w_out = total[:, hidden : hidden + width].T
    grad_b_up = small[0, :hidden]
    small_own = small[:, hidden : hidden + shard]

    kept = kept + wide(core(sent))
    kept = low(kept[0] + wide(swapped(low(kept[1]), "fsdp", 2)))
    kept = wide(kept) + wide(swapped(kept, "ctx", 1))

    def unpack(array, part):
        return jnp.concatenate(
            [
                array[:, (3 * head + part) * HEAD_DIM : (3 * head + part + 1) * HEAD_DIM]
                for head in range(heads)
            ],
            axis=1,
        )

    grad_w_query, grad_w_key, grad_w_value = (unpack(kept[:shard], part) for part in range(3))
    grad_b_query, grad_b_value = (unpack(kept[shard : shard + 1], part)[0] for part in (0, 2))
    return (
        output_full,
        grad_tokens,
        grad_w_query,
        grad_w_key,
        grad_w_value,
        grad_b_query,
        grad_b_value,
        grad_w_out,
        small_own[0],
        small_own[1],
        small_own[2],
        grad_w_up,
        grad_b_up,
        grad_w_down,
        small_own[3],
        small_own[4],
        small_own[5],
    )


def rows_path_fits(mesh, tokens, w_query, w_up):
    shape = dict(mesh.shape)
    return (
        shape["ctx"] == 2
        and shape["fsdp"] == 4
        and shape["tp"] == 4
        and tokens.shape[0] == 8
        and tokens.shape[1] % 1024 == 0
        and w_query.shape[0] == w_query.shape[1]
        and w_query.shape[0] % 768 == 0
        and w_up.shape[1] == 4 * w_up.shape[0]
    )


def solution(mesh):
    placed = (
        P("fsdp", "ctx", None),
        P("fsdp"),
        P("fsdp", "ctx", None),
        P("fsdp", "tp"),
        P("fsdp", "tp"),
        P("fsdp", "tp"),
        P("tp"),
        P("tp"),
        P("tp", "fsdp"),
        P("fsdp"),
        P("fsdp"),
        P("fsdp"),
        P("fsdp", "tp"),
        P("tp"),
        P("tp", "fsdp"),
        P("fsdp"),
        P("fsdp"),
        P("fsdp"),
    )
    def split(function):
        return jax.shard_map(
        function,
        mesh=mesh,
        in_specs=placed,
        out_specs=(
            P("fsdp", "ctx", None),
            P("fsdp", "ctx", None),
            P("fsdp", "tp"),
            P("fsdp", "tp"),
            P("fsdp", "tp"),
            P("tp"),
            P("tp"),
            P("tp", "fsdp"),
            P("fsdp"),
            P("fsdp"),
            P("fsdp"),
            P("fsdp", "tp"),
            P("tp"),
            P("tp", "fsdp"),
            P("fsdp"),
            P("fsdp"),
            P("fsdp"),
        ),
        check_vma=False,
    )

    def run(*arrays):
        fits = rows_path_fits(mesh, arrays[0], arrays[3], arrays[12])
        return split(per_device_rows if fits else per_device)(*arrays)

    return run
```

```python
import math

import jax
import jax.numpy as jnp
from jax import lax
from jax.experimental import pallas as pl
from jax.experimental.pallas import tpu as pltpu
from jax.sharding import PartitionSpec as P

HEAD_DIM = 64


epsilon = 1e-12
masked_score = -1e30


def passed_along(value, axis, steps):
    count = lax.axis_size(axis)
    pairs = [(source, (source + steps) % count) for source in range(count)]
    return lax.ppermute(value, axis, pairs)


def layer_norm(inputs, gain_vector, shift_vector):
    center = jnp.mean(inputs, axis=-1, keepdims=True)
    centered = inputs - center
    spread = jnp.mean(centered * centered, axis=-1, keepdims=True)
    return centered * lax.rsqrt(spread + epsilon) * gain_vector + shift_vector


def gelu_exact(inputs):
    return jax.nn.gelu(inputs, approximate=False)


def live_keys(lengths, first_key, key_count):
    places = first_key + lax.iota(jnp.int32, key_count)
    return (places[None, :] < lengths[:, None])[:, None, None, :]


def absorb(carried, queries, key_block, value_block, usable, score_scale):
    row_peak, row_total, summed = carried
    scores = (
        jnp.einsum("sqhe,skhe->shqk", queries, key_block, preferred_element_type=jnp.float32)
        * score_scale
    )
    masked = jnp.where(usable, scores, masked_score)
    new_peak = jnp.maximum(row_peak, jnp.max(masked, axis=-1))
    factor = jnp.exp(row_peak - new_peak)
    weights = jnp.where(usable, jnp.exp(masked - new_peak[..., None]), 0.0)
    row_total = row_total * factor + jnp.sum(weights, axis=-1)
    summed = summed * factor[..., None] + jnp.einsum(
        "shqk,skhe->shqe",
        weights.astype(jnp.bfloat16),
        value_block,
        preferred_element_type=jnp.float32,
    )
    return (new_peak, row_total, summed)


def block_grads(
    queries, grad_att, log_total, row_delta, key_block, value_block, usable, score_scale
):
    scores = (
        jnp.einsum("sqhe,skhe->shqk", queries, key_block, preferred_element_type=jnp.float32)
        * score_scale
    )
    masked = jnp.where(usable, scores, masked_score)
    weights = jnp.where(usable, jnp.exp(masked - log_total[..., None]), 0.0)
    grad_value = jnp.einsum(
        "shqk,sqhe->skhe",
        weights.astype(jnp.bfloat16),
        grad_att,
        preferred_element_type=jnp.float32,
    )
    grad_weights = jnp.einsum(
        "sqhe,skhe->shqk", grad_att, value_block, preferred_element_type=jnp.float32
    )
    grad_scores = (weights * (grad_weights - row_delta[..., None])).astype(jnp.bfloat16)
    grad_query = (
        jnp.einsum("shqk,skhe->sqhe", grad_scores, key_block, preferred_element_type=jnp.float32)
        * score_scale
    )
    grad_key = (
        jnp.einsum("shqk,sqhe->skhe", grad_scores, queries, preferred_element_type=jnp.float32)
        * score_scale
    )
    return (grad_query, grad_key, grad_value)


def per_device(
    tokens,
    lengths,
    cotangent,
    w_query,
    w_key,
    w_value,
    b_query,
    b_value,
    w_out,
    b_out,
    ln1_gain,
    ln1_shift,
    w_up,
    b_up,
    w_down,
    b_down,
    ln2_gain,
    ln2_shift,
):
    sequences, local_rows, model_width = tokens.shape
    token_count = sequences * local_rows
    ctx_count = lax.axis_size("ctx")
    ctx_index = lax.axis_index("ctx")
    (
        query_full,
        key_full,
        value_full,
        out_full,
        up_full,
        down_full,
        bias_out,
        gain_one,
        shift_one,
        bias_down,
        gain_two,
        shift_two,
    ) = (
        lax.all_gather(w_query, "fsdp", axis=0, tiled=True),
        lax.all_gather(w_key, "fsdp", axis=0, tiled=True),
        lax.all_gather(w_value, "fsdp", axis=0, tiled=True),
        lax.all_gather(w_out, "fsdp", axis=1, tiled=True),
        lax.all_gather(w_up, "fsdp", axis=0, tiled=True),
        lax.all_gather(w_down, "fsdp", axis=1, tiled=True),
        lax.all_gather(b_out, "fsdp", axis=0, tiled=True),
        lax.all_gather(ln1_gain, "fsdp", axis=0, tiled=True),
        lax.all_gather(ln1_shift, "fsdp", axis=0, tiled=True),
        lax.all_gather(b_down, "fsdp", axis=0, tiled=True),
        lax.all_gather(ln2_gain, "fsdp", axis=0, tiled=True),
        lax.all_gather(ln2_shift, "fsdp", axis=0, tiled=True),
    )
    flat_tokens = tokens.reshape(token_count, model_width)
    local_width = query_full.shape[1]
    head_count = local_width // HEAD_DIM
    score_scale = HEAD_DIM ** (-0.5)
    query_low = (
        jnp.dot(flat_tokens, query_full, preferred_element_type=jnp.float32)
        + b_query.astype(jnp.float32)
    ).astype(jnp.bfloat16)
    key_low = jnp.dot(flat_tokens, key_full, preferred_element_type=jnp.float32).astype(
        jnp.bfloat16
    )
    value_low = (
        jnp.dot(flat_tokens, value_full, preferred_element_type=jnp.float32)
        + b_value.astype(jnp.float32)
    ).astype(jnp.bfloat16)
    query_heads = query_low.reshape(sequences, local_rows, head_count, HEAD_DIM)
    key_local = key_low.reshape(sequences, local_rows, local_width)
    value_local = value_low.reshape(sequences, local_rows, local_width)
    query_first = ctx_index * local_rows
    start_state = (
        jnp.full((sequences, head_count, local_rows), masked_score, jnp.float32),
        jnp.zeros((sequences, head_count, local_rows), jnp.float32),
        jnp.zeros((sequences, head_count, local_rows, HEAD_DIM), jnp.float32),
    )
    key_part = lax.all_gather(key_local, "ctx", axis=1, tiled=True)
    value_part = lax.all_gather(value_local, "ctx", axis=1, tiled=True)
    key_count = key_part.shape[1]
    block_size = math.gcd(key_count, 512)

    def one_block(position, state_in):
        offset = position * block_size
        key_block = lax.dynamic_slice_in_dim(key_part, offset, block_size, 1).reshape(
            sequences, block_size, head_count, HEAD_DIM
        )
        value_block = lax.dynamic_slice_in_dim(value_part, offset, block_size, 1).reshape(
            sequences, block_size, head_count, HEAD_DIM
        )
        usable = live_keys(lengths, offset, block_size)
        return absorb(state_in, query_heads, key_block, value_block, usable, score_scale)

    row_peak, row_total, summed = lax.fori_loop(0, key_count // block_size, one_block, start_state)
    attended = (summed / row_total[..., None]).transpose(0, 2, 1, 3)
    log_total = row_peak + jnp.log(row_total)
    attended_low = attended.reshape(token_count, local_width).astype(jnp.bfloat16)
    branch = lax.psum(
        jnp.dot(attended_low, out_full, preferred_element_type=jnp.float32).astype(jnp.bfloat16),
        "tp",
    ).astype(jnp.float32) + bias_out.astype(jnp.float32)
    normed_one, norm_one_back = jax.vjp(
        layer_norm,
        flat_tokens.astype(jnp.float32) + branch,
        gain_one.astype(jnp.float32),
        shift_one.astype(jnp.float32),
    )
    normed_low = normed_one.astype(jnp.bfloat16)
    hidden_in = jnp.dot(normed_low, up_full, preferred_element_type=jnp.float32) + b_up.astype(
        jnp.float32
    )
    active, gelu_back = jax.vjp(gelu_exact, hidden_in)
    active_low = active.astype(jnp.bfloat16)
    second = lax.psum(
        jnp.dot(active_low, down_full, preferred_element_type=jnp.float32).astype(jnp.bfloat16),
        "tp",
    ).astype(jnp.float32) + bias_down.astype(jnp.float32)
    output, norm_two_back = jax.vjp(
        layer_norm, normed_one + second, gain_two.astype(jnp.float32), shift_two.astype(jnp.float32)
    )
    positions = query_first + lax.iota(jnp.int32, local_rows)
    row_valid = (positions[None, :] < lengths[:, None]).astype(jnp.float32).reshape(token_count, 1)
    grad_output = cotangent.reshape(token_count, model_width).astype(jnp.float32) * row_valid
    grad_resid_two, grad_gain_two, grad_shift_two = norm_two_back(grad_output)
    grad_second = grad_resid_two.astype(jnp.bfloat16)
    grad_w_down = jnp.einsum(
        "nf,nd->fd", active_low, grad_second, preferred_element_type=jnp.float32
    )
    grad_b_down = jnp.sum(grad_second.astype(jnp.float32), axis=0)
    (grad_hidden,) = gelu_back(
        jnp.einsum("nd,fd->nf", grad_second, down_full, preferred_element_type=jnp.float32)
    )
    grad_hidden_low = grad_hidden.astype(jnp.bfloat16)
    grad_w_up = jnp.einsum(
        "nd,nf->df", normed_low, grad_hidden_low, preferred_element_type=jnp.float32
    )
    grad_b_up = jnp.sum(grad_hidden_low.astype(jnp.float32), axis=0)
    grad_normed = grad_resid_two + lax.psum(
        jnp.einsum(
            "nf,df->nd", grad_hidden_low, up_full, preferred_element_type=jnp.float32
        ).astype(jnp.bfloat16),
        "tp",
    ).astype(jnp.float32)
    grad_resid_one, grad_gain_one, grad_shift_one = norm_one_back(grad_normed)
    grad_branch = grad_resid_one.astype(jnp.bfloat16)
    grad_w_out = jnp.einsum(
        "nc,nd->cd", attended_low, grad_branch, preferred_element_type=jnp.float32
    )
    grad_b_out = jnp.sum(grad_branch.astype(jnp.float32), axis=0)
    grad_att = jnp.einsum(
        "nd,cd->nc", grad_branch, out_full, preferred_element_type=jnp.float32
    ).astype(jnp.bfloat16)
    grad_att_heads = grad_att.reshape(sequences, local_rows, head_count, HEAD_DIM)
    row_delta = jnp.sum(grad_att_heads.astype(jnp.float32) * attended, axis=-1).transpose(0, 2, 1)
    zero_block = jnp.zeros((sequences, local_rows, head_count, HEAD_DIM), jnp.float32)

    def turn_grads(first_key, key_block, value_block):
        usable = live_keys(lengths, first_key, local_rows)
        key_heads = key_block.reshape(sequences, local_rows, head_count, HEAD_DIM)
        value_heads = value_block.reshape(sequences, local_rows, head_count, HEAD_DIM)
        return block_grads(
            query_heads,
            grad_att_heads,
            log_total,
            row_delta,
            key_heads,
            value_heads,
            usable,
            score_scale,
        )

    def cycle_turn(turn_index, carried):
        key_block, value_block, grad_key, grad_value, grad_query = carried
        source = (ctx_index - turn_index) % ctx_count
        added_query, added_key, added_value = turn_grads(
            source * local_rows, key_block, value_block
        )
        key_block, value_block = passed_along((key_block, value_block), "ctx", 1)
        grad_key, grad_value = (
            passed_along((grad_key + added_key).astype(jnp.bfloat16), "ctx", 1).astype(jnp.float32),
            passed_along((grad_value + added_value).astype(jnp.bfloat16), "ctx", 1).astype(
                jnp.float32
            ),
        )
        return (key_block, value_block, grad_key, grad_value, grad_query + added_query)

    cycle_end = lax.fori_loop(
        0, ctx_count, cycle_turn, (key_local, value_local, zero_block, zero_block, zero_block)
    )
    grad_key, grad_value, grad_query = (cycle_end[2], cycle_end[3], cycle_end[4])
    grad_query_low = grad_query.reshape(token_count, local_width).astype(jnp.bfloat16)
    grad_key_low = grad_key.reshape(token_count, local_width).astype(jnp.bfloat16)
    grad_value_low = grad_value.reshape(token_count, local_width).astype(jnp.bfloat16)
    grad_w_query = jnp.einsum(
        "nd,nc->dc", flat_tokens, grad_query_low, preferred_element_type=jnp.float32
    )
    grad_w_key = jnp.einsum(
        "nd,nc->dc", flat_tokens, grad_key_low, preferred_element_type=jnp.float32
    )
    grad_w_value = jnp.einsum(
        "nd,nc->dc", flat_tokens, grad_value_low, preferred_element_type=jnp.float32
    )
    grad_b_query = jnp.sum(grad_query_low.astype(jnp.float32), axis=0)
    grad_b_value = jnp.sum(grad_value_low.astype(jnp.float32), axis=0)
    back_in = (
        jnp.einsum("nc,dc->nd", grad_query_low, query_full, preferred_element_type=jnp.float32)
        + jnp.einsum("nc,dc->nd", grad_key_low, key_full, preferred_element_type=jnp.float32)
        + jnp.einsum("nc,dc->nd", grad_value_low, value_full, preferred_element_type=jnp.float32)
    )
    grad_tokens = grad_resid_one + lax.psum(back_in.astype(jnp.bfloat16), "tp").astype(jnp.float32)
    (
        share_query,
        share_key,
        share_value,
        share_out,
        share_up,
        share_down,
        share_bias_out,
        share_gain_one,
        share_shift_one,
        share_bias_down,
        share_gain_two,
        share_shift_two,
    ) = (
        lax.psum_scatter(
            grad_w_query.astype(jnp.bfloat16), "fsdp", scatter_dimension=0, tiled=True
        ).astype(jnp.float32),
        lax.psum_scatter(
            grad_w_key.astype(jnp.bfloat16), "fsdp", scatter_dimension=0, tiled=True
        ).astype(jnp.float32),
        lax.psum_scatter(
            grad_w_value.astype(jnp.bfloat16), "fsdp", scatter_dimension=0, tiled=True
        ).astype(jnp.float32),
        lax.psum_scatter(
            grad_w_out.astype(jnp.bfloat16), "fsdp", scatter_dimension=1, tiled=True
        ).astype(jnp.float32),
        lax.psum_scatter(
            grad_w_up.astype(jnp.bfloat16), "fsdp", scatter_dimension=0, tiled=True
        ).astype(jnp.float32),
        lax.psum_scatter(
            grad_w_down.astype(jnp.bfloat16), "fsdp", scatter_dimension=1, tiled=True
        ).astype(jnp.float32),
        lax.psum_scatter(
            grad_b_out.astype(jnp.bfloat16), "fsdp", scatter_dimension=0, tiled=True
        ).astype(jnp.float32),
        lax.psum_scatter(
            grad_gain_one.astype(jnp.bfloat16), "fsdp", scatter_dimension=0, tiled=True
        ).astype(jnp.float32),
        lax.psum_scatter(
            grad_shift_one.astype(jnp.bfloat16), "fsdp", scatter_dimension=0, tiled=True
        ).astype(jnp.float32),
        lax.psum_scatter(
            grad_b_down.astype(jnp.bfloat16), "fsdp", scatter_dimension=0, tiled=True
        ).astype(jnp.float32),
        lax.psum_scatter(
            grad_gain_two.astype(jnp.bfloat16), "fsdp", scatter_dimension=0, tiled=True
        ).astype(jnp.float32),
        lax.psum_scatter(
            grad_shift_two.astype(jnp.bfloat16), "fsdp", scatter_dimension=0, tiled=True
        ).astype(jnp.float32),
    )
    (
        share_query,
        share_key,
        share_value,
        share_out,
        share_up,
        share_down,
        share_bias_out,
        share_gain_one,
        share_shift_one,
        share_bias_down,
        share_gain_two,
        share_shift_two,
    ) = (
        lax.psum(share_query.astype(jnp.bfloat16), "ctx").astype(jnp.float32),
        lax.psum(share_key.astype(jnp.bfloat16), "ctx").astype(jnp.float32),
        lax.psum(share_value.astype(jnp.bfloat16), "ctx").astype(jnp.float32),
        lax.psum(share_out.astype(jnp.bfloat16), "ctx").astype(jnp.float32),
        lax.psum(share_up.astype(jnp.bfloat16), "ctx").astype(jnp.float32),
        lax.psum(share_down.astype(jnp.bfloat16), "ctx").astype(jnp.float32),
        lax.psum(share_bias_out.astype(jnp.bfloat16), "ctx").astype(jnp.float32),
        lax.psum(share_gain_one.astype(jnp.bfloat16), "ctx").astype(jnp.float32),
        lax.psum(share_shift_one.astype(jnp.bfloat16), "ctx").astype(jnp.float32),
        lax.psum(share_bias_down.astype(jnp.bfloat16), "ctx").astype(jnp.float32),
        lax.psum(share_gain_two.astype(jnp.bfloat16), "ctx").astype(jnp.float32),
        lax.psum(share_shift_two.astype(jnp.bfloat16), "ctx").astype(jnp.float32),
    )
    total_b_query, total_b_value, total_b_up = lax.psum(
        (grad_b_query, grad_b_value, grad_b_up), ("fsdp", "ctx")
    )
    return (
        output.astype(jnp.bfloat16).reshape(sequences, local_rows, model_width),
        grad_tokens.reshape(sequences, local_rows, model_width),
        share_query,
        share_key,
        share_value,
        total_b_query,
        total_b_value,
        share_out,
        share_bias_out,
        share_gain_one,
        share_shift_one,
        share_up,
        total_b_up,
        share_down,
        share_bias_down,
        share_gain_two,
        share_shift_two,
    )


def swapped(value, axis, bit):
    count = lax.axis_size(axis)
    return lax.ppermute(value, axis, [(place, place ^ bit) for place in range(count)])


def shifted(value, axis, steps):
    count = lax.axis_size(axis)
    return lax.ppermute(value, axis, [(place, (place + steps) % count) for place in range(count)])


def to_owner(value, step, back=False):
    pairs = []
    for x in range(2):
        for z in range(4):
            block = z ^ step
            source = x * 4 + z
            target = (block >> 1) * 4 + (block ^ (2 * x))
            pairs.append((target, source) if back else (source, target))
    return lax.ppermute(value, ("ctx", "tp"), pairs)


ANY = pl.BlockSpec(memory_space=pl.ANY)
WHOLE = pl.BlockSpec(memory_space=pltpu.VMEM)
log2_e = math.log2(math.e)
EXTRA = 8


def low(value):
    return value.astype(jnp.bfloat16)


def wide(value):
    return value.astype(jnp.float32)


def dot32(left, right, left_dim, right_dim):
    return lax.dot_general(
        left, right, (((left_dim,), (right_dim,)), ((), ())), preferred_element_type=jnp.float32
    )


def struct(shape, dtype=jnp.bfloat16):
    return jax.ShapeDtypeStruct(shape, dtype)


def cost(flops, moved, special=0):
    return pl.CostEstimate(flops=int(flops), bytes_accessed=int(moved), transcendentals=int(special))


def stack_kernel(*refs):
    for place, ref in enumerate(refs[:-1]):
        refs[-1][place] = ref[...]


def stacked(pieces):
    shape = (len(pieces),) + pieces[0].shape
    return pl.pallas_call(
        stack_kernel,
        out_shape=struct(shape),
        in_specs=[WHOLE] * len(pieces),
        out_specs=WHOLE,
        cost_estimate=cost(0, 4 * math.prod(shape)),
        name="stack_pieces",
    )(*pieces)


def piece_copies(meta, pieces, taken, columns, target, sems, first):
    x, z, f = meta[0], meta[1], meta[2]
    copies = []
    parts = [(piece, step) for piece in pieces for step in range(piece.shape[0])]
    for index, (piece, step) in enumerate(parts):
        place, slot = index // 4, index % 4
        across = (place % 2, 2 * ((place // 2) % 2) + place // 4)
        start = pl.multiple_of(((f ^ across[1]) * 2 + (x ^ across[0])) * taken, taken)
        copies.append(
            pltpu.make_async_copy(
                piece.at[step, pl.ds(0, taken), columns],
                target.at[z ^ slot, pl.ds(start, taken), :],
                sems.at[first + len(copies)],
            )
        )
    return copies


def attend_kernel(
    meta, own, other, w0, w1, w2, w3, bias, qkv, o0, o1, o2, o3, stats, weight, vectors,
    mask, shards, *, block, heads
):
    step = pl.program_id(0)
    shard = w0.shape[0] - EXTRA
    half = own.shape[1]
    scale = log2_e * HEAD_DIM ** (-0.5)

    @pl.when(step == 0)
    def _():
        for place, piece in enumerate((w0, w1, w2, w3)):
            start = pl.multiple_of((meta[2] ^ place) * shard, shard)
            weight[pl.ds(start, shard), :] = piece[:shard, :]
            shards[meta[2] ^ place] = piece[shard:, :]
        vectors[6:8, :] = jnp.zeros((2, 4 * shard), jnp.float32)
        for place in range(4):
            for row in range(6):
                first = row % 3 * shard
                vectors[row : row + 1, place * shard : (place + 1) * shard] = wide(
                    shards[place, row // 3 : row // 3 + 1, first : first + shard]
                )
        for place, rows in enumerate((own, other)):
            source = rows[0] if place == 0 else rows[...]
            qkv[place * half : (place + 1) * half, :] = low(
                dot32(source, weight[...], 1, 0) + bias[...]
            )
            first = (meta[0] ^ place) * half
            position = first + lax.broadcasted_iota(jnp.int32, (half, block), 0)
            mask[place * half : (place + 1) * half, :] = jnp.where(
                position < meta[3], 0.0, masked_score
            )

    rows = pl.ds(pl.multiple_of((meta[7] ^ step) * block, block), block)
    outs, logs = [], []
    for head in range(heads):
        base = 3 * head * HEAD_DIM
        query = qkv[rows, base : base + HEAD_DIM]
        key = qkv[:, base + HEAD_DIM : base + 2 * HEAD_DIM]
        value = qkv[:, base + 2 * HEAD_DIM : base + 3 * HEAD_DIM]
        scores = dot32(key, query, 1, 1) * scale + mask[...]
        peak = jnp.max(scores, axis=0, keepdims=True)
        weights = jnp.exp2(scores - peak)
        total = jnp.sum(weights, axis=0, keepdims=True)
        outs.append((dot32(value, low(weights), 0, 0) / total).T)
        logs.append(peak + jnp.log2(total))
    result = low(jnp.concatenate(outs, axis=1))
    for place, out in enumerate((o0, o1, o2, o3)):

        @pl.when(step == place)
        def _(out=out):
            out[...] = result

    stats[0] = jnp.concatenate(logs + [jnp.zeros((8 - heads, block), jnp.float32)], axis=0)


def attend_call(meta, tokens, other, pieces, bias, heads):
    half, width = other.shape
    block = half // 2
    columns = pieces[0].shape[1]
    whole = lambda shape: pl.BlockSpec(shape, lambda step, meta: (0,) * len(shape))
    rows = 2 * half
    return pl.pallas_call(
        lambda *refs: attend_kernel(*refs, block=block, heads=heads),
        grid_spec=pltpu.PrefetchScalarGridSpec(
            num_scalar_prefetch=1,
            grid=(4,),
            in_specs=[
                pl.BlockSpec((1, half, width), lambda step, meta: (meta[0], 0, 0)),
                whole((half, width)),
                *[whole(piece.shape) for piece in pieces],
                whole((1, columns)),
            ],
            out_specs=[
                whole((rows, columns)),
                *[whole((block, columns // 3))] * 4,
                pl.BlockSpec((1, 8, block), lambda step, meta: (step, 0, 0)),
                whole((width, columns)),
                whole((EXTRA, width)),
            ],
            scratch_shapes=[
                pltpu.VMEM((rows, block), jnp.float32),
                pltpu.VMEM((4, EXTRA, columns), jnp.bfloat16),
            ],
        ),
        out_shape=[struct((rows, columns))]
        + [struct((block, columns // 3))] * 4
        + [struct((4, 8, block), jnp.float32), struct((width, columns))]
        + [struct((EXTRA, width), jnp.float32)],
        cost_estimate=cost(2 * rows * width * columns + 16 * rows * rows * columns, 8e6, rows * rows * 3),
        name="attend",
    )(meta, tokens, other, *pieces, bias)


def attend_back_kernel(
    meta, qkv, d0, d1, d2, d3, o0, o1, o2, o3, stats, weight, full, p0, p1, p2, p3,
    grads, mask, grad_att, attended, *, block, heads
):
    step = pl.program_id(0)
    rows_all = qkv.shape[0]
    half = rows_all // 2
    scale = log2_e * HEAD_DIM ** (-0.5)

    @pl.when(step == 0)
    def _():
        grads[...] = jnp.zeros_like(grads)
        for place in range(2):
            first = (meta[0] ^ place) * half
            position = first + lax.broadcasted_iota(jnp.int32, (half, block), 0)
            mask[place * half : (place + 1) * half, :] = jnp.where(
                position < meta[3], 0.0, masked_score
            )

    for place, (grad, out) in enumerate(zip((d0, d1, d2, d3), (o0, o1, o2, o3))):

        @pl.when(step == place)
        def _(grad=grad, out=out):
            grad_att[...] = grad[...]
            attended[...] = out[...]

    rows = pl.ds(pl.multiple_of((meta[7] ^ step) * block, block), block)
    for head in range(heads):
        base = 3 * head * HEAD_DIM
        span = slice(head * HEAD_DIM, (head + 1) * HEAD_DIM)
        query = qkv[rows, base : base + HEAD_DIM]
        key = qkv[:, base + HEAD_DIM : base + 2 * HEAD_DIM]
        value = qkv[:, base + 2 * HEAD_DIM : base + 3 * HEAD_DIM]
        grad_out = grad_att[:, span]
        products = wide(grad_out) * wide(attended[:, span])
        delta = lax.dot_general(
            jnp.ones((8, HEAD_DIM), jnp.float32),
            products,
            (((1,), (1,)), ((), ())),
            precision=lax.Precision.HIGHEST,
            preferred_element_type=jnp.float32,
        )[:1]
        scores = dot32(key, query, 1, 1) * scale + mask[...]
        weights = jnp.exp2(scores - stats[0, head : head + 1, :])
        grad_weights = dot32(value, grad_out, 1, 1)
        grad_scores = low(weights * (grad_weights - delta))
        grads[2 * head] += dot32(grad_scores, query, 1, 0)
        grads[2 * head + 1] += dot32(low(weights), grad_out, 1, 0)
        full[rows, base : base + HEAD_DIM] = low(
            dot32(grad_scores, key, 0, 0) * HEAD_DIM ** (-0.5)
        )

    @pl.when(step == 3)
    def _():
        for head in range(heads):
            base = 3 * head * HEAD_DIM
            full[:, base + HEAD_DIM : base + 2 * HEAD_DIM] = low(
                grads[2 * head] * HEAD_DIM ** (-0.5)
            )
            full[:, base + 2 * HEAD_DIM : base + 3 * HEAD_DIM] = low(grads[2 * head + 1])
        for place, part in enumerate((p0, p1, p2, p3)):
            span = pl.ds(pl.multiple_of((meta[7] ^ place) * block, block), block)
            part[...] = low(dot32(full[span, :], weight[...], 1, 1))


def attend_back_call(meta, qkv, grad_parts, parts, stats, weight, heads):
    rows, columns = qkv.shape
    width = weight.shape[0]
    block = rows // 4
    whole = lambda shape: pl.BlockSpec(shape, lambda step, meta: (0,) * len(shape))
    small = whole((block, columns // 3))
    return pl.pallas_call(
        lambda *refs: attend_back_kernel(*refs, block=block, heads=heads),
        grid_spec=pltpu.PrefetchScalarGridSpec(
            num_scalar_prefetch=1,
            grid=(4,),
            in_specs=[whole((rows, columns))]
            + [small] * 8
            + [pl.BlockSpec((1, 8, block), lambda step, meta: (step, 0, 0)), whole(weight.shape)],
            out_specs=[whole((rows, columns))] + [whole((block, width))] * 4,
            scratch_shapes=[
                pltpu.VMEM((2 * heads, rows, HEAD_DIM), jnp.float32),
                pltpu.VMEM((rows, block), jnp.float32),
                pltpu.VMEM((block, columns // 3), jnp.bfloat16),
                pltpu.VMEM((block, columns // 3), jnp.bfloat16),
            ],
        ),
        out_shape=[struct((rows, columns))] + [struct((block, width))] * 4,
        cost_estimate=cost(40 * rows * rows * columns, 8e6, rows * rows * 3),
        name="attend_back",
    )(meta, qkv, *grad_parts, *parts, stats, weight)


def norm_parts(inputs):
    center = jnp.mean(inputs, axis=-1, keepdims=True)
    centered = inputs - center
    spread = jnp.mean(centered * centered, axis=-1, keepdims=True)
    inverse = lax.rsqrt(spread + epsilon)
    return centered * inverse, inverse


def norm_back(grad_out, hat, inverse, gain):
    scaled = grad_out * gain
    return inverse * (
        scaled
        - jnp.mean(scaled, axis=-1, keepdims=True)
        - hat * jnp.mean(scaled * hat, axis=-1, keepdims=True)
    )


BIAS_OUT, GAIN_ONE, SHIFT_ONE, BIAS_DOWN, GAIN_TWO, SHIFT_TWO = range(6)


def first_kernel(meta, *refs, width):
    att, tok, vectors, lines, pieces = refs[:4], refs[4], refs[5], refs[6], refs[7:15]
    hat, inverse, both, slope, out_w, up_w, sems = refs[15:]
    hidden = up_w.shape[2]
    taken = pieces[0].shape[1]
    copies = piece_copies(meta, pieces, taken, pl.ds(hidden, out_w.shape[2]), out_w, sems, 0)
    up_copies = piece_copies(meta, pieces, taken, pl.ds(0, hidden), up_w, sems, 32)
    for copy in copies + up_copies:
        copy.start()
    for step in range(4):
        both[step, :, hidden : hidden + width] = att[step][...]
        both[step, :, hidden + width :] = jnp.zeros_like(both[step, :, hidden + width :])
    for copy in copies:
        copy.wait()
    branch = vectors[BIAS_OUT : BIAS_OUT + 1, :]
    for step in range(4):
        branch = branch + dot32(att[step][...], out_w[meta[4] ^ step][:, :width], 1, 1)
    hat_one, inverse_one = norm_parts(wide(tok[0]) + branch)
    hat[...] = hat_one
    inverse[...] = inverse_one
    normed = low(hat_one * vectors[GAIN_ONE : GAIN_ONE + 1, :] + vectors[SHIFT_ONE : SHIFT_ONE + 1, :])
    for copy in up_copies:
        copy.wait()
    for place in range(4):
        inputs = dot32(normed, up_w[place], 1, 0) + wide(lines[meta[1] ^ place, 0:1, :])
        cumulative = 0.5 * (1.0 + lax.erf(inputs * (0.5**0.5)))
        density = jnp.exp(-0.5 * inputs * inputs) * ((0.5 / math.pi) ** 0.5)
        both[place, :, :hidden] = low(inputs * cumulative)
        slope[place] = low(cumulative + inputs * density)


def second_kernel(meta, *refs, width):
    hat, inverse, both, slope, cot, vectors = refs[:6]
    pieces_a, pieces_b = refs[6:14], refs[14:24]
    output, resid, g0, g1, g2, g3, mixed, keep = refs[24:32]
    out_w, up_w, down_w, blocks, small, small_blocks, sems = refs[32:]
    rows, model = hat.shape
    hidden = up_w.shape[2]
    taken = pieces_a[0].shape[1]
    down_copies = piece_copies(meta, pieces_b, taken, pl.ds(0, hidden), down_w, sems, 0)
    copies = piece_copies(meta, pieces_a, taken, pl.ds(0, hidden), up_w, sems, 32)
    copies += piece_copies(meta, pieces_a, taken, pl.ds(hidden, out_w.shape[2]), out_w, sems, 64)
    for copy in down_copies + copies:
        copy.start()
    row = lambda place: vectors[place : place + 1, :]
    hat_one, inverse_one = hat[...], inverse[...]
    normed_one = hat_one * row(GAIN_ONE) + row(SHIFT_ONE)
    for copy in down_copies:
        copy.wait()
    second = row(BIAS_DOWN)
    for place in range(4):
        second = second + dot32(both[place, :, :hidden], down_w[place], 1, 1)
    hat_two, inverse_two = norm_parts(normed_one + second)
    output[...] = low(hat_two * row(GAIN_TWO) + row(SHIFT_TWO))
    position = meta[4] * rows + lax.broadcasted_iota(jnp.int32, (rows, model), 0)
    grad_output = jnp.where(position < meta[8], wide(cot[0]), 0.0)
    grad_two = norm_back(grad_output, hat_two, inverse_two, row(GAIN_TWO))
    grad_second = low(grad_two)
    for copy in copies:
        copy.wait()
    grad_normed = grad_two
    sums = lambda array: jnp.sum(array, axis=0, keepdims=True)
    for place in range(4):
        grad_hidden = low(dot32(grad_second, down_w[place], 1, 0) * wide(slope[place]))
        mixed[place, :rows, :] = grad_hidden
        mixed[place, rows:, :] = low(
            jnp.broadcast_to(sums(wide(grad_hidden)), (EXTRA, hidden))
        )
        grad_normed = grad_normed + dot32(grad_hidden, up_w[place], 1, 1)
    grad_one = norm_back(grad_normed, hat_one, inverse_one, row(GAIN_ONE))
    resid[...] = grad_one
    grad_branch = low(grad_one)
    for step, out in enumerate((g0, g1, g2, g3)):
        out[...] = low(dot32(grad_branch, out_w[meta[4] ^ step][:, :width], 1, 0))
    small[0:1, :] = sums(wide(grad_branch))
    small[1:2, :] = sums(grad_normed * hat_one)
    small[2:3, :] = sums(grad_normed)
    small[3:4, :] = sums(wide(grad_second))
    small[4:5, :] = sums(grad_output * hat_two)
    small[5:6, :] = sums(grad_output)
    small[6:8, :] = jnp.zeros((2, model), jnp.float32)
    shard = model // 4
    for place in range(4):
        small_blocks[place] = low(small[:, place * shard : (place + 1) * shard])
    for kind, array in enumerate((grad_second, low(normed_one), grad_branch)):
        for place in range(4):
            blocks[place] = array[:, place * shard : (place + 1) * shard]
        for far in range(2):
            keep[kind, far, :rows, :] = blocks[meta[2] ^ (2 * far)]
            keep[kind, far, rows:, :] = small_blocks[meta[2] ^ (2 * far)]
            columns = slice(kind * shard, (kind + 1) * shard)
            mixed[4 + far, :rows, columns] = blocks[meta[2] ^ (2 * far + 1)]
            mixed[4 + far, rows:, columns] = small_blocks[meta[2] ^ (2 * far + 1)]
    for far in range(2):
        mixed[4 + far, :, 3 * shard :] = jnp.zeros((rows + EXTRA, hidden - 3 * shard), jnp.bfloat16)


def slot_of(block, z):
    apart = block ^ z
    return 2 * (apart & 1) + (apart >> 1)


def weights_kernel(meta, *refs):
    keep, tail_sib, both, both_sib, att, att_sib, mixed, mixed_sib = refs[:8]
    near_up, far_up, mine_down, theirs_down, turned, ordered = refs[8:]
    shard = keep.shape[3]
    rows = both.shape[1]
    half = shard // 2
    hidden, padded = mixed.shape[2], att.shape[2]
    starts = [pl.multiple_of(side * half, half) for side in (meta[0], 1 - meta[0])]

    @pl.when(pl.program_id(0) == 0)
    def _():
        for kind in range(3):
            for far in range(2):
                span = slice(far * shard, (far + 1) * shard)
                turned[span, :rows] = keep[kind, far, :rows, :].T
                turned[span, rows:] = tail_sib[far, :rows, kind * shard : (kind + 1) * shard].T
                for side, start in enumerate(starts):
                    first = (2 * far + side) * half
                    ordered[kind, first : first + half, :] = turned[
                        pl.ds(far * shard + start, half), :
                    ]

    operands = (
        (both[0], both_sib[0]),
        (mixed[0, :rows, :], mixed_sib[0, :rows, :]),
        (att[0], att_sib[0]),
    )
    for kind, (left, right) in enumerate(operands):
        value = dot32(ordered[kind, :, :rows], left, 1, 0)
        value = value + dot32(ordered[kind, :, rows:], right, 1, 0)
        for far in range(2):
            for side in range(2):
                first = (2 * far + side) * half
                part = low(value[first : first + half, :])
                up = (near_up, far_up)[far]
                if kind == 0:
                    split = hidden - mine_down.shape[3]
                    (mine_down, theirs_down)[side][far, 0, :half, :] = part[:, split:]
                    up[side, 0, :half, hidden + padded :] = part[:, :split]
                elif kind == 1:
                    up[side, 0, :half, :hidden] = part
                else:
                    up[side, 0, :half, hidden : hidden + padded] = part
    hidden_sums = low(wide(mixed[0, rows:, :]) + wide(mixed_sib[0, rows:, :]))
    for far in range(2):
        vector_sums = low(wide(keep[0, far, rows:, :]) + wide(tail_sib[far, rows:, :shard]))
        for side in range(2):
            out = (mine_down, theirs_down)[side]
            out[far, 0, half:, :] = jnp.zeros((EXTRA, out.shape[3]), jnp.bfloat16)
            out = (near_up, far_up)[far]
            out[side, 0, half:, :hidden] = hidden_sums
            out[side, 0, half:, hidden : hidden + shard] = vector_sums
            rest = slice(hidden + shard, None)
            out[side, 0, half:, rest] = jnp.zeros_like(out[side, 0, half:, rest])


def projections_kernel(meta, own, other, grads, kept, sent, whole):
    half, shard = other.shape[0], other.shape[1] // 4
    count = grads.shape[1]
    whole[...] = dot32(own[0], grads[:half, :], 0, 0) + dot32(other[...], grads[half:, :], 0, 0)
    sums = jnp.broadcast_to(jnp.sum(wide(grads[...]), axis=0, keepdims=True), (EXTRA, count))
    for far in range(2):
        for out, place in ((kept, meta[2] ^ (2 * far)), (sent, meta[2] ^ (2 * far + 1))):
            value = whole[pl.ds(pl.multiple_of(place * shard, shard), shard), :]
            out[far, :shard, :count] = value.astype(out.dtype)
            out[far, shard:, :count] = sums.astype(out.dtype)
            out[far, :, count:] = jnp.zeros_like(out[far, :, count:])


def per_device_rows(
    tokens,
    lengths,
    cotangent,
    w_query,
    w_key,
    w_value,
    b_query,
    b_value,
    w_out,
    b_out,
    ln1_gain,
    ln1_shift,
    w_up,
    b_up,
    w_down,
    b_down,
    ln2_gain,
    ln2_shift,
):
    sequences, local_rows, model = tokens.shape
    x, f, z = lax.axis_index("ctx"), lax.axis_index("fsdp"), lax.axis_index("tp")
    rows = local_rows // 2
    width = w_query.shape[1]
    heads = width // HEAD_DIM
    hidden = w_up.shape[1]
    shard = w_query.shape[0]
    half = shard // 2
    padded = -(-width // 128) * 128
    own_seq, own_place = (z // 2) ^ x, z % 2
    quarter = 2 * x + own_place
    length_of = lambda place: lax.dynamic_index_in_dim(lengths, place, 0, keepdims=False)
    entries = (x, z, f, length_of(x), quarter, own_seq, own_place, z ^ (2 * x), length_of(own_seq))
    places = lax.iota(jnp.int32, len(entries))
    meta = sum(jnp.where(places == place, entry, 0) for place, entry in enumerate(entries))
    meta = meta.astype(jnp.int32)
    tied = lambda *values: lax.optimization_barrier(values)

    take_half = lambda pack: lax.dynamic_slice_in_dim(pack, x * half, half, 0)
    wider = lambda array, columns: jnp.pad(array, ((0, 0), (0, columns - array.shape[1])))
    columns_a = hidden + padded
    half_a = wider(take_half(jnp.concatenate([w_up, w_out.T], axis=1)), columns_a)
    half_b = jnp.concatenate(
        [take_half(w_down.T), b_up[None], jnp.zeros((EXTRA - 1, hidden), jnp.bfloat16)]
    )

    other = lax.dynamic_index_in_dim(tokens, 1 - x, 0, keepdims=False)
    other, half_a = tied(other, half_a)
    other = swapped(other, "ctx", 1)
    far_a, near_half = swapped(half_a, "tp", 2), swapped(half_a, "tp", 1)
    per_head = lambda weights: jnp.concatenate(
        [
            weight[..., head * HEAD_DIM : (head + 1) * HEAD_DIM]
            for head in range(heads)
            for weight in weights
        ],
        axis=-1,
    )
    vectors = jnp.concatenate([b_out, ln1_gain, ln1_shift, b_down, ln2_gain, ln2_shift])
    qkv_shard = jnp.concatenate(
        [
            per_head((w_query, w_key, w_value)),
            jnp.pad(vectors.reshape(2, 3 * width), ((0, EXTRA - 2), (0, 0))),
        ]
    )
    qkv_bias = wide(per_head((b_query, jnp.zeros_like(b_query), b_value)))[None, :]
    far_a, meta = tied(far_a, meta)
    last_a, qkv_y = tied(swapped(far_a, "tp", 1), swapped(qkv_shard, "fsdp", 2))
    line_a = stacked([half_a, near_half, far_a, last_a])
    qkv_pieces = (qkv_shard, swapped(qkv_shard, "fsdp", 1), qkv_y, swapped(qkv_y, "fsdp", 1))

    core = lambda array: swapped(array, "fsdp", 1)
    meta, qkv_bias, other, line_a, half_b, *qkv_pieces = tied(
        meta, qkv_bias, other, line_a, half_b, *qkv_pieces
    )
    x_a, y_a = swapped(line_a, "ctx", 1), swapped(line_a, "fsdp", 2)
    qkv, *parts, stats, weight, vectors = attend_call(
        meta, tokens, other, qkv_pieces, qkv_bias, heads
    )
    b_pieces = [swapped(half_b, "tp", bit) for bit in (1, 2, 3)]

    x_a, y_a, line_a, *rest = tied(x_a, y_a, line_a, *b_pieces, *parts)
    b_pieces, parts = rest[:3], rest[3:]
    line_b = stacked([half_b, *b_pieces])
    att = [to_owner(part, step) for step, part in enumerate(parts)]
    x_y_a = swapped(x_a, "fsdp", 2)
    x_y_a, x_a, y_a, line_a, line_b, *att = tied(x_y_a, x_a, y_a, line_a, line_b, *att)
    near_a = (line_a, x_a, y_a, x_y_a)
    pieces_a = (*near_a, *map(core, near_a))
    x_b, y_b, line_core = swapped(line_b, "ctx", 1), swapped(line_b, "fsdp", 2), core(line_b)

    def row_spec(array):
        return pl.BlockSpec((1, rows, model), lambda step, meta: (meta[5], meta[6], 0))

    vm = lambda shape, dtype=jnp.bfloat16: pltpu.VMEM(shape, dtype)
    weights_scratch = [vm((4, model, padded)), vm((4, model, hidden))]
    grid = lambda inputs, outputs, scratch: pltpu.PrefetchScalarGridSpec(
        num_scalar_prefetch=1, grid=(1,), in_specs=inputs, out_specs=outputs, scratch_shapes=scratch
    )
    full = lambda shape: pl.BlockSpec(shape, lambda step, meta: (0,) * len(shape))
    specs = lambda shapes: [full(item.shape) for item in shapes]

    first_out = [
        struct((rows, model), jnp.float32),
        struct((rows, 1), jnp.float32),
        struct((4, rows, columns_a)),
        struct((4, rows, hidden)),
    ]
    hat, inverse, both, slope = pl.pallas_call(
        lambda *refs: first_kernel(*refs, width=width),
        grid_spec=grid(
            [full((rows, width))] * 4
            + [row_spec(tokens), full((EXTRA, model))]
            + [pl.BlockSpec((4, EXTRA, hidden), lambda step, meta: (0, half // EXTRA, 0))]
            + [ANY] * 8,
            specs(first_out),
            weights_scratch + [pltpu.SemaphoreType.DMA((64,))],
        ),
        out_shape=first_out,
        cost_estimate=cost(2 * rows * model * (model + 4 * hidden), 12e6, rows * hidden * 8),
        name="feed_first",
    )(meta, *att, tokens, vectors, line_b, *pieces_a)

    both, x_b, y_b, line_b, line_core = tied(both, x_b, y_b, line_b, line_core)
    x_y_b = [swapped(x_b[:2], "fsdp", 2), swapped(y_b[2:], "ctx", 1)]
    *x_y_b, x_core, y_core, both_sib = tied(*x_y_b, core(x_b), core(y_b), core(both))
    pieces_b = (line_b, x_b, y_b, *x_y_b, line_core, x_core, y_core, *map(core, x_y_b))

    second_out = [
        struct((rows, model)),
        struct((rows, model), jnp.float32),
        *[struct((rows, width))] * 4,
        struct((6, rows + EXTRA, hidden)),
        struct((3, 2, rows + EXTRA, shard)),
    ]
    output, resid, g0, g1, g2, g3, mixed, keep = pl.pallas_call(
        lambda *refs: second_kernel(*refs, width=width),
        grid_spec=grid(
            [full(item.shape) for item in (hat, inverse, both, slope)]
            + [row_spec(cotangent), full((EXTRA, model))]
            + [ANY] * 18,
            specs(second_out),
            weights_scratch
            + [
                vm((4, model, hidden)),
                vm((4, rows, shard)),
                vm((EXTRA, model), jnp.float32),
                vm((4, EXTRA, shard)),
                pltpu.SemaphoreType.DMA((96,)),
            ],
        ),
        out_shape=second_out,
        cost_estimate=cost(2 * rows * model * (model + 12 * hidden), 20e6),
        name="feed_second",
    )(meta, hat, inverse, both, slope, cotangent, vectors, *pieces_a, *pieces_b)

    grad_att = [to_owner(part, step, True) for step, part in enumerate((g0, g1, g2, g3))]

    first_x = 2 * padded
    pack = struct((2, 4, half + EXTRA, first_x))
    pack_up = struct((2, 4, half + EXTRA, columns_a + hidden - first_x))
    mixed_sib = core(mixed)
    per_block = lambda item, place=lambda block, meta: block, columns=None, lanes=0: pl.BlockSpec(
        (1, item.shape[1], columns or item.shape[2]),
        lambda block, meta: (place(block, meta), 0, lanes),
    )
    heads_of = lambda block, meta: block ^ meta[4]
    sent_block = lambda item: pl.BlockSpec(
        (2, 1) + item.shape[2:], lambda block, meta: (0, slot_of(block, meta[1]), 0, 0)
    )
    near_up, far_up, mine_down, theirs_down = pl.pallas_call(
        weights_kernel,
        grid_spec=pltpu.PrefetchScalarGridSpec(
            num_scalar_prefetch=1,
            grid=(4,),
            in_specs=[
                full(keep.shape),
                pl.BlockSpec((2,) + mixed.shape[1:], lambda block, meta: (2, 0, 0)),
                *[per_block(both, columns=hidden)] * 2,
                *[per_block(both, heads_of, padded, hidden // padded)] * 2,
                *[per_block(mixed)] * 2,
            ],
            out_specs=[sent_block(pack_up)] * 2 + [sent_block(pack)] * 2,
            scratch_shapes=[vm((2 * shard, 2 * rows)), vm((3, 2 * shard, 2 * rows))],
        ),
        out_shape=[pack_up] * 2 + [pack] * 2,
        cost_estimate=cost(8 * rows * shard * (8 * hidden + 4 * width), 20e6),
        name="feed_weights",
    )(meta, keep, mixed_sib, both, both_sib, both, both_sib, mixed, mixed_sib)

    near_out = swapped(output, "tp", 1)
    far_up, theirs_down, output, *grad_att = tied(far_up, theirs_down, output, *grad_att)
    got_up, got_down = swapped(far_up, "fsdp", 2), swapped(theirs_down, "ctx", 1)
    far_out = swapped(output, "tp", 2)
    grad_full, *grad_parts = attend_back_call(meta, qkv, grad_att, parts, stats, weight, heads)

    got_down, near_out, far_out, *grad_parts = tied(got_down, near_out, far_out, *grad_parts)
    grad_rows = [to_owner(part, step) for step, part in enumerate(grad_parts)]
    far_out, up_sent, down_sent, grad_full, *grad_rows = tied(
        far_out,
        low(wide(near_up[1]) + wide(got_up[1])),
        low(wide(mine_down[1]) + wide(got_down[1])),
        grad_full,
        *grad_rows,
    )
    kept, sent = pl.pallas_call(
        projections_kernel,
        grid_spec=grid(
            [pl.BlockSpec((1, local_rows, model), lambda step, meta: (meta[0], 0, 0))]
            + [full((local_rows, model)), full(grad_full.shape)],
            [full((2, shard + EXTRA, 640 * width // 192))] * 2,
            [vm((model, 3 * width), jnp.float32)],
        ),
        out_shape=[
            struct((2, shard + EXTRA, 640 * width // 192), dtype) for dtype in (jnp.float32, jnp.bfloat16)
        ],
        cost_estimate=cost(12 * local_rows * model * width, 8e6),
        name="projection_weights",
    )(meta, tokens, other, grad_full)
    second_up, second_down = swapped(up_sent, "ctx", 1), swapped(down_sent, "fsdp", 2)
    def spread_rows(pieces, dtype):
        blocks = [
            lax.select_n(z ^ (2 * x), *[pieces[block ^ place] for place in range(4)]).astype(dtype)
            for block in range(4)
        ]
        return jnp.stack([jnp.concatenate(blocks[2 * seq : 2 * seq + 2]) for seq in range(2)])

    token_rows = resid
    for part in grad_rows:
        token_rows = token_rows + wide(part)

    token_rows = low(token_rows)
    far_z, last_out, near_z, sent, second_up, second_down = tied(
        swapped(token_rows, "tp", 2),
        swapped(far_out, "tp", 1),
        token_rows,
        sent,
        second_up,
        second_down,
    )
    output_full = spread_rows([output, near_out, far_out, last_out], jnp.bfloat16)
    up_lines = wide(near_up[0]) + wide(got_up[0]) + wide(second_up)
    down_lines = wide(mine_down[0]) + wide(got_down[0]) + wide(second_down)
    lines = jnp.concatenate([up_lines, down_lines], axis=2)
    lines, line_sent = lines[:2], low(lines[2:])
    line_got, last_z = tied(swapped(line_sent, "tp", 1), far_z)
    lines = lines + wide(line_got)
    near_z, last_z = swapped(near_z, "tp", 1), swapped(last_z, "tp", 1)
    grad_tokens = spread_rows([token_rows, near_z, far_z, last_z], jnp.float32)
    line_last = swapped(low(lines[1]), "tp", 2)
    total = low(lines[0] + wide(line_last))
    other_half = swapped(total, "ctx", 1)
    small = wide(total[half:])
    total = wide(
        jnp.concatenate(
            [
                jnp.where(x == 0, total[:half], other_half[:half]),
                jnp.where(x == 0, other_half[:half], total[:half]),
            ]
        )
    )
    grad_w_up = total[:, :hidden]
    grad_w_down = total[:, columns_a:].T
    grad_w_out = total[:, hidden : hidden + width].T
    grad_b_up = small[0, :hidden]
    small_own = small[:, hidden : hidden + shard]

    kept = kept + wide(core(sent))
    kept = low(kept[0] + wide(swapped(low(kept[1]), "fsdp", 2)))
    kept = wide(kept) + wide(swapped(kept, "ctx", 1))

    def unpack(array, part):
        return jnp.concatenate(
            [
                array[:, (3 * head + part) * HEAD_DIM : (3 * head + part + 1) * HEAD_DIM]
                for head in range(heads)
            ],
            axis=1,
        )

    grad_w_query, grad_w_key, grad_w_value = (unpack(kept[:shard], part) for part in range(3))
    grad_b_query, grad_b_value = (unpack(kept[shard : shard + 1], part)[0] for part in (0, 2))
    return (
        output_full,
        grad_tokens,
        grad_w_query,
        grad_w_key,
        grad_w_value,
        grad_b_query,
        grad_b_value,
        grad_w_out,
        small_own[0],
        small_own[1],
        small_own[2],
        grad_w_up,
        grad_b_up,
        grad_w_down,
        small_own[3],
        small_own[4],
        small_own[5],
    )


def rows_path_fits(mesh, tokens, w_query, w_up):
    shape = dict(mesh.shape)
    return (
        shape["ctx"] == 2
        and shape["fsdp"] == 4
        and shape["tp"] == 4
        and tokens.shape[0] == 8
        and tokens.shape[1] % 1024 == 0
        and w_query.shape[0] == w_query.shape[1]
        and w_query.shape[0] % 768 == 0
        and w_up.shape[1] == 4 * w_up.shape[0]
    )


def solution(mesh):
    placed = (
        P("fsdp", "ctx", None),
        P("fsdp"),
        P("fsdp", "ctx", None),
        P("fsdp", "tp"),
        P("fsdp", "tp"),
        P("fsdp", "tp"),
        P("tp"),
        P("tp"),
        P("tp", "fsdp"),
        P("fsdp"),
        P("fsdp"),
        P("fsdp"),
        P("fsdp", "tp"),
        P("tp"),
        P("tp", "fsdp"),
        P("fsdp"),
        P("fsdp"),
        P("fsdp"),
    )
    def split(function):
        return jax.shard_map(
        function,
        mesh=mesh,
        in_specs=placed,
        out_specs=(
            P("fsdp", "ctx", None),
            P("fsdp", "ctx", None),
            P("fsdp", "tp"),
            P("fsdp", "tp"),
            P("fsdp", "tp"),
            P("tp"),
            P("tp"),
            P("tp", "fsdp"),
            P("fsdp"),
            P("fsdp"),
            P("fsdp"),
            P("fsdp", "tp"),
            P("tp"),
            P("tp", "fsdp"),
            P("fsdp"),
            P("fsdp"),
            P("fsdp"),
        ),
        check_vma=False,
    )

    def run(*arrays):
        fits = rows_path_fits(mesh, arrays[0], arrays[3], arrays[12])
        return split(per_device_rows if fits else per_device)(*arrays)

    return run
```

```python
import math

import jax
import jax.numpy as jnp
from jax import lax
from jax.experimental import pallas as pl
from jax.experimental.pallas import tpu as pltpu
from jax.sharding import PartitionSpec as P

HEAD_DIM = 64


epsilon = 1e-12
masked_score = -1e30


def passed_along(value, axis, steps):
    count = lax.axis_size(axis)
    pairs = [(source, (source + steps) % count) for source in range(count)]
    return lax.ppermute(value, axis, pairs)


def layer_norm(inputs, gain_vector, shift_vector):
    center = jnp.mean(inputs, axis=-1, keepdims=True)
    centered = inputs - center
    spread = jnp.mean(centered * centered, axis=-1, keepdims=True)
    return centered * lax.rsqrt(spread + epsilon) * gain_vector + shift_vector


def gelu_exact(inputs):
    return jax.nn.gelu(inputs, approximate=False)


def live_keys(lengths, first_key, key_count):
    places = first_key + lax.iota(jnp.int32, key_count)
    return (places[None, :] < lengths[:, None])[:, None, None, :]


def absorb(carried, queries, key_block, value_block, usable, score_scale):
    row_peak, row_total, summed = carried
    scores = (
        jnp.einsum("sqhe,skhe->shqk", queries, key_block, preferred_element_type=jnp.float32)
        * score_scale
    )
    masked = jnp.where(usable, scores, masked_score)
    new_peak = jnp.maximum(row_peak, jnp.max(masked, axis=-1))
    factor = jnp.exp(row_peak - new_peak)
    weights = jnp.where(usable, jnp.exp(masked - new_peak[..., None]), 0.0)
    row_total = row_total * factor + jnp.sum(weights, axis=-1)
    summed = summed * factor[..., None] + jnp.einsum(
        "shqk,skhe->shqe",
        weights.astype(jnp.bfloat16),
        value_block,
        preferred_element_type=jnp.float32,
    )
    return (new_peak, row_total, summed)


def block_grads(
    queries, grad_att, log_total, row_delta, key_block, value_block, usable, score_scale
):
    scores = (
        jnp.einsum("sqhe,skhe->shqk", queries, key_block, preferred_element_type=jnp.float32)
        * score_scale
    )
    masked = jnp.where(usable, scores, masked_score)
    weights = jnp.where(usable, jnp.exp(masked - log_total[..., None]), 0.0)
    grad_value = jnp.einsum(
        "shqk,sqhe->skhe",
        weights.astype(jnp.bfloat16),
        grad_att,
        preferred_element_type=jnp.float32,
    )
    grad_weights = jnp.einsum(
        "sqhe,skhe->shqk", grad_att, value_block, preferred_element_type=jnp.float32
    )
    grad_scores = (weights * (grad_weights - row_delta[..., None])).astype(jnp.bfloat16)
    grad_query = (
        jnp.einsum("shqk,skhe->sqhe", grad_scores, key_block, preferred_element_type=jnp.float32)
        * score_scale
    )
    grad_key = (
        jnp.einsum("shqk,sqhe->skhe", grad_scores, queries, preferred_element_type=jnp.float32)
        * score_scale
    )
    return (grad_query, grad_key, grad_value)


def per_device(
    tokens,
    lengths,
    cotangent,
    w_query,
    w_key,
    w_value,
    b_query,
    b_value,
    w_out,
    b_out,
    ln1_gain,
    ln1_shift,
    w_up,
    b_up,
    w_down,
    b_down,
    ln2_gain,
    ln2_shift,
):
    sequences, local_rows, model_width = tokens.shape
    token_count = sequences * local_rows
    ctx_count = lax.axis_size("ctx")
    ctx_index = lax.axis_index("ctx")
    (
        query_full,
        key_full,
        value_full,
        out_full,
        up_full,
        down_full,
        bias_out,
        gain_one,
        shift_one,
        bias_down,
        gain_two,
        shift_two,
    ) = (
        lax.all_gather(w_query, "fsdp", axis=0, tiled=True),
        lax.all_gather(w_key, "fsdp", axis=0, tiled=True),
        lax.all_gather(w_value, "fsdp", axis=0, tiled=True),
        lax.all_gather(w_out, "fsdp", axis=1, tiled=True),
        lax.all_gather(w_up, "fsdp", axis=0, tiled=True),
        lax.all_gather(w_down, "fsdp", axis=1, tiled=True),
        lax.all_gather(b_out, "fsdp", axis=0, tiled=True),
        lax.all_gather(ln1_gain, "fsdp", axis=0, tiled=True),
        lax.all_gather(ln1_shift, "fsdp", axis=0, tiled=True),
        lax.all_gather(b_down, "fsdp", axis=0, tiled=True),
        lax.all_gather(ln2_gain, "fsdp", axis=0, tiled=True),
        lax.all_gather(ln2_shift, "fsdp", axis=0, tiled=True),
    )
    flat_tokens = tokens.reshape(token_count, model_width)
    local_width = query_full.shape[1]
    head_count = local_width // HEAD_DIM
    score_scale = HEAD_DIM ** (-0.5)
    query_low = (
        jnp.dot(flat_tokens, query_full, preferred_element_type=jnp.float32)
        + b_query.astype(jnp.float32)
    ).astype(jnp.bfloat16)
    key_low = jnp.dot(flat_tokens, key_full, preferred_element_type=jnp.float32).astype(
        jnp.bfloat16
    )
    value_low = (
        jnp.dot(flat_tokens, value_full, preferred_element_type=jnp.float32)
        + b_value.astype(jnp.float32)
    ).astype(jnp.bfloat16)
    query_heads = query_low.reshape(sequences, local_rows, head_count, HEAD_DIM)
    key_local = key_low.reshape(sequences, local_rows, local_width)
    value_local = value_low.reshape(sequences, local_rows, local_width)
    query_first = ctx_index * local_rows
    start_state = (
        jnp.full((sequences, head_count, local_rows), masked_score, jnp.float32),
        jnp.zeros((sequences, head_count, local_rows), jnp.float32),
        jnp.zeros((sequences, head_count, local_rows, HEAD_DIM), jnp.float32),
    )
    key_part = lax.all_gather(key_local, "ctx", axis=1, tiled=True)
    value_part = lax.all_gather(value_local, "ctx", axis=1, tiled=True)
    key_count = key_part.shape[1]
    block_size = math.gcd(key_count, 512)

    def one_block(position, state_in):
        offset = position * block_size
        key_block = lax.dynamic_slice_in_dim(key_part, offset, block_size, 1).reshape(
            sequences, block_size, head_count, HEAD_DIM
        )
        value_block = lax.dynamic_slice_in_dim(value_part, offset, block_size, 1).reshape(
            sequences, block_size, head_count, HEAD_DIM
        )
        usable = live_keys(lengths, offset, block_size)
        return absorb(state_in, query_heads, key_block, value_block, usable, score_scale)

    row_peak, row_total, summed = lax.fori_loop(0, key_count // block_size, one_block, start_state)
    attended = (summed / row_total[..., None]).transpose(0, 2, 1, 3)
    log_total = row_peak + jnp.log(row_total)
    attended_low = attended.reshape(token_count, local_width).astype(jnp.bfloat16)
    branch = lax.psum(
        jnp.dot(attended_low, out_full, preferred_element_type=jnp.float32).astype(jnp.bfloat16),
        "tp",
    ).astype(jnp.float32) + bias_out.astype(jnp.float32)
    normed_one, norm_one_back = jax.vjp(
        layer_norm,
        flat_tokens.astype(jnp.float32) + branch,
        gain_one.astype(jnp.float32),
        shift_one.astype(jnp.float32),
    )
    normed_low = normed_one.astype(jnp.bfloat16)
    hidden_in = jnp.dot(normed_low, up_full, preferred_element_type=jnp.float32) + b_up.astype(
        jnp.float32
    )
    active, gelu_back = jax.vjp(gelu_exact, hidden_in)
    active_low = active.astype(jnp.bfloat16)
    second = lax.psum(
        jnp.dot(active_low, down_full, preferred_element_type=jnp.float32).astype(jnp.bfloat16),
        "tp",
    ).astype(jnp.float32) + bias_down.astype(jnp.float32)
    output, norm_two_back = jax.vjp(
        layer_norm, normed_one + second, gain_two.astype(jnp.float32), shift_two.astype(jnp.float32)
    )
    positions = query_first + lax.iota(jnp.int32, local_rows)
    row_valid = (positions[None, :] < lengths[:, None]).astype(jnp.float32).reshape(token_count, 1)
    grad_output = cotangent.reshape(token_count, model_width).astype(jnp.float32) * row_valid
    grad_resid_two, grad_gain_two, grad_shift_two = norm_two_back(grad_output)
    grad_second = grad_resid_two.astype(jnp.bfloat16)
    grad_w_down = jnp.einsum(
        "nf,nd->fd", active_low, grad_second, preferred_element_type=jnp.float32
    )
    grad_b_down = jnp.sum(grad_second.astype(jnp.float32), axis=0)
    (grad_hidden,) = gelu_back(
        jnp.einsum("nd,fd->nf", grad_second, down_full, preferred_element_type=jnp.float32)
    )
    grad_hidden_low = grad_hidden.astype(jnp.bfloat16)
    grad_w_up = jnp.einsum(
        "nd,nf->df", normed_low, grad_hidden_low, preferred_element_type=jnp.float32
    )
    grad_b_up = jnp.sum(grad_hidden_low.astype(jnp.float32), axis=0)
    grad_normed = grad_resid_two + lax.psum(
        jnp.einsum(
            "nf,df->nd", grad_hidden_low, up_full, preferred_element_type=jnp.float32
        ).astype(jnp.bfloat16),
        "tp",
    ).astype(jnp.float32)
    grad_resid_one, grad_gain_one, grad_shift_one = norm_one_back(grad_normed)
    grad_branch = grad_resid_one.astype(jnp.bfloat16)
    grad_w_out = jnp.einsum(
        "nc,nd->cd", attended_low, grad_branch, preferred_element_type=jnp.float32
    )
    grad_b_out = jnp.sum(grad_branch.astype(jnp.float32), axis=0)
    grad_att = jnp.einsum(
        "nd,cd->nc", grad_branch, out_full, preferred_element_type=jnp.float32
    ).astype(jnp.bfloat16)
    grad_att_heads = grad_att.reshape(sequences, local_rows, head_count, HEAD_DIM)
    row_delta = jnp.sum(grad_att_heads.astype(jnp.float32) * attended, axis=-1).transpose(0, 2, 1)
    zero_block = jnp.zeros((sequences, local_rows, head_count, HEAD_DIM), jnp.float32)

    def turn_grads(first_key, key_block, value_block):
        usable = live_keys(lengths, first_key, local_rows)
        key_heads = key_block.reshape(sequences, local_rows, head_count, HEAD_DIM)
        value_heads = value_block.reshape(sequences, local_rows, head_count, HEAD_DIM)
        return block_grads(
            query_heads,
            grad_att_heads,
            log_total,
            row_delta,
            key_heads,
            value_heads,
            usable,
            score_scale,
        )

    def cycle_turn(turn_index, carried):
        key_block, value_block, grad_key, grad_value, grad_query = carried
        source = (ctx_index - turn_index) % ctx_count
        added_query, added_key, added_value = turn_grads(
            source * local_rows, key_block, value_block
        )
        key_block, value_block = passed_along((key_block, value_block), "ctx", 1)
        grad_key, grad_value = (
            passed_along((grad_key + added_key).astype(jnp.bfloat16), "ctx", 1).astype(jnp.float32),
            passed_along((grad_value + added_value).astype(jnp.bfloat16), "ctx", 1).astype(
                jnp.float32
            ),
        )
        return (key_block, value_block, grad_key, grad_value, grad_query + added_query)

    cycle_end = lax.fori_loop(
        0, ctx_count, cycle_turn, (key_local, value_local, zero_block, zero_block, zero_block)
    )
    grad_key, grad_value, grad_query = (cycle_end[2], cycle_end[3], cycle_end[4])
    grad_query_low = grad_query.reshape(token_count, local_width).astype(jnp.bfloat16)
    grad_key_low = grad_key.reshape(token_count, local_width).astype(jnp.bfloat16)
    grad_value_low = grad_value.reshape(token_count, local_width).astype(jnp.bfloat16)
    grad_w_query = jnp.einsum(
        "nd,nc->dc", flat_tokens, grad_query_low, preferred_element_type=jnp.float32
    )
    grad_w_key = jnp.einsum(
        "nd,nc->dc", flat_tokens, grad_key_low, preferred_element_type=jnp.float32
    )
    grad_w_value = jnp.einsum(
        "nd,nc->dc", flat_tokens, grad_value_low, preferred_element_type=jnp.float32
    )
    grad_b_query = jnp.sum(grad_query_low.astype(jnp.float32), axis=0)
    grad_b_value = jnp.sum(grad_value_low.astype(jnp.float32), axis=0)
    back_in = (
        jnp.einsum("nc,dc->nd", grad_query_low, query_full, preferred_element_type=jnp.float32)
        + jnp.einsum("nc,dc->nd", grad_key_low, key_full, preferred_element_type=jnp.float32)
        + jnp.einsum("nc,dc->nd", grad_value_low, value_full, preferred_element_type=jnp.float32)
    )
    grad_tokens = grad_resid_one + lax.psum(back_in.astype(jnp.bfloat16), "tp").astype(jnp.float32)
    (
        share_query,
        share_key,
        share_value,
        share_out,
        share_up,
        share_down,
        share_bias_out,
        share_gain_one,
        share_shift_one,
        share_bias_down,
        share_gain_two,
        share_shift_two,
    ) = (
        lax.psum_scatter(
            grad_w_query.astype(jnp.bfloat16), "fsdp", scatter_dimension=0, tiled=True
        ).astype(jnp.float32),
        lax.psum_scatter(
            grad_w_key.astype(jnp.bfloat16), "fsdp", scatter_dimension=0, tiled=True
        ).astype(jnp.float32),
        lax.psum_scatter(
            grad_w_value.astype(jnp.bfloat16), "fsdp", scatter_dimension=0, tiled=True
        ).astype(jnp.float32),
        lax.psum_scatter(
            grad_w_out.astype(jnp.bfloat16), "fsdp", scatter_dimension=1, tiled=True
        ).astype(jnp.float32),
        lax.psum_scatter(
            grad_w_up.astype(jnp.bfloat16), "fsdp", scatter_dimension=0, tiled=True
        ).astype(jnp.float32),
        lax.psum_scatter(
            grad_w_down.astype(jnp.bfloat16), "fsdp", scatter_dimension=1, tiled=True
        ).astype(jnp.float32),
        lax.psum_scatter(
            grad_b_out.astype(jnp.bfloat16), "fsdp", scatter_dimension=0, tiled=True
        ).astype(jnp.float32),
        lax.psum_scatter(
            grad_gain_one.astype(jnp.bfloat16), "fsdp", scatter_dimension=0, tiled=True
        ).astype(jnp.float32),
        lax.psum_scatter(
            grad_shift_one.astype(jnp.bfloat16), "fsdp", scatter_dimension=0, tiled=True
        ).astype(jnp.float32),
        lax.psum_scatter(
            grad_b_down.astype(jnp.bfloat16), "fsdp", scatter_dimension=0, tiled=True
        ).astype(jnp.float32),
        lax.psum_scatter(
            grad_gain_two.astype(jnp.bfloat16), "fsdp", scatter_dimension=0, tiled=True
        ).astype(jnp.float32),
        lax.psum_scatter(
            grad_shift_two.astype(jnp.bfloat16), "fsdp", scatter_dimension=0, tiled=True
        ).astype(jnp.float32),
    )
    (
        share_query,
        share_key,
        share_value,
        share_out,
        share_up,
        share_down,
        share_bias_out,
        share_gain_one,
        share_shift_one,
        share_bias_down,
        share_gain_two,
        share_shift_two,
    ) = (
        lax.psum(share_query.astype(jnp.bfloat16), "ctx").astype(jnp.float32),
        lax.psum(share_key.astype(jnp.bfloat16), "ctx").astype(jnp.float32),
        lax.psum(share_value.astype(jnp.bfloat16), "ctx").astype(jnp.float32),
        lax.psum(share_out.astype(jnp.bfloat16), "ctx").astype(jnp.float32),
        lax.psum(share_up.astype(jnp.bfloat16), "ctx").astype(jnp.float32),
        lax.psum(share_down.astype(jnp.bfloat16), "ctx").astype(jnp.float32),
        lax.psum(share_bias_out.astype(jnp.bfloat16), "ctx").astype(jnp.float32),
        lax.psum(share_gain_one.astype(jnp.bfloat16), "ctx").astype(jnp.float32),
        lax.psum(share_shift_one.astype(jnp.bfloat16), "ctx").astype(jnp.float32),
        lax.psum(share_bias_down.astype(jnp.bfloat16), "ctx").astype(jnp.float32),
        lax.psum(share_gain_two.astype(jnp.bfloat16), "ctx").astype(jnp.float32),
        lax.psum(share_shift_two.astype(jnp.bfloat16), "ctx").astype(jnp.float32),
    )
    total_b_query, total_b_value, total_b_up = lax.psum(
        (grad_b_query, grad_b_value, grad_b_up), ("fsdp", "ctx")
    )
    return (
        output.astype(jnp.bfloat16).reshape(sequences, local_rows, model_width),
        grad_tokens.reshape(sequences, local_rows, model_width),
        share_query,
        share_key,
        share_value,
        total_b_query,
        total_b_value,
        share_out,
        share_bias_out,
        share_gain_one,
        share_shift_one,
        share_up,
        total_b_up,
        share_down,
        share_bias_down,
        share_gain_two,
        share_shift_two,
    )


def swapped(value, axis, bit):
    count = lax.axis_size(axis)
    return lax.ppermute(value, axis, [(place, place ^ bit) for place in range(count)])


def shifted(value, axis, steps):
    count = lax.axis_size(axis)
    return lax.ppermute(value, axis, [(place, (place + steps) % count) for place in range(count)])


def to_owner(value, step, back=False):
    pairs = []
    for x in range(2):
        for z in range(4):
            block = z ^ step
            source = x * 4 + z
            target = (block >> 1) * 4 + (block ^ (2 * x))
            pairs.append((target, source) if back else (source, target))
    return lax.ppermute(value, ("ctx", "tp"), pairs)


ANY = pl.BlockSpec(memory_space=pl.ANY)
WHOLE = pl.BlockSpec(memory_space=pltpu.VMEM)
log2_e = math.log2(math.e)
EXTRA = 8


def low(value):
    return value.astype(jnp.bfloat16)


def wide(value):
    return value.astype(jnp.float32)


def dot32(left, right, left_dim, right_dim):
    return lax.dot_general(
        left, right, (((left_dim,), (right_dim,)), ((), ())), preferred_element_type=jnp.float32
    )


def struct(shape, dtype=jnp.bfloat16):
    return jax.ShapeDtypeStruct(shape, dtype)


def cost(flops, moved, special=0):
    return pl.CostEstimate(flops=int(flops), bytes_accessed=int(moved), transcendentals=int(special))


def stack_kernel(*refs):
    for place, ref in enumerate(refs[:-1]):
        refs[-1][place] = ref[...]


def stacked(pieces):
    shape = (len(pieces),) + pieces[0].shape
    return pl.pallas_call(
        stack_kernel,
        out_shape=struct(shape),
        in_specs=[WHOLE] * len(pieces),
        out_specs=WHOLE,
        cost_estimate=cost(0, 4 * math.prod(shape)),
        name="stack_pieces",
    )(*pieces)


def piece_copies(meta, pieces, taken, columns, target, sems, first):
    x, z, f = meta[0], meta[1], meta[2]
    copies = []
    parts = [(piece, step) for piece in pieces for step in range(piece.shape[0])]
    for index, (piece, step) in enumerate(parts):
        place, slot = index // 4, index % 4
        across = (place % 2, 2 * ((place // 2) % 2) + place // 4)
        start = pl.multiple_of(((f ^ across[1]) * 2 + (x ^ across[0])) * taken, taken)
        copies.append(
            pltpu.make_async_copy(
                piece.at[step, pl.ds(0, taken), columns],
                target.at[z ^ slot, pl.ds(start, taken), :],
                sems.at[first + len(copies)],
            )
        )
    return copies


def attend_kernel(
    meta, own, other, w0, w1, w2, w3, bias, qkv, o0, o1, o2, o3, stats, weight, vectors,
    mask, shards, *, block, heads
):
    step = pl.program_id(0)
    shard = w0.shape[0] - EXTRA
    half = own.shape[1]
    scale = log2_e * HEAD_DIM ** (-0.5)

    @pl.when(step == 0)
    def _():
        for place, piece in enumerate((w0, w1, w2, w3)):
            start = pl.multiple_of((meta[2] ^ place) * shard, shard)
            weight[pl.ds(start, shard), :] = piece[:shard, :]
            shards[meta[2] ^ place] = piece[shard:, :]
        vectors[6:8, :] = jnp.zeros((2, 4 * shard), jnp.float32)
        for place in range(4):
            for row in range(6):
                first = row % 3 * shard
                vectors[row : row + 1, place * shard : (place + 1) * shard] = wide(
                    shards[place, row // 3 : row // 3 + 1, first : first + shard]
                )
        for place, rows in enumerate((own, other)):
            source = rows[0] if place == 0 else rows[...]
            qkv[place * half : (place + 1) * half, :] = low(
                dot32(source, weight[...], 1, 0) + bias[...]
            )
            first = (meta[0] ^ place) * half
            position = first + lax.broadcasted_iota(jnp.int32, (half, block), 0)
            mask[place * half : (place + 1) * half, :] = jnp.where(
                position < meta[3], 0.0, masked_score
            )

    rows = pl.ds(pl.multiple_of((meta[7] ^ step) * block, block), block)
    outs, logs = [], []
    for head in range(heads):
        base = 3 * head * HEAD_DIM
        query = qkv[rows, base : base + HEAD_DIM]
        key = qkv[:, base + HEAD_DIM : base + 2 * HEAD_DIM]
        value = qkv[:, base + 2 * HEAD_DIM : base + 3 * HEAD_DIM]
        scores = dot32(key, query, 1, 1) * scale + mask[...]
        peak = jnp.max(scores, axis=0, keepdims=True)
        weights = jnp.exp2(scores - peak)
        total = jnp.sum(weights, axis=0, keepdims=True)
        outs.append((dot32(value, low(weights), 0, 0) / total).T)
        logs.append(peak + jnp.log2(total))
    result = low(jnp.concatenate(outs, axis=1))
    for place, out in enumerate((o0, o1, o2, o3)):

        @pl.when(step == place)
        def _(out=out):
            out[...] = result

    stats[0] = jnp.concatenate(logs + [jnp.zeros((8 - heads, block), jnp.float32)], axis=0)


def attend_call(meta, tokens, other, pieces, bias, heads):
    half, width = other.shape
    block = half // 2
    columns = pieces[0].shape[1]
    whole = lambda shape: pl.BlockSpec(shape, lambda step, meta: (0,) * len(shape))
    rows = 2 * half
    return pl.pallas_call(
        lambda *refs: attend_kernel(*refs, block=block, heads=heads),
        grid_spec=pltpu.PrefetchScalarGridSpec(
            num_scalar_prefetch=1,
            grid=(4,),
            in_specs=[
                pl.BlockSpec((1, half, width), lambda step, meta: (meta[0], 0, 0)),
                whole((half, width)),
                *[whole(piece.shape) for piece in pieces],
                whole((1, columns)),
            ],
            out_specs=[
                whole((rows, columns)),
                *[whole((block, columns // 3))] * 4,
                pl.BlockSpec((1, 8, block), lambda step, meta: (step, 0, 0)),
                whole((width, columns)),
                whole((EXTRA, width)),
            ],
            scratch_shapes=[
                pltpu.VMEM((rows, block), jnp.float32),
                pltpu.VMEM((4, EXTRA, columns), jnp.bfloat16),
            ],
        ),
        out_shape=[struct((rows, columns))]
        + [struct((block, columns // 3))] * 4
        + [struct((4, 8, block), jnp.float32), struct((width, columns))]
        + [struct((EXTRA, width), jnp.float32)],
        cost_estimate=cost(2 * rows * width * columns + 16 * rows * rows * columns, 8e6, rows * rows * 3),
        name="attend",
    )(meta, tokens, other, *pieces, bias)


def attend_back_kernel(
    meta, qkv, d0, d1, d2, d3, o0, o1, o2, o3, stats, weight, full, p0, p1, p2, p3,
    grads, mask, grad_att, attended, *, block, heads
):
    step = pl.program_id(0)
    rows_all = qkv.shape[0]
    half = rows_all // 2
    scale = log2_e * HEAD_DIM ** (-0.5)

    @pl.when(step == 0)
    def _():
        grads[...] = jnp.zeros_like(grads)
        for place in range(2):
            first = (meta[0] ^ place) * half
            position = first + lax.broadcasted_iota(jnp.int32, (half, block), 0)
            mask[place * half : (place + 1) * half, :] = jnp.where(
                position < meta[3], 0.0, masked_score
            )

    for place, (grad, out) in enumerate(zip((d0, d1, d2, d3), (o0, o1, o2, o3))):

        @pl.when(step == place)
        def _(grad=grad, out=out):
            grad_att[...] = grad[...]
            attended[...] = out[...]

    rows = pl.ds(pl.multiple_of((meta[7] ^ step) * block, block), block)
    for head in range(heads):
        base = 3 * head * HEAD_DIM
        span = slice(head * HEAD_DIM, (head + 1) * HEAD_DIM)
        query = qkv[rows, base : base + HEAD_DIM]
        key = qkv[:, base + HEAD_DIM : base + 2 * HEAD_DIM]
        value = qkv[:, base + 2 * HEAD_DIM : base + 3 * HEAD_DIM]
        grad_out = grad_att[:, span]
        products = wide(grad_out) * wide(attended[:, span])
        delta = lax.dot_general(
            jnp.ones((8, HEAD_DIM), jnp.float32),
            products,
            (((1,), (1,)), ((), ())),
            precision=lax.Precision.HIGHEST,
            preferred_element_type=jnp.float32,
        )[:1]
        scores = dot32(key, query, 1, 1) * scale + mask[...]
        weights = jnp.exp2(scores - stats[0, head : head + 1, :])
        grad_weights = dot32(value, grad_out, 1, 1)
        grad_scores = low(weights * (grad_weights - delta))
        grads[2 * head] += dot32(grad_scores, query, 1, 0)
        grads[2 * head + 1] += dot32(low(weights), grad_out, 1, 0)
        full[rows, base : base + HEAD_DIM] = low(
            dot32(grad_scores, key, 0, 0) * HEAD_DIM ** (-0.5)
        )

    @pl.when(step == 3)
    def _():
        for head in range(heads):
            base = 3 * head * HEAD_DIM
            full[:, base + HEAD_DIM : base + 2 * HEAD_DIM] = low(
                grads[2 * head] * HEAD_DIM ** (-0.5)
            )
            full[:, base + 2 * HEAD_DIM : base + 3 * HEAD_DIM] = low(grads[2 * head + 1])
        for place, part in enumerate((p0, p1, p2, p3)):
            span = pl.ds(pl.multiple_of((meta[7] ^ place) * block, block), block)
            part[...] = low(dot32(full[span, :], weight[...], 1, 1))


def attend_back_call(meta, qkv, grad_parts, parts, stats, weight, heads):
    rows, columns = qkv.shape
    width = weight.shape[0]
    block = rows // 4
    whole = lambda shape: pl.BlockSpec(shape, lambda step, meta: (0,) * len(shape))
    small = whole((block, columns // 3))
    return pl.pallas_call(
        lambda *refs: attend_back_kernel(*refs, block=block, heads=heads),
        grid_spec=pltpu.PrefetchScalarGridSpec(
            num_scalar_prefetch=1,
            grid=(4,),
            in_specs=[whole((rows, columns))]
            + [small] * 8
            + [pl.BlockSpec((1, 8, block), lambda step, meta: (step, 0, 0)), whole(weight.shape)],
            out_specs=[whole((rows, columns))] + [whole((block, width))] * 4,
            scratch_shapes=[
                pltpu.VMEM((2 * heads, rows, HEAD_DIM), jnp.float32),
                pltpu.VMEM((rows, block), jnp.float32),
                pltpu.VMEM((block, columns // 3), jnp.bfloat16),
                pltpu.VMEM((block, columns // 3), jnp.bfloat16),
            ],
        ),
        out_shape=[struct((rows, columns))] + [struct((block, width))] * 4,
        cost_estimate=cost(40 * rows * rows * columns, 8e6, rows * rows * 3),
        name="attend_back",
    )(meta, qkv, *grad_parts, *parts, stats, weight)


def norm_parts(inputs):
    center = jnp.mean(inputs, axis=-1, keepdims=True)
    centered = inputs - center
    spread = jnp.mean(centered * centered, axis=-1, keepdims=True)
    inverse = lax.rsqrt(spread + epsilon)
    return centered * inverse, inverse


def norm_back(grad_out, hat, inverse, gain):
    scaled = grad_out * gain
    return inverse * (
        scaled
        - jnp.mean(scaled, axis=-1, keepdims=True)
        - hat * jnp.mean(scaled * hat, axis=-1, keepdims=True)
    )


BIAS_OUT, GAIN_ONE, SHIFT_ONE, BIAS_DOWN, GAIN_TWO, SHIFT_TWO = range(6)


def first_kernel(meta, *refs, width):
    att, tok, vectors, lines, pieces = refs[:4], refs[4], refs[5], refs[6], refs[7:15]
    hat, inverse, both, slope, out_w, up_w, sems = refs[15:]
    hidden = up_w.shape[2]
    taken = pieces[0].shape[1]
    copies = piece_copies(meta, pieces, taken, pl.ds(hidden, out_w.shape[2]), out_w, sems, 0)
    up_copies = piece_copies(meta, pieces, taken, pl.ds(0, hidden), up_w, sems, 32)
    for copy in copies + up_copies:
        copy.start()
    for step in range(4):
        both[step, :, hidden : hidden + width] = att[step][...]
        both[step, :, hidden + width :] = jnp.zeros_like(both[step, :, hidden + width :])
    for copy in copies:
        copy.wait()
    branch = vectors[BIAS_OUT : BIAS_OUT + 1, :]
    for step in range(4):
        branch = branch + dot32(att[step][...], out_w[meta[4] ^ step][:, :width], 1, 1)
    hat_one, inverse_one = norm_parts(wide(tok[0]) + branch)
    hat[...] = hat_one
    inverse[...] = inverse_one
    normed = low(hat_one * vectors[GAIN_ONE : GAIN_ONE + 1, :] + vectors[SHIFT_ONE : SHIFT_ONE + 1, :])
    for copy in up_copies:
        copy.wait()
    for place in range(4):
        inputs = dot32(normed, up_w[place], 1, 0) + wide(lines[meta[1] ^ place, 0:1, :])
        cumulative = 0.5 * (1.0 + lax.erf(inputs * (0.5**0.5)))
        density = jnp.exp(-0.5 * inputs * inputs) * ((0.5 / math.pi) ** 0.5)
        both[place, :, :hidden] = low(inputs * cumulative)
        slope[place] = low(cumulative + inputs * density)


def second_kernel(meta, *refs, width):
    hat, inverse, both, slope, cot, vectors = refs[:6]
    pieces_a, pieces_b = refs[6:14], refs[14:24]
    output, resid, g0, g1, g2, g3, mixed, keep = refs[24:32]
    out_w, up_w, down_w, blocks, small, small_blocks, sems = refs[32:]
    rows, model = hat.shape
    hidden = up_w.shape[2]
    taken = pieces_a[0].shape[1]
    down_copies = piece_copies(meta, pieces_b, taken, pl.ds(0, hidden), down_w, sems, 0)
    copies = piece_copies(meta, pieces_a, taken, pl.ds(0, hidden), up_w, sems, 32)
    copies += piece_copies(meta, pieces_a, taken, pl.ds(hidden, out_w.shape[2]), out_w, sems, 64)
    for copy in down_copies + copies:
        copy.start()
    row = lambda place: vectors[place : place + 1, :]
    hat_one, inverse_one = hat[...], inverse[...]
    normed_one = hat_one * row(GAIN_ONE) + row(SHIFT_ONE)
    for copy in down_copies:
        copy.wait()
    second = row(BIAS_DOWN)
    for place in range(4):
        second = second + dot32(both[place, :, :hidden], down_w[place], 1, 1)
    hat_two, inverse_two = norm_parts(normed_one + second)
    output[...] = low(hat_two * row(GAIN_TWO) + row(SHIFT_TWO))
    position = meta[4] * rows + lax.broadcasted_iota(jnp.int32, (rows, model), 0)
    grad_output = jnp.where(position < meta[8], wide(cot[0]), 0.0)
    grad_two = norm_back(grad_output, hat_two, inverse_two, row(GAIN_TWO))
    grad_second = low(grad_two)
    for copy in copies:
        copy.wait()
    grad_normed = grad_two
    sums = lambda array: jnp.sum(array, axis=0, keepdims=True)
    for place in range(4):
        grad_hidden = low(dot32(grad_second, down_w[place], 1, 0) * wide(slope[place]))
        mixed[place, :rows, :] = grad_hidden
        mixed[place, rows:, :] = low(
            jnp.broadcast_to(sums(wide(grad_hidden)), (EXTRA, hidden))
        )
        grad_normed = grad_normed + dot32(grad_hidden, up_w[place], 1, 1)
    grad_one = norm_back(grad_normed, hat_one, inverse_one, row(GAIN_ONE))
    resid[...] = grad_one
    grad_branch = low(grad_one)
    for step, out in enumerate((g0, g1, g2, g3)):
        out[...] = low(dot32(grad_branch, out_w[meta[4] ^ step][:, :width], 1, 0))
    small[0:1, :] = sums(wide(grad_branch))
    small[1:2, :] = sums(grad_normed * hat_one)
    small[2:3, :] = sums(grad_normed)
    small[3:4, :] = sums(wide(grad_second))
    small[4:5, :] = sums(grad_output * hat_two)
    small[5:6, :] = sums(grad_output)
    small[6:8, :] = jnp.zeros((2, model), jnp.float32)
    shard = model // 4
    for place in range(4):
        small_blocks[place] = low(small[:, place * shard : (place + 1) * shard])
    for kind, array in enumerate((grad_second, low(normed_one), grad_branch)):
        for place in range(4):
            blocks[place] = array[:, place * shard : (place + 1) * shard]
        for far in range(2):
            keep[kind, far, :rows, :] = blocks[meta[2] ^ (2 * far)]
            keep[kind, far, rows:, :] = small_blocks[meta[2] ^ (2 * far)]
            columns = slice(kind * shard, (kind + 1) * shard)
            mixed[4 + far, :rows, columns] = blocks[meta[2] ^ (2 * far + 1)]
            mixed[4 + far, rows:, columns] = small_blocks[meta[2] ^ (2 * far + 1)]
    for far in range(2):
        mixed[4 + far, :, 3 * shard :] = jnp.zeros((rows + EXTRA, hidden - 3 * shard), jnp.bfloat16)


def slot_of(block, z):
    apart = block ^ z
    return 2 * (apart & 1) + (apart >> 1)


def weights_kernel(meta, *refs):
    keep, tail_sib, both, both_sib, att, att_sib, mixed, mixed_sib = refs[:8]
    near_up, far_up, mine_down, theirs_down, turned, ordered = refs[8:]
    shard = keep.shape[3]
    rows = both.shape[1]
    half = shard // 2
    hidden, padded = mixed.shape[2], att.shape[2]
    starts = [pl.multiple_of(side * half, half) for side in (meta[0], 1 - meta[0])]

    @pl.when(pl.program_id(0) == 0)
    def _():
        for kind in range(3):
            for far in range(2):
                span = slice(far * shard, (far + 1) * shard)
                turned[span, :rows] = keep[kind, far, :rows, :].T
                turned[span, rows:] = tail_sib[far, :rows, kind * shard : (kind + 1) * shard].T
                for side, start in enumerate(starts):
                    first = (2 * far + side) * half
                    ordered[kind, first : first + half, :] = turned[
                        pl.ds(far * shard + start, half), :
                    ]

    operands = (
        (both[0], both_sib[0]),
        (mixed[0, :rows, :], mixed_sib[0, :rows, :]),
        (att[0], att_sib[0]),
    )
    for kind, (left, right) in enumerate(operands):
        value = dot32(ordered[kind, :, :rows], left, 1, 0)
        value = value + dot32(ordered[kind, :, rows:], right, 1, 0)
        for far in range(2):
            for side in range(2):
                first = (2 * far + side) * half
                part = low(value[first : first + half, :])
                up = (near_up, far_up)[far]
                if kind == 0:
                    split = hidden - mine_down.shape[3]
                    (mine_down, theirs_down)[side][far, 0, :half, :] = part[:, split:]
                    up[side, 0, :half, hidden + padded :] = part[:, :split]
                elif kind == 1:
                    up[side, 0, :half, :hidden] = part
                else:
                    up[side, 0, :half, hidden : hidden + padded] = part
    hidden_sums = low(wide(mixed[0, rows:, :]) + wide(mixed_sib[0, rows:, :]))
    for far in range(2):
        vector_sums = low(wide(keep[0, far, rows:, :]) + wide(tail_sib[far, rows:, :shard]))
        for side in range(2):
            out = (mine_down, theirs_down)[side]
            out[far, 0, half:, :] = jnp.zeros((EXTRA, out.shape[3]), jnp.bfloat16)
            out = (near_up, far_up)[far]
            out[side, 0, half:, :hidden] = hidden_sums
            out[side, 0, half:, hidden : hidden + shard] = vector_sums
            rest = slice(hidden + shard, None)
            out[side, 0, half:, rest] = jnp.zeros_like(out[side, 0, half:, rest])


def projections_kernel(meta, own, other, grads, kept, sent, whole):
    half, shard = other.shape[0], other.shape[1] // 4
    count = grads.shape[1]
    whole[...] = dot32(own[0], grads[:half, :], 0, 0) + dot32(other[...], grads[half:, :], 0, 0)
    sums = jnp.broadcast_to(jnp.sum(wide(grads[...]), axis=0, keepdims=True), (EXTRA, count))
    for far in range(2):
        for out, place in ((kept, meta[2] ^ (2 * far)), (sent, meta[2] ^ (2 * far + 1))):
            value = whole[pl.ds(pl.multiple_of(place * shard, shard), shard), :]
            out[far, :shard, :count] = value.astype(out.dtype)
            out[far, shard:, :count] = sums.astype(out.dtype)
            out[far, :, count:] = jnp.zeros_like(out[far, :, count:])


def per_device_rows(
    tokens,
    lengths,
    cotangent,
    w_query,
    w_key,
    w_value,
    b_query,
    b_value,
    w_out,
    b_out,
    ln1_gain,
    ln1_shift,
    w_up,
    b_up,
    w_down,
    b_down,
    ln2_gain,
    ln2_shift,
):
    sequences, local_rows, model = tokens.shape
    x, f, z = lax.axis_index("ctx"), lax.axis_index("fsdp"), lax.axis_index("tp")
    rows = local_rows // 2
    width = w_query.shape[1]
    heads = width // HEAD_DIM
    hidden = w_up.shape[1]
    shard = w_query.shape[0]
    half = shard // 2
    padded = -(-width // 128) * 128
    own_seq, own_place = (z // 2) ^ x, z % 2
    quarter = 2 * x + own_place
    length_of = lambda place: lax.dynamic_index_in_dim(lengths, place, 0, keepdims=False)
    entries = (x, z, f, length_of(x), quarter, own_seq, own_place, z ^ (2 * x), length_of(own_seq))
    places = lax.iota(jnp.int32, len(entries))
    meta = sum(jnp.where(places == place, entry, 0) for place, entry in enumerate(entries))
    meta = meta.astype(jnp.int32)
    tied = lambda *values: lax.optimization_barrier(values)

    take_half = lambda pack: lax.dynamic_slice_in_dim(pack, x * half, half, 0)
    wider = lambda array, columns: jnp.pad(array, ((0, 0), (0, columns - array.shape[1])))
    columns_a = hidden + padded
    half_a = wider(take_half(jnp.concatenate([w_up, w_out.T], axis=1)), columns_a)
    half_b = jnp.concatenate(
        [take_half(w_down.T), b_up[None], jnp.zeros((EXTRA - 1, hidden), jnp.bfloat16)]
    )

    other = lax.dynamic_index_in_dim(tokens, 1 - x, 0, keepdims=False)
    other, half_a = tied(other, half_a)
    other = swapped(other, "ctx", 1)
    far_a, near_half = swapped(half_a, "tp", 2), swapped(half_a, "tp", 1)
    per_head = lambda weights: jnp.concatenate(
        [
            weight[..., head * HEAD_DIM : (head + 1) * HEAD_DIM]
            for head in range(heads)
            for weight in weights
        ],
        axis=-1,
    )
    vectors = jnp.concatenate([b_out, ln1_gain, ln1_shift, b_down, ln2_gain, ln2_shift])
    qkv_shard = jnp.concatenate(
        [
            per_head((w_query, w_key, w_value)),
            jnp.pad(vectors.reshape(2, 3 * width), ((0, EXTRA - 2), (0, 0))),
        ]
    )
    qkv_bias = wide(per_head((b_query, jnp.zeros_like(b_query), b_value)))[None, :]
    far_a, meta = tied(far_a, meta)
    last_a, qkv_y = tied(swapped(far_a, "tp", 1), swapped(qkv_shard, "fsdp", 2))
    line_a = stacked([half_a, near_half, far_a, last_a])
    qkv_pieces = (qkv_shard, swapped(qkv_shard, "fsdp", 1), qkv_y, swapped(qkv_y, "fsdp", 1))

    core = lambda array: swapped(array, "fsdp", 1)
    meta, qkv_bias, other, line_a, half_b, *qkv_pieces = tied(
        meta, qkv_bias, other, line_a, half_b, *qkv_pieces
    )
    x_a, y_a = swapped(line_a, "ctx", 1), swapped(line_a, "fsdp", 2)
    qkv, *parts, stats, weight, vectors = attend_call(
        meta, tokens, other, qkv_pieces, qkv_bias, heads
    )
    b_pieces = [swapped(half_b, "tp", bit) for bit in (1, 2, 3)]

    x_a, y_a, line_a, *rest = tied(x_a, y_a, line_a, *b_pieces, *parts)
    b_pieces, parts = rest[:3], rest[3:]
    line_b = stacked([half_b, *b_pieces])
    att = [to_owner(part, step) for step, part in enumerate(parts)]
    x_y_a = swapped(x_a, "fsdp", 2)
    x_y_a, x_a, y_a, line_a, line_b, *att = tied(x_y_a, x_a, y_a, line_a, line_b, *att)
    near_a = (line_a, x_a, y_a, x_y_a)
    pieces_a = (*near_a, *map(core, near_a))
    x_b, y_b, line_core = swapped(line_b, "ctx", 1), swapped(line_b, "fsdp", 2), core(line_b)

    def row_spec(array):
        return pl.BlockSpec((1, rows, model), lambda step, meta: (meta[5], meta[6], 0))

    vm = lambda shape, dtype=jnp.bfloat16: pltpu.VMEM(shape, dtype)
    weights_scratch = [vm((4, model, padded)), vm((4, model, hidden))]
    grid = lambda inputs, outputs, scratch: pltpu.PrefetchScalarGridSpec(
        num_scalar_prefetch=1, grid=(1,), in_specs=inputs, out_specs=outputs, scratch_shapes=scratch
    )
    full = lambda shape: pl.BlockSpec(shape, lambda step, meta: (0,) * len(shape))
    specs = lambda shapes: [full(item.shape) for item in shapes]

    first_out = [
        struct((rows, model), jnp.float32),
        struct((rows, 1), jnp.float32),
        struct((4, rows, columns_a)),
        struct((4, rows, hidden)),
    ]
    hat, inverse, both, slope = pl.pallas_call(
        lambda *refs: first_kernel(*refs, width=width),
        grid_spec=grid(
            [full((rows, width))] * 4
            + [row_spec(tokens), full((EXTRA, model))]
            + [pl.BlockSpec((4, EXTRA, hidden), lambda step, meta: (0, half // EXTRA, 0))]
            + [ANY] * 8,
            specs(first_out),
            weights_scratch + [pltpu.SemaphoreType.DMA((64,))],
        ),
        out_shape=first_out,
        cost_estimate=cost(2 * rows * model * (model + 4 * hidden), 12e6, rows * hidden * 8),
        name="feed_first",
    )(meta, *att, tokens, vectors, line_b, *pieces_a)

    both, x_b, y_b, line_b, line_core = tied(both, x_b, y_b, line_b, line_core)
    x_y_b = [swapped(x_b[:2], "fsdp", 2), swapped(y_b[2:], "ctx", 1)]
    *x_y_b, x_core, y_core, both_sib = tied(*x_y_b, core(x_b), core(y_b), core(both))
    pieces_b = (line_b, x_b, y_b, *x_y_b, line_core, x_core, y_core, *map(core, x_y_b))

    second_out = [
        struct((rows, model)),
        struct((rows, model), jnp.float32),
        *[struct((rows, width))] * 4,
        struct((6, rows + EXTRA, hidden)),
        struct((3, 2, rows + EXTRA, shard)),
    ]
    output, resid, g0, g1, g2, g3, mixed, keep = pl.pallas_call(
        lambda *refs: second_kernel(*refs, width=width),
        grid_spec=grid(
            [full(item.shape) for item in (hat, inverse, both, slope)]
            + [row_spec(cotangent), full((EXTRA, model))]
            + [ANY] * 18,
            specs(second_out),
            weights_scratch
            + [
                vm((4, model, hidden)),
                vm((4, rows, shard)),
                vm((EXTRA, model), jnp.float32),
                vm((4, EXTRA, shard)),
                pltpu.SemaphoreType.DMA((96,)),
            ],
        ),
        out_shape=second_out,
        cost_estimate=cost(2 * rows * model * (model + 12 * hidden), 20e6),
        name="feed_second",
    )(meta, hat, inverse, both, slope, cotangent, vectors, *pieces_a, *pieces_b)

    grad_att = [to_owner(part, step, True) for step, part in enumerate((g0, g1, g2, g3))]

    first_x = 2 * padded
    pack = struct((2, 4, half + EXTRA, first_x))
    pack_up = struct((2, 4, half + EXTRA, columns_a + hidden - first_x))
    mixed_sib = core(mixed)
    per_block = lambda item, place=lambda block, meta: block, columns=None, lanes=0: pl.BlockSpec(
        (1, item.shape[1], columns or item.shape[2]),
        lambda block, meta: (place(block, meta), 0, lanes),
    )
    heads_of = lambda block, meta: block ^ meta[4]
    sent_block = lambda item: pl.BlockSpec(
        (2, 1) + item.shape[2:], lambda block, meta: (0, slot_of(block, meta[1]), 0, 0)
    )
    near_up, far_up, mine_down, theirs_down = pl.pallas_call(
        weights_kernel,
        grid_spec=pltpu.PrefetchScalarGridSpec(
            num_scalar_prefetch=1,
            grid=(4,),
            in_specs=[
                full(keep.shape),
                pl.BlockSpec((2,) + mixed.shape[1:], lambda block, meta: (2, 0, 0)),
                *[per_block(both, columns=hidden)] * 2,
                *[per_block(both, heads_of, padded, hidden // padded)] * 2,
                *[per_block(mixed)] * 2,
            ],
            out_specs=[sent_block(pack_up)] * 2 + [sent_block(pack)] * 2,
            scratch_shapes=[vm((2 * shard, 2 * rows)), vm((3, 2 * shard, 2 * rows))],
        ),
        out_shape=[pack_up] * 2 + [pack] * 2,
        cost_estimate=cost(8 * rows * shard * (8 * hidden + 4 * width), 20e6),
        name="feed_weights",
    )(meta, keep, mixed_sib, both, both_sib, both, both_sib, mixed, mixed_sib)

    far_up, theirs_down, output, *grad_att = tied(far_up, theirs_down, output, *grad_att)
    got_up, got_down = swapped(far_up, "fsdp", 2), swapped(theirs_down, "ctx", 1)
    far_out, near_out = swapped(output, "tp", 2), swapped(output, "tp", 1)
    grad_full, *grad_parts = attend_back_call(meta, qkv, grad_att, parts, stats, weight, heads)

    got_down, near_out, far_out, *grad_parts = tied(got_down, near_out, far_out, *grad_parts)
    grad_rows = [to_owner(part, step) for step, part in enumerate(grad_parts)]
    far_out, up_sent, down_sent, grad_full, *grad_rows = tied(
        far_out,
        low(wide(near_up[1]) + wide(got_up[1])),
        low(wide(mine_down[1]) + wide(got_down[1])),
        grad_full,
        *grad_rows,
    )
    kept, sent = pl.pallas_call(
        projections_kernel,
        grid_spec=grid(
            [pl.BlockSpec((1, local_rows, model), lambda step, meta: (meta[0], 0, 0))]
            + [full((local_rows, model)), full(grad_full.shape)],
            [full((2, shard + EXTRA, 640 * width // 192))] * 2,
            [vm((model, 3 * width), jnp.float32)],
        ),
        out_shape=[
            struct((2, shard + EXTRA, 640 * width // 192), dtype) for dtype in (jnp.float32, jnp.bfloat16)
        ],
        cost_estimate=cost(12 * local_rows * model * width, 8e6),
        name="projection_weights",
    )(meta, tokens, other, grad_full)
    second_up, second_down = swapped(up_sent, "ctx", 1), swapped(down_sent, "fsdp", 2)
    def spread_rows(pieces, dtype):
        blocks = [
            lax.select_n(z ^ (2 * x), *[pieces[block ^ place] for place in range(4)]).astype(dtype)
            for block in range(4)
        ]
        return jnp.stack([jnp.concatenate(blocks[2 * seq : 2 * seq + 2]) for seq in range(2)])

    token_rows = resid
    for part in grad_rows:
        token_rows = token_rows + wide(part)

    token_rows = low(token_rows)
    far_z, last_out, near_z, sent, second_up, second_down = tied(
        swapped(token_rows, "tp", 2),
        swapped(far_out, "tp", 1),
        token_rows,
        sent,
        second_up,
        second_down,
    )
    output_full = spread_rows([output, near_out, far_out, last_out], jnp.bfloat16)
    up_lines = wide(near_up[0]) + wide(got_up[0]) + wide(second_up)
    down_lines = wide(mine_down[0]) + wide(got_down[0]) + wide(second_down)
    lines = jnp.concatenate([up_lines, down_lines], axis=2)
    lines, line_sent = lines[:2], low(lines[2:])
    line_got, last_z = tied(swapped(line_sent, "tp", 1), far_z)
    lines = lines + wide(line_got)
    near_z, last_z = swapped(near_z, "tp", 1), swapped(last_z, "tp", 1)
    grad_tokens = spread_rows([token_rows, near_z, far_z, last_z], jnp.float32)
    line_last = swapped(low(lines[1]), "tp", 2)
    total = low(lines[0] + wide(line_last))
    other_half = swapped(total, "ctx", 1)
    small = wide(total[half:])
    total = wide(
        jnp.concatenate(
            [
                jnp.where(x == 0, total[:half], other_half[:half]),
                jnp.where(x == 0, other_half[:half], total[:half]),
            ]
        )
    )
    grad_w_up = total[:, :hidden]
    grad_w_down = total[:, columns_a:].T
    grad_w_out = total[:, hidden : hidden + width].T
    grad_b_up = small[0, :hidden]
    small_own = small[:, hidden : hidden + shard]

    kept = kept + wide(core(sent))
    kept = low(kept[0] + wide(swapped(low(kept[1]), "fsdp", 2)))
    kept = wide(kept) + wide(swapped(kept, "ctx", 1))

    def unpack(array, part):
        return jnp.concatenate(
            [
                array[:, (3 * head + part) * HEAD_DIM : (3 * head + part + 1) * HEAD_DIM]
                for head in range(heads)
            ],
            axis=1,
        )

    grad_w_query, grad_w_key, grad_w_value = (unpack(kept[:shard], part) for part in range(3))
    grad_b_query, grad_b_value = (unpack(kept[shard : shard + 1], part)[0] for part in (0, 2))
    return (
        output_full,
        grad_tokens,
        grad_w_query,
        grad_w_key,
        grad_w_value,
        grad_b_query,
        grad_b_value,
        grad_w_out,
        small_own[0],
        small_own[1],
        small_own[2],
        grad_w_up,
        grad_b_up,
        grad_w_down,
        small_own[3],
        small_own[4],
        small_own[5],
    )


def rows_path_fits(mesh, tokens, w_query, w_up):
    shape = dict(mesh.shape)
    return (
        shape["ctx"] == 2
        and shape["fsdp"] == 4
        and shape["tp"] == 4
        and tokens.shape[0] == 8
        and tokens.shape[1] % 1024 == 0
        and w_query.shape[0] == w_query.shape[1]
        and w_query.shape[0] % 768 == 0
        and w_up.shape[1] == 4 * w_up.shape[0]
    )


def solution(mesh):
    placed = (
        P("fsdp", "ctx", None),
        P("fsdp"),
        P("fsdp", "ctx", None),
        P("fsdp", "tp"),
        P("fsdp", "tp"),
        P("fsdp", "tp"),
        P("tp"),
        P("tp"),
        P("tp", "fsdp"),
        P("fsdp"),
        P("fsdp"),
        P("fsdp"),
        P("fsdp", "tp"),
        P("tp"),
        P("tp", "fsdp"),
        P("fsdp"),
        P("fsdp"),
        P("fsdp"),
    )
    def split(function):
        return jax.shard_map(
        function,
        mesh=mesh,
        in_specs=placed,
        out_specs=(
            P("fsdp", "ctx", None),
            P("fsdp", "ctx", None),
            P("fsdp", "tp"),
            P("fsdp", "tp"),
            P("fsdp", "tp"),
            P("tp"),
            P("tp"),
            P("tp", "fsdp"),
            P("fsdp"),
            P("fsdp"),
            P("fsdp"),
            P("fsdp", "tp"),
            P("tp"),
            P("tp", "fsdp"),
            P("fsdp"),
            P("fsdp"),
            P("fsdp"),
        ),
        check_vma=False,
    )

    def run(*arrays):
        fits = rows_path_fits(mesh, arrays[0], arrays[3], arrays[12])
        return split(per_device_rows if fits else per_device)(*arrays)

    return run
```
